32 devices in a mesh: fsdp: 8 (over z, y), seq: 4 (over x, core).
Axes of the slice: x: 2, y: 2, z: 4, core: 2. Of those that a mesh axis runs over, the one named last changes fastest.
Arguments:
- tokens: bfloat16 [4096, 1152], P(('fsdp', 'seq')), may hold values from -6 to 6
- doc_start: int32 [4096], P(('fsdp', 'seq')), may hold values from 0 to 511, as said below
- gains: bfloat16 [5120], P(('fsdp', 'seq')), may hold values from 0.5 to 1.5
- w_query: bfloat16 [1152, 1024], P(None, ('fsdp', 'seq')), may hold values from -0.1875 to 0.1875
- w_key: bfloat16 [1152, 256], P(None, ('fsdp', 'seq')), may hold values from -0.1875 to 0.1875
- w_value: bfloat16 [1152, 256], P(None, ('fsdp', 'seq')), may hold values from -0.1875 to 0.1875
- w_out: bfloat16 [1024, 1152], P(('fsdp', 'seq')), may hold values from -0.1875 to 0.1875
- w_gate: bfloat16 [1152, 6912], P(None, ('fsdp', 'seq')), may hold values from -0.1875 to 0.1875
- w_up: bfloat16 [1152, 6912], P(None, ('fsdp', 'seq')), may hold values from -0.1875 to 0.1875
- w_down: bfloat16 [6912, 1152], P(('fsdp', 'seq')), may hold values from -0.078125 to 0.078125
- cotangent: bfloat16 [4096, 1152], P(('fsdp', 'seq')), may hold values from -6 to 6
Outputs:
- output: bfloat16 [4096, 1152], P(('fsdp', 'seq'))
- grad_tokens: float32 [4096, 1152], P(('fsdp', 'seq'))
- grad_gains: float32 [5120], P(('fsdp', 'seq'))
- grad_query: float32 [1152, 1024], P(None, ('fsdp', 'seq'))
- grad_key: float32 [1152, 256], P(None, ('fsdp', 'seq'))
- grad_value: float32 [1152, 256], P(None, ('fsdp', 'seq'))
- grad_out: float32 [1024, 1152], P(('fsdp', 'seq'))
- grad_gate: float32 [1152, 6912], P(None, ('fsdp', 'seq'))
- grad_up: float32 [1152, 6912], P(None, ('fsdp', 'seq'))
- grad_down: float32 [6912, 1152], P(('fsdp', 'seq'))
The draws below stay inside these ranges and needn't reach their ends.
Inputs may be any that keep to these rules, and one draw needn't show every extreme that they name: For the token at place t of its sequence of 512 tokens, doc_start is the place where its document begins: t - 383 <= doc_start <= t, and it equals t or the previous token's value; the first token of a sequence begins a document, and every sequence holds one document of exactly 384 tokens.
All inputs are finite; a program needn't handle non-finite values.
Results may differ from the reference program's by a relative error of at most 0.019.
Values may be sent and summed in bfloat16 or wider, within the bound.
A program may use at most 256 MiB of HBM per device.

```python
from functools import partial
import jax
import jax.numpy as jnp
from jax import lax

D = 1152
FF = 6912
HEADS = 4
HD = 256
SEQ = 512
TOKENS = 4096
DOC_MOST = 384
GAINS = 5120


def draw_doc_start(key, part):
    seq_count = TOKENS // SEQ
    place_key = jax.random.fold_in(key, 11)
    flag_key = jax.random.fold_in(key, 23)
    anchor = jax.random.randint(place_key, (seq_count, 1), 0, SEQ - DOC_MOST)
    places = jnp.arange(SEQ, dtype=jnp.int32)[None, :]
    spacing = max(SEQ // 8, 2)
    starts_at = jax.random.randint(flag_key, (seq_count, SEQ), 0, spacing) == 0
    inside = (places > anchor) & (places < anchor + DOC_MOST)
    forced = (places - anchor) % DOC_MOST == 0
    starts_at = starts_at & jnp.logical_not(inside) | forced | (places == 0) | (places == SEQ - 1)
    start_marks = jnp.where(starts_at, places, 0)
    starts = lax.cummax(start_marks, axis=1)
    return starts.reshape(-1).astype(jnp.int32)


def block_levels(rng, shape, pieces, smallest, high):
    def one(axis_at, blocks):
        steps = jax.random.uniform(jax.random.fold_in(jax.random.fold_in(rng, 6), axis_at), (blocks,), jnp.float32, smallest / len(pieces), high / len(pieces))
        return jnp.repeat(jnp.exp(steps), shape[axis_at] // blocks).reshape((-1,) + (1,) * (len(shape) - axis_at - 1))

    level = one(*pieces[0])
    for cut in pieces[1:]:
        level = level * one(*cut)
    return level


def noise(own_key, dims, deviation, limit, split=(), held_as=jnp.bfloat16):
    values = deviation * jax.random.normal(own_key, dims, jnp.float32)
    if split:
        values = values * block_levels(own_key, dims, split, -0.22, 0.18)
    return jnp.clip(values, -limit, limit).astype(held_as)


def setup_inputs(seed: int = 0) -> dict:
    seeds = jax.random.split(jax.random.key(seed), 12)
    return {
        "tokens": noise(seeds[0], (TOKENS, D), 1.0, 6.0, ((0, 32),)),
        "doc_start": draw_doc_start(jax.random.fold_in(seeds[11], 71), 0),
        "gains": jnp.clip(1.0 + 0.1 * jax.random.normal(seeds[2], (GAINS,), jnp.float32), 0.5, 1.5).astype(jnp.bfloat16),
        "w_query": noise(seeds[3], (D, HEADS * HD), D ** -0.5, 0.1875, ((1, 32),)),
        "w_key": noise(seeds[4], (D, HD), D ** -0.5, 0.1875, ((1, 32),)),
        "w_value": noise(seeds[5], (D, HD), D ** -0.5, 0.1875, ((1, 32),)),
        "w_out": noise(seeds[6], (HEADS * HD, D), (HEADS * HD) ** -0.5, 0.1875, ((0, 32),)),
        "w_gate": noise(seeds[7], (D, FF), D ** -0.5, 0.1875, ((1, 32),)),
        "w_up": noise(seeds[8], (D, FF), D ** -0.5, 0.1875, ((1, 32),)),
        "w_down": noise(seeds[9], (FF, D), FF ** -0.5, 0.078125, ((0, 32),)),
        "cotangent": noise(seeds[10], (TOKENS, D), 1.0, 6.0, ((0, 32),)),
    }


norm_eps = 1e-06
rope_base = 1000000.0
score_scale = 0.0625
masked_value = -1e+30

@jax.custom_vjp
def low(v):
    return lax.optimization_barrier(v.astype(jnp.bfloat16)).astype(jnp.float32)

@jax.custom_vjp
def low_back(v):
    return v

def low_keep(v):
    return (low(v), None)

def low_pass(kept, grad):
    return (grad,)

def back_keep(v):
    return (v, None)

def back_low(kept, grad):
    return (low(grad),)
low.defvjp(low_keep, low_pass)
low_back.defvjp(back_keep, back_low)

def high_dot(former, latter):
    return jnp.dot(former, latter, precision=lax.Precision.HIGHEST)

def scaled_norm(values, factor):
    return values * lax.rsqrt(lax.optimization_barrier(jnp.mean(values * values, axis=-1, keepdims=True)) + norm_eps) * factor

def rotate(values, cos_table, sin_table):
    half_width = values.shape[-1] // 2
    leading = values[..., :half_width]
    trailing = values[..., half_width:]
    return jnp.concatenate([leading * cos_table - trailing * sin_table, trailing * cos_table + leading * sin_table], axis=-1)

def head_norm(values, factor, cos_table, sin_table):
    return rotate(scaled_norm(values, factor), cos_table, sin_table)

def rope_tables(places, rot_width):
    half_width = rot_width // 2
    frequency = rope_base ** (-2.0 * jnp.arange(half_width, dtype=jnp.float32) / rot_width)
    angles = places.astype(jnp.float32)[:, None] * frequency[None, :]
    return (jnp.cos(angles)[:, None, :], jnp.sin(angles)[:, None, :])

def layer(doc_row, inputs, gain_values, query_w, key_w, value_w, out_w, gate_w, up_w, down_w):
    gain_pre = gain_values[:D]
    gain_query = gain_values[D:D + HD]
    gain_key = gain_values[D + HD:D + 2 * HD]
    gain_post = gain_values[D + 2 * HD:2 * D + 2 * HD]
    gain_pre_ffn = gain_values[2 * D + 2 * HD:3 * D + 2 * HD]
    gain_post_ffn = gain_values[3 * D + 2 * HD:]
    normed = low(scaled_norm(inputs, gain_pre))
    query_raw = low_back(high_dot(normed, query_w)).reshape(SEQ, HEADS, HD)
    key_raw = low_back(high_dot(normed, key_w)).reshape(SEQ, 1, HD)
    value_rows = low(low_back(high_dot(normed, value_w)))
    places = jnp.arange(SEQ, dtype=jnp.int32) - doc_row
    cos_table, sin_table = rope_tables(places, HD)
    queries = low(head_norm(query_raw, gain_query, cos_table, sin_table))
    key_rows = low(head_norm(key_raw, gain_key, cos_table, sin_table))[:, 0, :]
    block_rows = min(512, SEQ)
    key_place = jnp.arange(SEQ, dtype=jnp.int32)

    def attend(block_index):
        offset = block_index * block_rows
        query_block = lax.dynamic_slice_in_dim(queries, offset, block_rows, 0)
        bounds = lax.dynamic_slice_in_dim(doc_row, offset, block_rows, 0)
        query_place = offset + jnp.arange(block_rows, dtype=jnp.int32)
        raw_scores = low_back(jnp.einsum('bhd,kd->hbk', query_block, key_rows, precision=lax.Precision.HIGHEST) * score_scale)
        allowed = (key_place[None, :] >= bounds[:, None]) & (key_place[None, :] <= query_place[:, None])
        scores = jnp.where(allowed[None], raw_scores, masked_value)
        row_max = lax.optimization_barrier(jnp.max(scores, axis=2, keepdims=True))
        weights = jnp.exp(scores - row_max)
        probability = low(weights / lax.optimization_barrier(jnp.sum(weights, axis=2, keepdims=True)))
        return low(low_back(jnp.einsum('hbk,kd->bhd', probability, value_rows, precision=lax.Precision.HIGHEST)))
    mixed_rows = lax.map(jax.checkpoint(attend), jnp.arange(SEQ // block_rows, dtype=jnp.int32)).reshape(SEQ, HEADS * HD)
    attn_raw = low_back(high_dot(mixed_rows, out_w))
    middle = inputs + scaled_norm(attn_raw, gain_post)
    normed_ffn = low(scaled_norm(middle, gain_pre_ffn))
    gate_act = low_back(high_dot(normed_ffn, gate_w))
    up_act = low_back(high_dot(normed_ffn, up_w))
    hidden = low(jax.nn.gelu(gate_act, approximate=True) * up_act)
    ffn_raw = low_back(high_dot(hidden, down_w))
    return middle + scaled_norm(ffn_raw, gain_post_ffn)

def reference(tokens, doc_start, gains, w_query, w_key, w_value, w_out, w_gate, w_up, w_down, cotangent):
    weight_set = tuple((member.astype(jnp.float32) for member in (gains, w_query, w_key, w_value, w_out, w_gate, w_up, w_down)))
    seq_count = TOKENS // SEQ
    input_rows = tokens.astype(jnp.float32).reshape(seq_count, SEQ, D)
    doc_rows = doc_start.reshape(seq_count, SEQ)
    cotan_rows = cotangent.astype(jnp.float32).reshape(seq_count, SEQ, D)

    def add_sequence(grad_total, seq_item):
        seq_input, seq_doc, seq_cotan = seq_item
        seq_output, pullback = jax.vjp(partial(layer, seq_doc), seq_input, *weight_set)
        seq_grads = pullback(seq_cotan)
        summed = tuple((former + latter for former, latter in zip(grad_total, seq_grads[1:])))
        return (summed, (seq_output.astype(jnp.bfloat16), seq_grads[0]))
    zero_grads = tuple((jnp.zeros_like(member) for member in weight_set))
    grad_total, (outputs_all, input_grads) = lax.scan(add_sequence, zero_grads, (input_rows, doc_rows, cotan_rows))
    return (outputs_all.reshape(TOKENS, D), input_grads.reshape(TOKENS, D), grad_total[0], grad_total[1], grad_total[2], grad_total[3], grad_total[4], grad_total[5], grad_total[6], grad_total[7])
```

```python
from functools import partial

import jax
import jax.numpy as jnp
from jax import lax
from jax.sharding import PartitionSpec as P

norm_eps = 1e-06
rope_base = 1000000.0
score_scale = 0.0625
masked_value = -1e30


def product(former, latter):
    return jnp.dot(former, latter, preferred_element_type=jnp.float32)


def inner_rows(former, latter):
    return lax.dot_general(
        former, latter, (((0,), (0,)), ((), ())), preferred_element_type=jnp.float32
    )


def outer_rows(former, latter):
    return lax.dot_general(
        former, latter, (((1,), (1,)), ((), ())), preferred_element_type=jnp.float32
    )


def scaled_norm(values, factor):
    return values * lax.rsqrt(jnp.mean(values * values, axis=-1, keepdims=True) + norm_eps) * factor


def rotate(values, cos_table, sin_table):
    half_width = values.shape[-1] // 2
    leading = values[..., :half_width]
    trailing = values[..., half_width:]
    return jnp.concatenate(
        [leading * cos_table - trailing * sin_table, trailing * cos_table + leading * sin_table],
        axis=-1,
    )


def head_norm(values, factor, cos_table, sin_table):
    return rotate(scaled_norm(values, factor), cos_table, sin_table)


def gated_unit(gate_in, up_in):
    return jax.nn.gelu(gate_in, approximate=True) * up_in


def rope_tables(places, rot_width):
    half_width = rot_width // 2
    frequency = rope_base ** (-2.0 * jnp.arange(half_width, dtype=jnp.float32) / rot_width)
    angles = places.astype(jnp.float32)[:, None] * frequency[None, :]
    return (jnp.cos(angles)[:, None, :], jnp.sin(angles)[:, None, :])


def masked_scores(queries, key_rows, bounds, offset):
    raw_scores = outer_rows(queries, key_rows) * score_scale
    query_place = offset + jnp.arange(queries.shape[0], dtype=jnp.int32)
    key_place = jnp.arange(key_rows.shape[0], dtype=jnp.int32)
    allowed = (key_place[None, :] >= bounds[:, None]) & (key_place[None, :] <= query_place[:, None])
    return jnp.where(allowed, raw_scores, masked_value)


def local(
    tokens, doc_start, gains, w_query, w_key, w_value, w_out, w_gate, w_up, w_down, cotangent
):
    tok_rows = tokens.shape[0]
    model_width = tokens.shape[1]
    run_index = lax.axis_index("seq")
    gains_all, query_w, key_w, value_w, out_w = (
        lax.all_gather(gains, ("fsdp", "seq"), axis=0, tiled=True),
        lax.all_gather(w_query, ("fsdp", "seq"), axis=1, tiled=True),
        lax.all_gather(w_key, ("fsdp", "seq"), axis=1, tiled=True),
        lax.all_gather(w_value, ("fsdp", "seq"), axis=1, tiled=True),
        lax.all_gather(w_out, ("fsdp", "seq"), axis=0, tiled=True),
    )
    gate_w, up_w, down_w = (
        lax.all_gather(w_gate, ("fsdp", "seq"), axis=1, tiled=True),
        lax.all_gather(w_up, ("fsdp", "seq"), axis=1, tiled=True),
        lax.all_gather(w_down, ("fsdp", "seq"), axis=0, tiled=True),
    )
    head_width = key_w.shape[1]
    head_count = query_w.shape[1] // head_width
    gain_values = gains_all.astype(jnp.float32)
    gain_pre = gain_values[:model_width]
    gain_query = gain_values[model_width : model_width + head_width]
    gain_key = gain_values[model_width + head_width : model_width + 2 * head_width]
    gain_post = gain_values[model_width + 2 * head_width : 2 * model_width + 2 * head_width]
    gain_pre_ffn = gain_values[2 * model_width + 2 * head_width : 3 * model_width + 2 * head_width]
    gain_post_ffn = gain_values[3 * model_width + 2 * head_width :]
    residual = tokens.astype(jnp.float32)
    normed, pre_pull = jax.vjp(scaled_norm, residual, gain_pre)
    normed_b = normed.astype(jnp.bfloat16)
    query_raw = product(normed_b, query_w).reshape(tok_rows, head_count, head_width)
    key_raw = product(normed_b, key_w).reshape(tok_rows, 1, head_width)
    value_b = product(normed_b, value_w).astype(jnp.bfloat16)
    places = run_index * tok_rows + jnp.arange(tok_rows, dtype=jnp.int32) - doc_start
    cos_table, sin_table = rope_tables(places, head_width)
    rope_norm = partial(head_norm, cos_table=cos_table, sin_table=sin_table)
    query_rot, query_pull = jax.vjp(rope_norm, query_raw, gain_query)
    key_rot, key_pull = jax.vjp(rope_norm, key_raw, gain_key)
    query_b = query_rot.reshape(tok_rows, head_count * head_width).astype(jnp.bfloat16)
    key_b = key_rot.reshape(tok_rows, head_width).astype(jnp.bfloat16)
    query_heads = lax.all_to_all(query_b, "seq", split_axis=1, concat_axis=0, tiled=True)
    key_rows, value_rows = (
        lax.all_gather(key_b, "seq", axis=0, tiled=True),
        lax.all_gather(value_b, "seq", axis=0, tiled=True),
    )
    starts = lax.all_gather(doc_start, "seq", axis=0, tiled=True)
    seq_tokens = key_rows.shape[0]
    block_rows = min(512, seq_tokens)
    block_count = seq_tokens // block_rows
    query_blocks = query_heads.reshape(block_count, block_rows, head_width)
    start_blocks = starts.reshape(block_count, block_rows)
    block_ids = jnp.arange(block_count, dtype=jnp.int32)

    def attend(block_item):
        queries, bounds, block_index = block_item
        scores = masked_scores(queries, key_rows, bounds, block_index * block_rows)
        row_max = jnp.max(scores, axis=1, keepdims=True)
        weights = jnp.exp(scores - row_max)
        row_total = jnp.sum(weights, axis=1, keepdims=True)
        probability = (weights / row_total).astype(jnp.bfloat16)
        mixed_block = product(probability, value_rows).astype(jnp.bfloat16)
        return (mixed_block, (row_max + jnp.log(row_total))[:, 0])

    mixed_blocks, lse_blocks = lax.map(attend, (query_blocks, start_blocks, block_ids))
    mixed_heads = mixed_blocks.reshape(seq_tokens, head_width)
    mixed_tokens = lax.all_to_all(mixed_heads, "seq", split_axis=0, concat_axis=1, tiled=True)
    attn_raw = product(mixed_tokens, out_w)
    attn_out, post_pull = jax.vjp(scaled_norm, attn_raw, gain_post)
    middle = residual + attn_out
    normed_ffn, pre_ffn_pull = jax.vjp(scaled_norm, middle, gain_pre_ffn)
    normed_ffn_b = normed_ffn.astype(jnp.bfloat16)
    gate_act = product(normed_ffn_b, gate_w)
    up_act = product(normed_ffn_b, up_w)
    hidden, glu_pull = jax.vjp(gated_unit, gate_act, up_act)
    hidden_b = hidden.astype(jnp.bfloat16)
    ffn_raw = product(hidden_b, down_w)
    ffn_out, post_ffn_pull = jax.vjp(scaled_norm, ffn_raw, gain_post_ffn)
    result = (middle + ffn_out).astype(jnp.bfloat16)
    gate_w, up_w, down_w = (
        lax.all_gather(w_gate, ("fsdp", "seq"), axis=1, tiled=True),
        lax.all_gather(w_up, ("fsdp", "seq"), axis=1, tiled=True),
        lax.all_gather(w_down, ("fsdp", "seq"), axis=0, tiled=True),
    )
    query_w, key_w, value_w, out_w = (
        lax.all_gather(w_query, ("fsdp", "seq"), axis=1, tiled=True),
        lax.all_gather(w_key, ("fsdp", "seq"), axis=1, tiled=True),
        lax.all_gather(w_value, ("fsdp", "seq"), axis=1, tiled=True),
        lax.all_gather(w_out, ("fsdp", "seq"), axis=0, tiled=True),
    )
    upstream = cotangent.astype(jnp.float32)
    ffn_grad, gain_post_ffn_grad = post_ffn_pull(upstream)
    ffn_grad_b = ffn_grad.astype(jnp.bfloat16)
    down_w_grad = inner_rows(hidden_b, ffn_grad_b)
    hidden_grad = outer_rows(ffn_grad_b, down_w)
    gate_grad, up_grad = glu_pull(hidden_grad)
    gate_grad_b = gate_grad.astype(jnp.bfloat16)
    up_grad_b = up_grad.astype(jnp.bfloat16)
    gate_w_grad_t = inner_rows(gate_grad_b, normed_ffn_b)
    up_w_grad_t = inner_rows(up_grad_b, normed_ffn_b)
    normed_ffn_grad = outer_rows(gate_grad_b, gate_w) + outer_rows(up_grad_b, up_w)
    middle_part, gain_pre_ffn_grad = pre_ffn_pull(normed_ffn_grad)
    middle_grad = upstream + middle_part
    attn_grad, gain_post_grad = post_pull(middle_grad)
    attn_grad_b = attn_grad.astype(jnp.bfloat16)
    out_w_grad = inner_rows(mixed_tokens, attn_grad_b)
    mixed_grad = outer_rows(attn_grad_b, out_w).astype(jnp.bfloat16)
    mixed_grad_heads = lax.all_to_all(mixed_grad, "seq", split_axis=1, concat_axis=0, tiled=True)
    grad_blocks = mixed_grad_heads.reshape(block_count, block_rows, head_width)

    def attend_back(carried, block_item):
        key_accum, value_accum = carried
        queries, bounds, block_index, lse_row, block_grad = block_item
        scores = masked_scores(queries, key_rows, bounds, block_index * block_rows)
        probability = jnp.exp(scores - lse_row[:, None])
        prob_grad = outer_rows(block_grad, value_rows)
        value_accum = value_accum + inner_rows(probability.astype(jnp.bfloat16), block_grad)
        row_delta = jnp.sum(probability * prob_grad, axis=1, keepdims=True)
        score_grad = (probability * (prob_grad - row_delta)).astype(jnp.bfloat16)
        query_grad = product(score_grad, key_rows) * score_scale
        key_accum = key_accum + inner_rows(score_grad, queries) * score_scale
        return ((key_accum, value_accum), query_grad)

    zero_rows = jnp.zeros((seq_tokens, head_width), jnp.float32)
    (key_part, value_part), query_grad_blocks = lax.scan(
        attend_back,
        (zero_rows, zero_rows),
        (query_blocks, start_blocks, block_ids, lse_blocks, grad_blocks),
    )
    key_sum, value_sum = (
        lax.psum_scatter(
            key_part.astype(jnp.bfloat16), "seq", scatter_dimension=0, tiled=True
        ).astype(jnp.float32),
        lax.psum_scatter(
            value_part.astype(jnp.bfloat16), "seq", scatter_dimension=0, tiled=True
        ).astype(jnp.float32),
    )
    query_grad_tokens = lax.all_to_all(
        query_grad_blocks.reshape(seq_tokens, head_width).astype(jnp.bfloat16),
        "seq",
        split_axis=0,
        concat_axis=1,
        tiled=True,
    ).astype(jnp.float32)
    query_raw_grad, gain_query_grad = query_pull(
        query_grad_tokens.reshape(tok_rows, head_count, head_width)
    )
    key_raw_grad, gain_key_grad = key_pull(key_sum.reshape(tok_rows, 1, head_width))
    query_raw_b = query_raw_grad.reshape(tok_rows, head_count * head_width).astype(jnp.bfloat16)
    key_raw_b = key_raw_grad.reshape(tok_rows, head_width).astype(jnp.bfloat16)
    value_raw_b = value_sum.astype(jnp.bfloat16)
    query_w_grad_t = inner_rows(query_raw_b, normed_b)
    key_w_grad_t = inner_rows(key_raw_b, normed_b)
    value_w_grad_t = inner_rows(value_raw_b, normed_b)
    normed_grad = (
        outer_rows(query_raw_b, query_w)
        + outer_rows(key_raw_b, key_w)
        + outer_rows(value_raw_b, value_w)
    )
    residual_part, gain_pre_grad = pre_pull(normed_grad)
    input_grad = middle_grad + residual_part
    gains_grad = jnp.concatenate(
        [
            gain_pre_grad,
            gain_query_grad,
            gain_key_grad,
            gain_post_grad,
            gain_pre_ffn_grad,
            gain_post_ffn_grad,
        ]
    )
    shares = (
        lax.psum_scatter(gains_grad, ("fsdp", "seq"), scatter_dimension=0, tiled=True),
        lax.psum_scatter(query_w_grad_t, ("fsdp", "seq"), scatter_dimension=0, tiled=True),
        lax.psum_scatter(key_w_grad_t, ("fsdp", "seq"), scatter_dimension=0, tiled=True),
        lax.psum_scatter(value_w_grad_t, ("fsdp", "seq"), scatter_dimension=0, tiled=True),
        lax.psum_scatter(out_w_grad, ("fsdp", "seq"), scatter_dimension=0, tiled=True),
        lax.psum_scatter(gate_w_grad_t, ("fsdp", "seq"), scatter_dimension=0, tiled=True),
        lax.psum_scatter(up_w_grad_t, ("fsdp", "seq"), scatter_dimension=0, tiled=True),
        lax.psum_scatter(down_w_grad, ("fsdp", "seq"), scatter_dimension=0, tiled=True),
    )
    return (
        result,
        input_grad,
        shares[0],
        shares[1].T,
        shares[2].T,
        shares[3].T,
        shares[4],
        shares[5].T,
        shares[6].T,
        shares[7],
    )


def gather_rows(block):
    return lax.all_gather(block, ("fsdp", "seq"), axis=0, tiled=True)


def scatter_rows(partial_sum):
    return lax.psum_scatter(
        partial_sum.astype(jnp.bfloat16), ("fsdp", "seq"), scatter_dimension=0, tiled=True
    ).astype(jnp.float32)


def split_model(
    tokens, doc_start, gains, w_query, w_key, w_value, w_out, w_gate, w_up, w_down, cotangent
):
    tok_rows, model_width = tokens.shape
    run_index = lax.axis_index("seq")
    seq_count = lax.axis_size("seq")
    dev_count = seq_count * lax.axis_size("fsdp")
    query_rows, key_rows_own = w_query.shape[1], w_key.shape[1]
    gain_row = jnp.pad(gains[None, :], ((0, 7), (0, model_width - gains.shape[0])))
    packed = jnp.concatenate([w_query.T, w_out, w_key.T, w_value.T, gain_row], axis=0)
    cuts = (query_rows, 2 * query_rows, 2 * query_rows + key_rows_own)
    cuts = cuts + (cuts[2] + key_rows_own,)
    everything = gather_rows(packed).reshape(dev_count, packed.shape[0], model_width)
    query_t = everything[:, : cuts[0]].reshape(-1, model_width)
    out_w = everything[:, cuts[0] : cuts[1]].reshape(-1, model_width)
    key_t = everything[:, cuts[1] : cuts[2]].reshape(-1, model_width)
    value_t = everything[:, cuts[2] : cuts[3]].reshape(-1, model_width)
    gain_values = everything[:, cuts[3], : gains.shape[0]].reshape(-1).astype(jnp.float32)
    head_width = key_t.shape[0]
    head_count = query_t.shape[0] // head_width
    places_in = [0, model_width, model_width + head_width, model_width + 2 * head_width]
    places_in += [places_in[3] + model_width, places_in[3] + 2 * model_width, gain_values.shape[0]]
    places_in[5:] = [places_in[4] + model_width, places_in[4] + 2 * model_width]
    gain_pre, gain_query, gain_key, gain_post, gain_pre_ffn, gain_post_ffn = (
        gain_values[first:last] for first, last in zip(places_in[:-1], places_in[1:])
    )
    residual = tokens.astype(jnp.float32)
    normed, pre_pull = jax.vjp(scaled_norm, residual, gain_pre)
    normed_b = normed.astype(jnp.bfloat16)
    query_raw = outer_rows(normed_b, query_t).reshape(tok_rows, head_count, head_width)
    key_raw = outer_rows(normed_b, key_t).reshape(tok_rows, 1, head_width)
    value_b = outer_rows(normed_b, value_t).astype(jnp.bfloat16)
    places = run_index * tok_rows + jnp.arange(tok_rows, dtype=jnp.int32) - doc_start
    cos_table, sin_table = rope_tables(places, head_width)
    rope_norm = partial(head_norm, cos_table=cos_table, sin_table=sin_table)
    query_rot, query_pull = jax.vjp(rope_norm, query_raw, gain_query)
    key_rot, key_pull = jax.vjp(rope_norm, key_raw, gain_key)
    query_b = query_rot.astype(jnp.bfloat16).transpose(1, 0, 2).reshape(-1, head_width)
    key_b = key_rot.reshape(tok_rows, head_width).astype(jnp.bfloat16)
    both = lax.all_gather(jnp.concatenate([key_b, value_b], axis=1), "seq", axis=0, tiled=True)
    key_rows, value_rows = both[:, :head_width], both[:, head_width:]
    raw_scores = outer_rows(query_b, key_rows) * score_scale
    query_place = run_index * tok_rows + jnp.arange(tok_rows, dtype=jnp.int32)
    key_place = jnp.arange(key_rows.shape[0], dtype=jnp.int32)
    allowed = (key_place[None, :] >= doc_start[:, None]) & (
        key_place[None, :] <= query_place[:, None]
    )
    allowed = jnp.tile(allowed, (head_count, 1))
    scores = jnp.where(allowed, raw_scores, masked_value)
    row_max = jnp.max(scores, axis=1, keepdims=True)
    weights = jnp.exp(scores - row_max)
    probability = weights / jnp.sum(weights, axis=1, keepdims=True)
    probability_b = probability.astype(jnp.bfloat16)
    mixed = product(probability_b, value_rows).astype(jnp.bfloat16)
    mixed_tokens = (
        mixed.reshape(head_count, tok_rows, head_width).transpose(1, 0, 2).reshape(tok_rows, -1)
    )
    attn_raw = product(mixed_tokens, out_w)
    attn_out, post_pull = jax.vjp(scaled_norm, attn_raw, gain_post)
    middle = residual + attn_out
    normed_ffn, pre_ffn_pull = jax.vjp(scaled_norm, middle, gain_pre_ffn)
    normed_all = gather_rows(normed_ffn.astype(jnp.bfloat16))
    gate_act = outer_rows(normed_all, w_gate.T)
    up_act = outer_rows(normed_all, w_up.T)
    hidden, glu_pull = jax.vjp(gated_unit, gate_act, up_act)
    hidden_b = hidden.astype(jnp.bfloat16)
    ffn_raw = scatter_rows(product(hidden_b, w_down))
    ffn_out, post_ffn_pull = jax.vjp(scaled_norm, ffn_raw, gain_post_ffn)
    result = (middle + ffn_out).astype(jnp.bfloat16)
    upstream = cotangent.astype(jnp.float32)
    ffn_grad, gain_post_ffn_grad = post_ffn_pull(upstream)
    ffn_grad_all = gather_rows(ffn_grad.astype(jnp.bfloat16))
    down_grad = inner_rows(hidden_b, ffn_grad_all)
    hidden_grad = outer_rows(ffn_grad_all, w_down)
    gate_grad, up_grad = glu_pull(hidden_grad)
    gate_grad_b = gate_grad.astype(jnp.bfloat16)
    up_grad_b = up_grad.astype(jnp.bfloat16)
    gate_w_grad_t = inner_rows(gate_grad_b, normed_all)
    up_w_grad_t = inner_rows(up_grad_b, normed_all)
    normed_ffn_grad = scatter_rows(product(gate_grad_b, w_gate.T) + product(up_grad_b, w_up.T))
    middle_part, gain_pre_ffn_grad = pre_ffn_pull(normed_ffn_grad)
    middle_grad = upstream + middle_part
    attn_grad, gain_post_grad = post_pull(middle_grad)
    attn_grad_b = attn_grad.astype(jnp.bfloat16)
    out_w_grad = inner_rows(mixed_tokens, attn_grad_b)
    mixed_grad = outer_rows(attn_grad_b, out_w).astype(jnp.bfloat16)
    mixed_grad = (
        mixed_grad.reshape(tok_rows, head_count, head_width)
        .transpose(1, 0, 2)
        .reshape(-1, head_width)
    )
    prob_grad = outer_rows(mixed_grad, value_rows)
    value_part = inner_rows(probability_b, mixed_grad)
    row_delta = jnp.sum(probability * prob_grad, axis=1, keepdims=True)
    score_grad = (probability * (prob_grad - row_delta)).astype(jnp.bfloat16)
    query_grad = product(score_grad, key_rows) * score_scale
    key_part = inner_rows(score_grad, query_b) * score_scale
    both_sum = lax.psum_scatter(
        jnp.concatenate([key_part, value_part], axis=1).astype(jnp.bfloat16),
        "seq",
        scatter_dimension=0,
        tiled=True,
    ).astype(jnp.float32)
    query_raw_grad, gain_query_grad = query_pull(
        query_grad.reshape(head_count, tok_rows, head_width).transpose(1, 0, 2)
    )
    key_raw_grad, gain_key_grad = key_pull(both_sum[:, None, :head_width])
    query_raw_b = query_raw_grad.reshape(tok_rows, -1).astype(jnp.bfloat16)
    key_raw_b = key_raw_grad.reshape(tok_rows, head_width).astype(jnp.bfloat16)
    value_raw_b = both_sum[:, head_width:].astype(jnp.bfloat16)
    normed_grad = (
        product(query_raw_b, query_t) + product(key_raw_b, key_t) + product(value_raw_b, value_t)
    )
    residual_part, gain_pre_grad = pre_pull(normed_grad)
    input_grad = middle_grad + residual_part
    gains_grad = jnp.concatenate(
        [
            gain_pre_grad,
            gain_query_grad,
            gain_key_grad,
            gain_post_grad,
            gain_pre_ffn_grad,
            gain_post_ffn_grad,
        ]
    )
    gains_block = jnp.pad(
        gains_grad.reshape(dev_count, 1, -1),
        ((0, 0), (0, 7), (0, model_width - gains.shape[0])),
    )
    by_device = lambda rows: rows.reshape(dev_count, -1, model_width)
    shares = scatter_rows(
        jnp.concatenate(
            [
                by_device(inner_rows(query_raw_b, normed_b)),
                by_device(out_w_grad),
                by_device(inner_rows(key_raw_b, normed_b)),
                by_device(inner_rows(value_raw_b, normed_b)),
                gains_block,
            ],
            axis=1,
        ).reshape(-1, model_width)
    )
    return (
        result,
        input_grad,
        shares[cuts[3], : gains.shape[0]],
        shares[: cuts[0]].T,
        shares[cuts[1] : cuts[2]].T,
        shares[cuts[2] : cuts[3]].T,
        shares[cuts[0] : cuts[1]],
        gate_w_grad_t.T,
        up_w_grad_t.T,
        down_grad,
    )


def solution(mesh):
    in_specs = (
        P(("fsdp", "seq"), None),
        P(("fsdp", "seq")),
        P(("fsdp", "seq")),
        P(None, ("fsdp", "seq")),
        P(None, ("fsdp", "seq")),
        P(None, ("fsdp", "seq")),
        P(("fsdp", "seq"), None),
        P(None, ("fsdp", "seq")),
        P(None, ("fsdp", "seq")),
        P(("fsdp", "seq"), None),
        P(("fsdp", "seq"), None),
    )
    out_specs = (
        P(("fsdp", "seq"), None),
        P(("fsdp", "seq"), None),
        P(("fsdp", "seq")),
        P(None, ("fsdp", "seq")),
        P(None, ("fsdp", "seq")),
        P(None, ("fsdp", "seq")),
        P(("fsdp", "seq"), None),
        P(None, ("fsdp", "seq")),
        P(None, ("fsdp", "seq")),
        P(("fsdp", "seq"), None),
    )
    body = split_model if mesh.size <= 32 else local
    return jax.shard_map(body, mesh=mesh, in_specs=in_specs, out_specs=out_specs, check_vma=False)
```

```python
from functools import partial

import jax
import jax.numpy as jnp
from jax import lax
from jax.experimental import pallas as pl
from jax.experimental.pallas import tpu as pltpu
from jax.sharding import PartitionSpec as P

norm_eps = 1e-06
rope_base = 1000000.0
score_scale = 0.0625
masked_value = -1e30


def product(former, latter):
    return jnp.dot(former, latter, preferred_element_type=jnp.float32)


def inner_rows(former, latter):
    return lax.dot_general(
        former, latter, (((0,), (0,)), ((), ())), preferred_element_type=jnp.float32
    )


def outer_rows(former, latter):
    return lax.dot_general(
        former, latter, (((1,), (1,)), ((), ())), preferred_element_type=jnp.float32
    )


def scaled_norm(values, factor):
    return values * lax.rsqrt(jnp.mean(values * values, axis=-1, keepdims=True) + norm_eps) * factor


def rotate(values, cos_table, sin_table):
    half_width = values.shape[-1] // 2
    leading = values[..., :half_width]
    trailing = values[..., half_width:]
    return jnp.concatenate(
        [leading * cos_table - trailing * sin_table, trailing * cos_table + leading * sin_table],
        axis=-1,
    )


def head_norm(values, factor, cos_table, sin_table):
    return rotate(scaled_norm(values, factor), cos_table, sin_table)


def gated_unit(gate_in, up_in):
    return jax.nn.gelu(gate_in, approximate=True) * up_in


def rope_tables(places, rot_width):
    half_width = rot_width // 2
    frequency = rope_base ** (-2.0 * jnp.arange(half_width, dtype=jnp.float32) / rot_width)
    angles = places.astype(jnp.float32)[:, None] * frequency[None, :]
    return (jnp.cos(angles)[:, None, :], jnp.sin(angles)[:, None, :])


def masked_scores(queries, key_rows, bounds, offset):
    raw_scores = outer_rows(queries, key_rows) * score_scale
    query_place = offset + jnp.arange(queries.shape[0], dtype=jnp.int32)
    key_place = jnp.arange(key_rows.shape[0], dtype=jnp.int32)
    allowed = (key_place[None, :] >= bounds[:, None]) & (key_place[None, :] <= query_place[:, None])
    return jnp.where(allowed, raw_scores, masked_value)


def local(
    tokens, doc_start, gains, w_query, w_key, w_value, w_out, w_gate, w_up, w_down, cotangent
):
    tok_rows = tokens.shape[0]
    model_width = tokens.shape[1]
    run_index = lax.axis_index("seq")
    gains_all, query_w, key_w, value_w, out_w = (
        lax.all_gather(gains, ("fsdp", "seq"), axis=0, tiled=True),
        lax.all_gather(w_query, ("fsdp", "seq"), axis=1, tiled=True),
        lax.all_gather(w_key, ("fsdp", "seq"), axis=1, tiled=True),
        lax.all_gather(w_value, ("fsdp", "seq"), axis=1, tiled=True),
        lax.all_gather(w_out, ("fsdp", "seq"), axis=0, tiled=True),
    )
    gate_w, up_w, down_w = (
        lax.all_gather(w_gate, ("fsdp", "seq"), axis=1, tiled=True),
        lax.all_gather(w_up, ("fsdp", "seq"), axis=1, tiled=True),
        lax.all_gather(w_down, ("fsdp", "seq"), axis=0, tiled=True),
    )
    head_width = key_w.shape[1]
    head_count = query_w.shape[1] // head_width
    gain_values = gains_all.astype(jnp.float32)
    gain_pre = gain_values[:model_width]
    gain_query = gain_values[model_width : model_width + head_width]
    gain_key = gain_values[model_width + head_width : model_width + 2 * head_width]
    gain_post = gain_values[model_width + 2 * head_width : 2 * model_width + 2 * head_width]
    gain_pre_ffn = gain_values[2 * model_width + 2 * head_width : 3 * model_width + 2 * head_width]
    gain_post_ffn = gain_values[3 * model_width + 2 * head_width :]
    residual = tokens.astype(jnp.float32)
    normed, pre_pull = jax.vjp(scaled_norm, residual, gain_pre)
    normed_b = normed.astype(jnp.bfloat16)
    query_raw = product(normed_b, query_w).reshape(tok_rows, head_count, head_width)
    key_raw = product(normed_b, key_w).reshape(tok_rows, 1, head_width)
    value_b = product(normed_b, value_w).astype(jnp.bfloat16)
    places = run_index * tok_rows + jnp.arange(tok_rows, dtype=jnp.int32) - doc_start
    cos_table, sin_table = rope_tables(places, head_width)
    rope_norm = partial(head_norm, cos_table=cos_table, sin_table=sin_table)
    query_rot, query_pull = jax.vjp(rope_norm, query_raw, gain_query)
    key_rot, key_pull = jax.vjp(rope_norm, key_raw, gain_key)
    query_b = query_rot.reshape(tok_rows, head_count * head_width).astype(jnp.bfloat16)
    key_b = key_rot.reshape(tok_rows, head_width).astype(jnp.bfloat16)
    query_heads = lax.all_to_all(query_b, "seq", split_axis=1, concat_axis=0, tiled=True)
    key_rows, value_rows = (
        lax.all_gather(key_b, "seq", axis=0, tiled=True),
        lax.all_gather(value_b, "seq", axis=0, tiled=True),
    )
    starts = lax.all_gather(doc_start, "seq", axis=0, tiled=True)
    seq_tokens = key_rows.shape[0]
    block_rows = min(512, seq_tokens)
    block_count = seq_tokens // block_rows
    query_blocks = query_heads.reshape(block_count, block_rows, head_width)
    start_blocks = starts.reshape(block_count, block_rows)
    block_ids = jnp.arange(block_count, dtype=jnp.int32)

    def attend(block_item):
        queries, bounds, block_index = block_item
        scores = masked_scores(queries, key_rows, bounds, block_index * block_rows)
        row_max = jnp.max(scores, axis=1, keepdims=True)
        weights = jnp.exp(scores - row_max)
        row_total = jnp.sum(weights, axis=1, keepdims=True)
        probability = (weights / row_total).astype(jnp.bfloat16)
        mixed_block = product(probability, value_rows).astype(jnp.bfloat16)
        return (mixed_block, (row_max + jnp.log(row_total))[:, 0])

    mixed_blocks, lse_blocks = lax.map(attend, (query_blocks, start_blocks, block_ids))
    mixed_heads = mixed_blocks.reshape(seq_tokens, head_width)
    mixed_tokens = lax.all_to_all(mixed_heads, "seq", split_axis=0, concat_axis=1, tiled=True)
    attn_raw = product(mixed_tokens, out_w)
    attn_out, post_pull = jax.vjp(scaled_norm, attn_raw, gain_post)
    middle = residual + attn_out
    normed_ffn, pre_ffn_pull = jax.vjp(scaled_norm, middle, gain_pre_ffn)
    normed_ffn_b = normed_ffn.astype(jnp.bfloat16)
    gate_act = product(normed_ffn_b, gate_w)
    up_act = product(normed_ffn_b, up_w)
    hidden, glu_pull = jax.vjp(gated_unit, gate_act, up_act)
    hidden_b = hidden.astype(jnp.bfloat16)
    ffn_raw = product(hidden_b, down_w)
    ffn_out, post_ffn_pull = jax.vjp(scaled_norm, ffn_raw, gain_post_ffn)
    result = (middle + ffn_out).astype(jnp.bfloat16)
    gate_w, up_w, down_w = (
        lax.all_gather(w_gate, ("fsdp", "seq"), axis=1, tiled=True),
        lax.all_gather(w_up, ("fsdp", "seq"), axis=1, tiled=True),
        lax.all_gather(w_down, ("fsdp", "seq"), axis=0, tiled=True),
    )
    query_w, key_w, value_w, out_w = (
        lax.all_gather(w_query, ("fsdp", "seq"), axis=1, tiled=True),
        lax.all_gather(w_key, ("fsdp", "seq"), axis=1, tiled=True),
        lax.all_gather(w_value, ("fsdp", "seq"), axis=1, tiled=True),
        lax.all_gather(w_out, ("fsdp", "seq"), axis=0, tiled=True),
    )
    upstream = cotangent.astype(jnp.float32)
    ffn_grad, gain_post_ffn_grad = post_ffn_pull(upstream)
    ffn_grad_b = ffn_grad.astype(jnp.bfloat16)
    down_w_grad = inner_rows(hidden_b, ffn_grad_b)
    hidden_grad = outer_rows(ffn_grad_b, down_w)
    gate_grad, up_grad = glu_pull(hidden_grad)
    gate_grad_b = gate_grad.astype(jnp.bfloat16)
    up_grad_b = up_grad.astype(jnp.bfloat16)
    gate_w_grad_t = inner_rows(gate_grad_b, normed_ffn_b)
    up_w_grad_t = inner_rows(up_grad_b, normed_ffn_b)
    normed_ffn_grad = outer_rows(gate_grad_b, gate_w) + outer_rows(up_grad_b, up_w)
    middle_part, gain_pre_ffn_grad = pre_ffn_pull(normed_ffn_grad)
    middle_grad = upstream + middle_part
    attn_grad, gain_post_grad = post_pull(middle_grad)
    attn_grad_b = attn_grad.astype(jnp.bfloat16)
    out_w_grad = inner_rows(mixed_tokens, attn_grad_b)
    mixed_grad = outer_rows(attn_grad_b, out_w).astype(jnp.bfloat16)
    mixed_grad_heads = lax.all_to_all(mixed_grad, "seq", split_axis=1, concat_axis=0, tiled=True)
    grad_blocks = mixed_grad_heads.reshape(block_count, block_rows, head_width)

    def attend_back(carried, block_item):
        key_accum, value_accum = carried
        queries, bounds, block_index, lse_row, block_grad = block_item
        scores = masked_scores(queries, key_rows, bounds, block_index * block_rows)
        probability = jnp.exp(scores - lse_row[:, None])
        prob_grad = outer_rows(block_grad, value_rows)
        value_accum = value_accum + inner_rows(probability.astype(jnp.bfloat16), block_grad)
        row_delta = jnp.sum(probability * prob_grad, axis=1, keepdims=True)
        score_grad = (probability * (prob_grad - row_delta)).astype(jnp.bfloat16)
        query_grad = product(score_grad, key_rows) * score_scale
        key_accum = key_accum + inner_rows(score_grad, queries) * score_scale
        return ((key_accum, value_accum), query_grad)

    zero_rows = jnp.zeros((seq_tokens, head_width), jnp.float32)
    (key_part, value_part), query_grad_blocks = lax.scan(
        attend_back,
        (zero_rows, zero_rows),
        (query_blocks, start_blocks, block_ids, lse_blocks, grad_blocks),
    )
    key_sum, value_sum = (
        lax.psum_scatter(
            key_part.astype(jnp.bfloat16), "seq", scatter_dimension=0, tiled=True
        ).astype(jnp.float32),
        lax.psum_scatter(
            value_part.astype(jnp.bfloat16), "seq", scatter_dimension=0, tiled=True
        ).astype(jnp.float32),
    )
    query_grad_tokens = lax.all_to_all(
        query_grad_blocks.reshape(seq_tokens, head_width).astype(jnp.bfloat16),
        "seq",
        split_axis=0,
        concat_axis=1,
        tiled=True,
    ).astype(jnp.float32)
    query_raw_grad, gain_query_grad = query_pull(
        query_grad_tokens.reshape(tok_rows, head_count, head_width)
    )
    key_raw_grad, gain_key_grad = key_pull(key_sum.reshape(tok_rows, 1, head_width))
    query_raw_b = query_raw_grad.reshape(tok_rows, head_count * head_width).astype(jnp.bfloat16)
    key_raw_b = key_raw_grad.reshape(tok_rows, head_width).astype(jnp.bfloat16)
    value_raw_b = value_sum.astype(jnp.bfloat16)
    query_w_grad_t = inner_rows(query_raw_b, normed_b)
    key_w_grad_t = inner_rows(key_raw_b, normed_b)
    value_w_grad_t = inner_rows(value_raw_b, normed_b)
    normed_grad = (
        outer_rows(query_raw_b, query_w)
        + outer_rows(key_raw_b, key_w)
        + outer_rows(value_raw_b, value_w)
    )
    residual_part, gain_pre_grad = pre_pull(normed_grad)
    input_grad = middle_grad + residual_part
    gains_grad = jnp.concatenate(
        [
            gain_pre_grad,
            gain_query_grad,
            gain_key_grad,
            gain_post_grad,
            gain_pre_ffn_grad,
            gain_post_ffn_grad,
        ]
    )
    shares = (
        lax.psum_scatter(gains_grad, ("fsdp", "seq"), scatter_dimension=0, tiled=True),
        lax.psum_scatter(query_w_grad_t, ("fsdp", "seq"), scatter_dimension=0, tiled=True),
        lax.psum_scatter(key_w_grad_t, ("fsdp", "seq"), scatter_dimension=0, tiled=True),
        lax.psum_scatter(value_w_grad_t, ("fsdp", "seq"), scatter_dimension=0, tiled=True),
        lax.psum_scatter(out_w_grad, ("fsdp", "seq"), scatter_dimension=0, tiled=True),
        lax.psum_scatter(gate_w_grad_t, ("fsdp", "seq"), scatter_dimension=0, tiled=True),
        lax.psum_scatter(up_w_grad_t, ("fsdp", "seq"), scatter_dimension=0, tiled=True),
        lax.psum_scatter(down_w_grad, ("fsdp", "seq"), scatter_dimension=0, tiled=True),
    )
    return (
        result,
        input_grad,
        shares[0],
        shares[1].T,
        shares[2].T,
        shares[3].T,
        shares[4],
        shares[5].T,
        shares[6].T,
        shares[7],
    )


gelu_c = 0.7978845608028654
MESH = pl.DeviceIdType.MESH
DMA = pltpu.SemaphoreType.DMA


def nt(former, latter):
    return lax.dot_general(
        former, latter, (((1,), (1,)), ((), ())), preferred_element_type=jnp.float32
    )


def nn(former, latter):
    return lax.dot_general(
        former, latter, (((1,), (0,)), ((), ())), preferred_element_type=jnp.float32
    )


def tn(former, latter):
    return lax.dot_general(
        former, latter, (((0,), (0,)), ((), ())), preferred_element_type=jnp.float32
    )


class Place:
    def __init__(self):
        self.f = lax.axis_index("fsdp")
        self.s = lax.axis_index("seq")
        self.z = self.f // 2
        self.y = lax.rem(self.f, 2)
        self.core = lax.rem(self.s, 2)
        self.high = self.z // 2
        self.inner = self.z * (3 - self.z) == 2
        self.outer = self.z * (3 - self.z) == 0
        self.sibling = (self.f, self.s + 1 - 2 * self.core)
        self.over_x = (self.f, lax.rem(self.s + 2, 4))
        self.over_y = (self.f + 1 - 2 * self.y, self.s)
        self.toward = 1 - 2 * self.high

    def at_z(self, z):
        return (z * 2 + self.y, self.s)

    def source(self, j):
        last = j // 3
        middle = j // 2 - last
        none = (3 - j) // 3
        first = 1 - last - middle - none
        return (
            none * self.z
            + first * (1 - self.z + 4 * self.high)
            + middle * (2 - self.high)
            + last * (3 - 3 * self.high)
        )


def remote(source, target, send_sem, recv_sem, device):
    return pltpu.make_async_remote_copy(
        src_ref=source,
        dst_ref=target,
        send_sem=send_sem,
        recv_sem=recv_sem,
        device_id=device,
        device_id_type=MESH,
    )


def greet(partners):
    entry = pltpu.get_barrier_semaphore()
    for partner in partners:
        pl.semaphore_signal(entry, inc=1, device_id=partner, device_id_type=MESH)
    pl.semaphore_wait(entry, len(partners))


def exchange_pass(at, held, gather_sems, sum_sems, sum_bufs, part_own, compute):
    z_own, z_next, z_in, y_out, y_in, c_out, c_in = gather_sems
    t_out, t_in, v_out, v_in, w_out, w_in = sum_sems
    to_sib, from_sib, chip_sum, from_y, to_z, from_z = sum_bufs
    f, core = at.f, at.core

    def block(chip):
        return held.at[chip, core]

    def over(chip, outgoing, incoming, device):
        return remote(block(chip), block(chip), outgoing, incoming, device)

    def own_z(step, slot):
        return over(f, z_own.at[slot], z_in.at[at.z], at.at_z(at.z + step))

    def own_z_toward():
        return own_z(at.toward, 0)

    def own_z_away():
        return own_z(-at.toward, 1)

    def pass_z(src, step):
        return over(src * 2 + at.y, z_next.at[src], z_in.at[src], at.at_z(at.z + step))

    def pass_y(src):
        return over(src * 2 + at.y, y_out.at[src], y_in.at[src], at.over_y)

    def pass_sib(chip):
        return over(chip, c_out.at[chip], c_in.at[chip], at.sibling)

    own_z_toward().start()

    @pl.when(at.inner)
    def _():
        own_z_away().start()

    pass_y(at.z).start()
    pass_sib(f).start()

    def from_z_block(src):
        return over(src * 2 + at.y, z_next.at[src], z_in.at[src], at.at_z(src))

    def take_z(j, step):
        src = at.source(j)
        from_z_block(src).wait_recv()

        @pl.when(at.inner)
        def _():
            pass_z(src, step).start()

        pass_y(src).start()
        pass_sib(src * 2 + at.y).start()

    def chip_of(i):
        return at.source(i // 2) * 2 + lax.rem(at.y + lax.rem(i, 2), 2)

    def sib_sum(i):
        return remote(to_sib.at[i], from_sib.at[i], t_out.at[i], t_in.at[i], at.sibling)

    def y_sum(i):
        return remote(chip_sum.at[i], from_y.at[i // 2], v_out.at[i // 2], v_in.at[i // 2], at.over_y)

    def finish_chip(i):
        sib_sum(i).wait_recv()
        chip_sum[i] = (part_own[...] + from_sib[i].astype(jnp.float32)).astype(jnp.bfloat16)

    def step(i, carried):
        side = lax.rem(i, 2)
        chip = chip_of(i)

        @pl.when(i == 1)
        def _():
            take_z(1, at.toward)

            @pl.when(at.inner)
            def _():
                take_z(2, -at.toward)

        @pl.when((i == 3) & at.outer)
        def _():
            take_z(2, -at.toward)

        @pl.when(i == 5)
        def _():
            take_z(3, -at.toward)

        @pl.when(side == 1)
        def _():
            pass_y(at.source(i // 2)).wait_recv()
            pass_sib(chip).start()

        pass_sib(chip).wait_recv()
        own_part, sib_part = compute(chip)
        to_sib[i] = sib_part.astype(jnp.bfloat16)
        sib_sum(i).start()

        @pl.when(i > 0)
        def _():
            finish_chip(i - 1)

        part_own[...] = own_part

        @pl.when((side == 0) & (i > 2))
        def _():
            y_sum(i - 1).start()

        return carried

    lax.fori_loop(0, 8, step, 0)
    finish_chip(7)
    y_sum(7).start()
    y_sum(1).start()

    def z_sum(j):
        target = at.source(j)
        return remote(to_z.at[j - 1], from_z.at[at.z], w_out.at[j - 1], w_in.at[at.z], at.at_z(target))

    def from_z_sum(j):
        src = at.source(j)
        return remote(to_z.at[j - 1], from_z.at[src], w_out.at[j - 1], w_in.at[src], at.at_z(src))

    for j in (1, 2, 3):
        y_sum(2 * j + 1).wait_recv()
        to_z[j - 1] = (
            chip_sum[2 * j].astype(jnp.float32) + from_y[j].astype(jnp.float32)
        ).astype(jnp.bfloat16)
        z_sum(j).start()

    def finish():
        y_sum(1).wait_recv()
        total = chip_sum[0].astype(jnp.float32) + from_y[0].astype(jnp.float32)
        for j in (1, 2, 3):
            from_z_sum(j).wait_recv()
            total = total + from_z[at.source(j)].astype(jnp.float32)
        return total

    def drain():
        own_z_toward().wait_send()

        @pl.when(at.inner)
        def _():
            own_z_away().wait_send()
            for j in (1, 2, 3):
                from_z_block(at.source(j)).wait_send()

        def drain_chip(i, carried):
            pass_sib(chip_of(i)).wait_send()
            sib_sum(i).wait_send()

            @pl.when(lax.rem(i, 2) == 1)
            def _():
                pass_y(at.source(i // 2)).wait_send()
                y_sum(i).wait_send()

            return carried

        lax.fori_loop(0, 8, drain_chip, 0)
        for j in (1, 2, 3):
            z_sum(j).wait_send()

    return finish, drain


def ffn_kernel(
    normed_ref,
    middle_ref,
    cotangent_ref,
    gain_ref,
    own_gate,
    own_up,
    own_down,
    peer_gate,
    peer_up,
    peer_down,
    result_ref,
    back_ref,
    gain_grad_ref,
    gate_grad_ref,
    up_grad_ref,
    down_grad_ref,
    normed_all,
    grad_all,
    gate_keep,
    up_keep,
    peer_sum,
    part_own,
    to_sib,
    from_sib,
    chip_sum,
    from_y,
    to_z,
    from_z,
    to_x,
    from_x,
    *sems,
):
    at = Place()
    core = at.core
    fwd_gather, fwd_sum = sems[:7], sems[7:13]
    bwd_gather, bwd_sum = sems[13:20], sems[20:26]
    x_out, x_in = sems[26:28]
    sum_bufs = (to_sib, from_sib, chip_sum, from_y, to_z, from_z)
    gates, ups, downs = (own_gate, peer_gate), (own_up, peer_up), (own_down, peer_down)
    normed_all[at.f, core] = normed_ref[...]
    greet(
        [at.sibling, at.over_x, at.over_y]
        + [at.at_z(lax.rem(at.z + step, 4)) for step in (1, 2, 3)]
    )

    def rows_of(ref, chip):
        return jnp.concatenate([ref[chip, core], ref[chip, 1 - core]], axis=0)

    def forward(chip):
        rows = rows_of(normed_all, chip)
        total = None
        for half in (0, 1):
            gate = nt(rows, gates[half][...])
            up = nt(rows, ups[half][...])
            gate_keep[half, chip] = gate
            up_keep[half, chip] = up
            bend = jnp.tanh(gelu_c * (gate + 0.044715 * gate * gate * gate))
            hidden = (0.5 * gate * (1.0 + bend) * up).astype(jnp.bfloat16)
            part = nn(hidden, downs[half][...])
            total = part if total is None else total + part
        return total[:128], total[128:]

    finish, drain = exchange_pass(
        at, normed_all, fwd_gather, fwd_sum, sum_bufs, part_own, forward
    )
    ffn_raw = finish()
    drain()
    gain = gain_ref[...]
    scale = lax.rsqrt(jnp.mean(ffn_raw * ffn_raw, axis=1, keepdims=True) + norm_eps)
    result_ref[...] = (middle_ref[...] + ffn_raw * scale * gain).astype(jnp.bfloat16)
    upstream = cotangent_ref[...].astype(jnp.float32)
    weighted = upstream * gain
    inner = jnp.mean(weighted * ffn_raw, axis=1, keepdims=True)
    ffn_grad = scale * weighted - ffn_raw * (scale * scale * scale * inner)
    gain_grad_ref[...] = jnp.sum(upstream * ffn_raw * scale, axis=0, keepdims=True)
    grad_all[at.f, core] = ffn_grad.astype(jnp.bfloat16)

    grads = ((gate_grad_ref, up_grad_ref, down_grad_ref), tuple(peer_sum.at[k] for k in range(3)))
    for half in (0, 1):
        for target in grads[half]:
            target[...] = jnp.zeros(target.shape, jnp.float32)

    def backward(chip):
        rows = rows_of(grad_all, chip)
        ahead = rows_of(normed_all, chip)
        total = None
        for half in (0, 1):
            dhidden = nt(rows, downs[half][...])
            gate = gate_keep[half, chip]
            up = up_keep[half, chip]
            square = gate * gate
            bend = jnp.tanh(gelu_c * (gate + 0.044715 * square * gate))
            unit = 0.5 * gate * (1.0 + bend)
            slope = 0.5 * (1.0 + bend) + 0.5 * gate * (1.0 - bend * bend) * (
                gelu_c * (1.0 + 3 * 0.044715 * square)
            )
            hidden = (unit * up).astype(jnp.bfloat16)
            dgate = (dhidden * up * slope).astype(jnp.bfloat16)
            dup = (dhidden * unit).astype(jnp.bfloat16)
            part = nn(dgate, gates[half][...]) + nn(dup, ups[half][...])
            total = part if total is None else total + part
            gate_sum, up_sum, down_sum = grads[half]
            gate_sum[...] += tn(dgate, ahead)
            up_sum[...] += tn(dup, ahead)
            down_sum[...] += tn(hidden, rows)
        return total[:128], total[128:]

    finish, drain = exchange_pass(
        at, grad_all, bwd_gather, bwd_sum, sum_bufs, part_own, backward
    )

    def x_copy(which):
        return remote(to_x.at[which], from_x.at[which], x_out.at[which], x_in.at[which], at.over_x)

    for which in range(3):
        to_x[which] = peer_sum[which].astype(jnp.bfloat16)
        x_copy(which).start()
    back_ref[...] = finish()
    drain()
    for which in range(3):
        x_copy(which).wait()
        grads[0][which][...] += from_x[which].astype(jnp.float32)


def ffn_both(normed, middle, cotangent, gain, own, peer):
    rows, width = normed.shape
    units = own[0].shape[0]
    b16, f32 = jnp.bfloat16, jnp.float32
    vmem = pl.BlockSpec(memory_space=pltpu.VMEM)
    gather_sems = [DMA((2,)), DMA((4,)), DMA((4,)), DMA((4,)), DMA((4,)), DMA((8,)), DMA((8,))]
    sum_sems = [DMA((8,)), DMA((8,)), DMA((4,)), DMA((4,)), DMA((3,)), DMA((4,))]
    return pl.pallas_call(
        ffn_kernel,
        out_shape=(
            jax.ShapeDtypeStruct((rows, width), b16),
            jax.ShapeDtypeStruct((rows, width), f32),
            jax.ShapeDtypeStruct((1, width), f32),
            jax.ShapeDtypeStruct((units, width), f32),
            jax.ShapeDtypeStruct((units, width), f32),
            jax.ShapeDtypeStruct((units, width), f32),
        ),
        in_specs=[vmem] * 10,
        out_specs=[vmem] * 6,
        scratch_shapes=[
            pltpu.VMEM((8, 2, rows, width), b16),
            pltpu.VMEM((8, 2, rows, width), b16),
            pltpu.VMEM((2, 8, 2 * rows, units), f32),
            pltpu.VMEM((2, 8, 2 * rows, units), f32),
            pltpu.VMEM((3, units, width), f32),
            pltpu.VMEM((rows, width), f32),
            pltpu.VMEM((8, rows, width), b16),
            pltpu.VMEM((8, rows, width), b16),
            pltpu.VMEM((8, rows, width), b16),
            pltpu.VMEM((4, rows, width), b16),
            pltpu.VMEM((3, rows, width), b16),
            pltpu.VMEM((4, rows, width), b16),
            pltpu.VMEM((3, units, width), b16),
            pltpu.VMEM((3, units, width), b16),
        ]
        + (gather_sems + sum_sems) * 2
        + [DMA((3,)), DMA((3,))],
        compiler_params=pltpu.CompilerParams(
            collective_id=1, has_side_effects=True, vmem_limit_bytes=62 << 20
        ),
        name="ffn_both",
    )(normed, middle, cotangent, gain, *own, *peer)


def gather_rows(block):
    return lax.all_gather(block, ("fsdp", "seq"), axis=0, tiled=True)


def scatter_rows(partial_sum):
    return lax.psum_scatter(
        partial_sum.astype(jnp.bfloat16), ("fsdp", "seq"), scatter_dimension=0, tiled=True
    ).astype(jnp.float32)


def split_model(
    tokens, doc_start, gains, w_query, w_key, w_value, w_out, w_gate, w_up, w_down, cotangent
):
    tok_rows, model_width = tokens.shape
    run_index = lax.axis_index("seq")
    seq_count = lax.axis_size("seq")
    dev_count = seq_count * lax.axis_size("fsdp")
    query_rows, key_rows_own = w_query.shape[1], w_key.shape[1]
    gain_row = jnp.pad(gains[None, :], ((0, 7), (0, model_width - gains.shape[0])))
    packed = jnp.concatenate([w_query.T, w_out, w_key.T, w_value.T, gain_row], axis=0)
    cuts = (query_rows, 2 * query_rows, 2 * query_rows + key_rows_own)
    cuts = cuts + (cuts[2] + key_rows_own,)
    everything = gather_rows(packed).reshape(dev_count, packed.shape[0], model_width)
    query_t = everything[:, : cuts[0]].reshape(-1, model_width)
    out_w = everything[:, cuts[0] : cuts[1]].reshape(-1, model_width)
    key_t = everything[:, cuts[1] : cuts[2]].reshape(-1, model_width)
    value_t = everything[:, cuts[2] : cuts[3]].reshape(-1, model_width)
    gain_values = everything[:, cuts[3], : gains.shape[0]].reshape(-1).astype(jnp.float32)
    head_width = key_t.shape[0]
    head_count = query_t.shape[0] // head_width
    places_in = [0, model_width, model_width + head_width, model_width + 2 * head_width]
    places_in += [places_in[3] + model_width, places_in[3] + 2 * model_width, gain_values.shape[0]]
    places_in[5:] = [places_in[4] + model_width, places_in[4] + 2 * model_width]
    gain_pre, gain_query, gain_key, gain_post, gain_pre_ffn, gain_post_ffn = (
        gain_values[first:last] for first, last in zip(places_in[:-1], places_in[1:])
    )
    residual = tokens.astype(jnp.float32)
    normed, pre_pull = jax.vjp(scaled_norm, residual, gain_pre)
    normed_b = normed.astype(jnp.bfloat16)
    query_raw = outer_rows(normed_b, query_t).reshape(tok_rows, head_count, head_width)
    key_raw = outer_rows(normed_b, key_t).reshape(tok_rows, 1, head_width)
    value_b = outer_rows(normed_b, value_t).astype(jnp.bfloat16)
    places = run_index * tok_rows + jnp.arange(tok_rows, dtype=jnp.int32) - doc_start
    cos_table, sin_table = rope_tables(places, head_width)
    rope_norm = partial(head_norm, cos_table=cos_table, sin_table=sin_table)
    query_rot, query_pull = jax.vjp(rope_norm, query_raw, gain_query)
    key_rot, key_pull = jax.vjp(rope_norm, key_raw, gain_key)
    query_b = query_rot.astype(jnp.bfloat16).transpose(1, 0, 2).reshape(-1, head_width)
    key_b = key_rot.reshape(tok_rows, head_width).astype(jnp.bfloat16)
    both = lax.all_gather(jnp.concatenate([key_b, value_b], axis=1), "seq", axis=0, tiled=True)
    key_rows, value_rows = both[:, :head_width], both[:, head_width:]
    raw_scores = outer_rows(query_b, key_rows) * score_scale
    query_place = run_index * tok_rows + jnp.arange(tok_rows, dtype=jnp.int32)
    key_place = jnp.arange(key_rows.shape[0], dtype=jnp.int32)
    allowed = (key_place[None, :] >= doc_start[:, None]) & (
        key_place[None, :] <= query_place[:, None]
    )
    allowed = jnp.tile(allowed, (head_count, 1))
    scores = jnp.where(allowed, raw_scores, masked_value)
    row_max = jnp.max(scores, axis=1, keepdims=True)
    weights = jnp.exp(scores - row_max)
    probability = weights / jnp.sum(weights, axis=1, keepdims=True)
    probability_b = probability.astype(jnp.bfloat16)
    mixed = product(probability_b, value_rows).astype(jnp.bfloat16)
    mixed_tokens = (
        mixed.reshape(head_count, tok_rows, head_width).transpose(1, 0, 2).reshape(tok_rows, -1)
    )
    attn_raw = product(mixed_tokens, out_w)
    attn_out, post_pull = jax.vjp(scaled_norm, attn_raw, gain_post)
    middle = residual + attn_out
    normed_ffn, pre_ffn_pull = jax.vjp(scaled_norm, middle, gain_pre_ffn)
    own_ffn = (w_gate.T, w_up.T, w_down)
    peer_ffn = tuple(
        lax.ppermute(block, "seq", [(0, 2), (2, 0), (1, 3), (3, 1)]) for block in own_ffn
    )
    result, normed_ffn_grad, gain_post_ffn_grad, gate_w_grad_t, up_w_grad_t, down_grad = ffn_both(
        normed_ffn.astype(jnp.bfloat16), middle, cotangent, gain_post_ffn[None], own_ffn, peer_ffn
    )
    gain_post_ffn_grad = gain_post_ffn_grad[0]
    upstream = cotangent.astype(jnp.float32)
    middle_part, gain_pre_ffn_grad = pre_ffn_pull(normed_ffn_grad)
    middle_grad = upstream + middle_part
    attn_grad, gain_post_grad = post_pull(middle_grad)
    attn_grad_b = attn_grad.astype(jnp.bfloat16)
    out_w_grad = inner_rows(mixed_tokens, attn_grad_b)
    mixed_grad = outer_rows(attn_grad_b, out_w).astype(jnp.bfloat16)
    mixed_grad = (
        mixed_grad.reshape(tok_rows, head_count, head_width)
        .transpose(1, 0, 2)
        .reshape(-1, head_width)
    )
    prob_grad = outer_rows(mixed_grad, value_rows)
    value_part = inner_rows(probability_b, mixed_grad)
    row_delta = jnp.sum(probability * prob_grad, axis=1, keepdims=True)
    score_grad = (probability * (prob_grad - row_delta)).astype(jnp.bfloat16)
    query_grad = product(score_grad, key_rows) * score_scale
    key_part = inner_rows(score_grad, query_b) * score_scale
    both_sum = lax.psum_scatter(
        jnp.concatenate([key_part, value_part], axis=1).astype(jnp.bfloat16),
        "seq",
        scatter_dimension=0,
        tiled=True,
    ).astype(jnp.float32)
    query_raw_grad, gain_query_grad = query_pull(
        query_grad.reshape(head_count, tok_rows, head_width).transpose(1, 0, 2)
    )
    key_raw_grad, gain_key_grad = key_pull(both_sum[:, None, :head_width])
    query_raw_b = query_raw_grad.reshape(tok_rows, -1).astype(jnp.bfloat16)
    key_raw_b = key_raw_grad.reshape(tok_rows, head_width).astype(jnp.bfloat16)
    value_raw_b = both_sum[:, head_width:].astype(jnp.bfloat16)
    normed_grad = (
        product(query_raw_b, query_t) + product(key_raw_b, key_t) + product(value_raw_b, value_t)
    )
    residual_part, gain_pre_grad = pre_pull(normed_grad)
    input_grad = middle_grad + residual_part
    gains_grad = jnp.concatenate(
        [
            gain_pre_grad,
            gain_query_grad,
            gain_key_grad,
            gain_post_grad,
            gain_pre_ffn_grad,
            gain_post_ffn_grad,
        ]
    )
    gains_block = jnp.pad(
        gains_grad.reshape(dev_count, 1, -1),
        ((0, 0), (0, 7), (0, model_width - gains.shape[0])),
    )
    by_device = lambda rows: rows.reshape(dev_count, -1, model_width)
    shares = scatter_rows(
        jnp.concatenate(
            [
                by_device(inner_rows(query_raw_b, normed_b)),
                by_device(out_w_grad),
                by_device(inner_rows(key_raw_b, normed_b)),
                by_device(inner_rows(value_raw_b, normed_b)),
                gains_block,
            ],
            axis=1,
        ).reshape(-1, model_width)
    )
    return (
        result,
        input_grad,
        shares[cuts[3], : gains.shape[0]],
        shares[: cuts[0]].T,
        shares[cuts[1] : cuts[2]].T,
        shares[cuts[2] : cuts[3]].T,
        shares[cuts[0] : cuts[1]],
        gate_w_grad_t.T,
        up_w_grad_t.T,
        down_grad,
    )


def solution(mesh):
    in_specs = (
        P(("fsdp", "seq"), None),
        P(("fsdp", "seq")),
        P(("fsdp", "seq")),
        P(None, ("fsdp", "seq")),
        P(None, ("fsdp", "seq")),
        P(None, ("fsdp", "seq")),
        P(("fsdp", "seq"), None),
        P(None, ("fsdp", "seq")),
        P(None, ("fsdp", "seq")),
        P(("fsdp", "seq"), None),
        P(("fsdp", "seq"), None),
    )
    out_specs = (
        P(("fsdp", "seq"), None),
        P(("fsdp", "seq"), None),
        P(("fsdp", "seq")),
        P(None, ("fsdp", "seq")),
        P(None, ("fsdp", "seq")),
        P(None, ("fsdp", "seq")),
        P(("fsdp", "seq"), None),
        P(None, ("fsdp", "seq")),
        P(None, ("fsdp", "seq")),
        P(("fsdp", "seq"), None),
    )
    body = split_model if dict(mesh.shape) == {"fsdp": 8, "seq": 4} else local
    return jax.shard_map(body, mesh=mesh, in_specs=in_specs, out_specs=out_specs, check_vma=False)
```

```python
from functools import partial

import jax
import jax.numpy as jnp
from jax import lax
from jax.experimental import pallas as pl
from jax.experimental.pallas import tpu as pltpu
from jax.sharding import PartitionSpec as P

norm_eps = 1e-06
rope_base = 1000000.0
score_scale = 0.0625
masked_value = -1e30


def product(former, latter):
    return jnp.dot(former, latter, preferred_element_type=jnp.float32)


def inner_rows(former, latter):
    return lax.dot_general(
        former, latter, (((0,), (0,)), ((), ())), preferred_element_type=jnp.float32
    )


def outer_rows(former, latter):
    return lax.dot_general(
        former, latter, (((1,), (1,)), ((), ())), preferred_element_type=jnp.float32
    )


def scaled_norm(values, factor):
    return values * lax.rsqrt(jnp.mean(values * values, axis=-1, keepdims=True) + norm_eps) * factor


def rotate(values, cos_table, sin_table):
    half_width = values.shape[-1] // 2
    leading = values[..., :half_width]
    trailing = values[..., half_width:]
    return jnp.concatenate(
        [leading * cos_table - trailing * sin_table, trailing * cos_table + leading * sin_table],
        axis=-1,
    )


def head_norm(values, factor, cos_table, sin_table):
    return rotate(scaled_norm(values, factor), cos_table, sin_table)


def gated_unit(gate_in, up_in):
    return jax.nn.gelu(gate_in, approximate=True) * up_in


def rope_tables(places, rot_width):
    half_width = rot_width // 2
    frequency = rope_base ** (-2.0 * jnp.arange(half_width, dtype=jnp.float32) / rot_width)
    angles = places.astype(jnp.float32)[:, None] * frequency[None, :]
    return (jnp.cos(angles)[:, None, :], jnp.sin(angles)[:, None, :])


def masked_scores(queries, key_rows, bounds, offset):
    raw_scores = outer_rows(queries, key_rows) * score_scale
    query_place = offset + jnp.arange(queries.shape[0], dtype=jnp.int32)
    key_place = jnp.arange(key_rows.shape[0], dtype=jnp.int32)
    allowed = (key_place[None, :] >= bounds[:, None]) & (key_place[None, :] <= query_place[:, None])
    return jnp.where(allowed, raw_scores, masked_value)


def local(
    tokens, doc_start, gains, w_query, w_key, w_value, w_out, w_gate, w_up, w_down, cotangent
):
    tok_rows = tokens.shape[0]
    model_width = tokens.shape[1]
    run_index = lax.axis_index("seq")
    gains_all, query_w, key_w, value_w, out_w = (
        lax.all_gather(gains, ("fsdp", "seq"), axis=0, tiled=True),
        lax.all_gather(w_query, ("fsdp", "seq"), axis=1, tiled=True),
        lax.all_gather(w_key, ("fsdp", "seq"), axis=1, tiled=True),
        lax.all_gather(w_value, ("fsdp", "seq"), axis=1, tiled=True),
        lax.all_gather(w_out, ("fsdp", "seq"), axis=0, tiled=True),
    )
    gate_w, up_w, down_w = (
        lax.all_gather(w_gate, ("fsdp", "seq"), axis=1, tiled=True),
        lax.all_gather(w_up, ("fsdp", "seq"), axis=1, tiled=True),
        lax.all_gather(w_down, ("fsdp", "seq"), axis=0, tiled=True),
    )
    head_width = key_w.shape[1]
    head_count = query_w.shape[1] // head_width
    gain_values = gains_all.astype(jnp.float32)
    gain_pre = gain_values[:model_width]
    gain_query = gain_values[model_width : model_width + head_width]
    gain_key = gain_values[model_width + head_width : model_width + 2 * head_width]
    gain_post = gain_values[model_width + 2 * head_width : 2 * model_width + 2 * head_width]
    gain_pre_ffn = gain_values[2 * model_width + 2 * head_width : 3 * model_width + 2 * head_width]
    gain_post_ffn = gain_values[3 * model_width + 2 * head_width :]
    residual = tokens.astype(jnp.float32)
    normed, pre_pull = jax.vjp(scaled_norm, residual, gain_pre)
    normed_b = normed.astype(jnp.bfloat16)
    query_raw = product(normed_b, query_w).reshape(tok_rows, head_count, head_width)
    key_raw = product(normed_b, key_w).reshape(tok_rows, 1, head_width)
    value_b = product(normed_b, value_w).astype(jnp.bfloat16)
    places = run_index * tok_rows + jnp.arange(tok_rows, dtype=jnp.int32) - doc_start
    cos_table, sin_table = rope_tables(places, head_width)
    rope_norm = partial(head_norm, cos_table=cos_table, sin_table=sin_table)
    query_rot, query_pull = jax.vjp(rope_norm, query_raw, gain_query)
    key_rot, key_pull = jax.vjp(rope_norm, key_raw, gain_key)
    query_b = query_rot.reshape(tok_rows, head_count * head_width).astype(jnp.bfloat16)
    key_b = key_rot.reshape(tok_rows, head_width).astype(jnp.bfloat16)
    query_heads = lax.all_to_all(query_b, "seq", split_axis=1, concat_axis=0, tiled=True)
    key_rows, value_rows = (
        lax.all_gather(key_b, "seq", axis=0, tiled=True),
        lax.all_gather(value_b, "seq", axis=0, tiled=True),
    )
    starts = lax.all_gather(doc_start, "seq", axis=0, tiled=True)
    seq_tokens = key_rows.shape[0]
    block_rows = min(512, seq_tokens)
    block_count = seq_tokens // block_rows
    query_blocks = query_heads.reshape(block_count, block_rows, head_width)
    start_blocks = starts.reshape(block_count, block_rows)
    block_ids = jnp.arange(block_count, dtype=jnp.int32)

    def attend(block_item):
        queries, bounds, block_index = block_item
        scores = masked_scores(queries, key_rows, bounds, block_index * block_rows)
        row_max = jnp.max(scores, axis=1, keepdims=True)
        weights = jnp.exp(scores - row_max)
        row_total = jnp.sum(weights, axis=1, keepdims=True)
        probability = (weights / row_total).astype(jnp.bfloat16)
        mixed_block = product(probability, value_rows).astype(jnp.bfloat16)
        return (mixed_block, (row_max + jnp.log(row_total))[:, 0])

    mixed_blocks, lse_blocks = lax.map(attend, (query_blocks, start_blocks, block_ids))
    mixed_heads = mixed_blocks.reshape(seq_tokens, head_width)
    mixed_tokens = lax.all_to_all(mixed_heads, "seq", split_axis=0, concat_axis=1, tiled=True)
    attn_raw = product(mixed_tokens, out_w)
    attn_out, post_pull = jax.vjp(scaled_norm, attn_raw, gain_post)
    middle = residual + attn_out
    normed_ffn, pre_ffn_pull = jax.vjp(scaled_norm, middle, gain_pre_ffn)
    normed_ffn_b = normed_ffn.astype(jnp.bfloat16)
    gate_act = product(normed_ffn_b, gate_w)
    up_act = product(normed_ffn_b, up_w)
    hidden, glu_pull = jax.vjp(gated_unit, gate_act, up_act)
    hidden_b = hidden.astype(jnp.bfloat16)
    ffn_raw = product(hidden_b, down_w)
    ffn_out, post_ffn_pull = jax.vjp(scaled_norm, ffn_raw, gain_post_ffn)
    result = (middle + ffn_out).astype(jnp.bfloat16)
    gate_w, up_w, down_w = (
        lax.all_gather(w_gate, ("fsdp", "seq"), axis=1, tiled=True),
        lax.all_gather(w_up, ("fsdp", "seq"), axis=1, tiled=True),
        lax.all_gather(w_down, ("fsdp", "seq"), axis=0, tiled=True),
    )
    query_w, key_w, value_w, out_w = (
        lax.all_gather(w_query, ("fsdp", "seq"), axis=1, tiled=True),
        lax.all_gather(w_key, ("fsdp", "seq"), axis=1, tiled=True),
        lax.all_gather(w_value, ("fsdp", "seq"), axis=1, tiled=True),
        lax.all_gather(w_out, ("fsdp", "seq"), axis=0, tiled=True),
    )
    upstream = cotangent.astype(jnp.float32)
    ffn_grad, gain_post_ffn_grad = post_ffn_pull(upstream)
    ffn_grad_b = ffn_grad.astype(jnp.bfloat16)
    down_w_grad = inner_rows(hidden_b, ffn_grad_b)
    hidden_grad = outer_rows(ffn_grad_b, down_w)
    gate_grad, up_grad = glu_pull(hidden_grad)
    gate_grad_b = gate_grad.astype(jnp.bfloat16)
    up_grad_b = up_grad.astype(jnp.bfloat16)
    gate_w_grad_t = inner_rows(gate_grad_b, normed_ffn_b)
    up_w_grad_t = inner_rows(up_grad_b, normed_ffn_b)
    normed_ffn_grad = outer_rows(gate_grad_b, gate_w) + outer_rows(up_grad_b, up_w)
    middle_part, gain_pre_ffn_grad = pre_ffn_pull(normed_ffn_grad)
    middle_grad = upstream + middle_part
    attn_grad, gain_post_grad = post_pull(middle_grad)
    attn_grad_b = attn_grad.astype(jnp.bfloat16)
    out_w_grad = inner_rows(mixed_tokens, attn_grad_b)
    mixed_grad = outer_rows(attn_grad_b, out_w).astype(jnp.bfloat16)
    mixed_grad_heads = lax.all_to_all(mixed_grad, "seq", split_axis=1, concat_axis=0, tiled=True)
    grad_blocks = mixed_grad_heads.reshape(block_count, block_rows, head_width)

    def attend_back(carried, block_item):
        key_accum, value_accum = carried
        queries, bounds, block_index, lse_row, block_grad = block_item
        scores = masked_scores(queries, key_rows, bounds, block_index * block_rows)
        probability = jnp.exp(scores - lse_row[:, None])
        prob_grad = outer_rows(block_grad, value_rows)
        value_accum = value_accum + inner_rows(probability.astype(jnp.bfloat16), block_grad)
        row_delta = jnp.sum(probability * prob_grad, axis=1, keepdims=True)
        score_grad = (probability * (prob_grad - row_delta)).astype(jnp.bfloat16)
        query_grad = product(score_grad, key_rows) * score_scale
        key_accum = key_accum + inner_rows(score_grad, queries) * score_scale
        return ((key_accum, value_accum), query_grad)

    zero_rows = jnp.zeros((seq_tokens, head_width), jnp.float32)
    (key_part, value_part), query_grad_blocks = lax.scan(
        attend_back,
        (zero_rows, zero_rows),
        (query_blocks, start_blocks, block_ids, lse_blocks, grad_blocks),
    )
    key_sum, value_sum = (
        lax.psum_scatter(
            key_part.astype(jnp.bfloat16), "seq", scatter_dimension=0, tiled=True
        ).astype(jnp.float32),
        lax.psum_scatter(
            value_part.astype(jnp.bfloat16), "seq", scatter_dimension=0, tiled=True
        ).astype(jnp.float32),
    )
    query_grad_tokens = lax.all_to_all(
        query_grad_blocks.reshape(seq_tokens, head_width).astype(jnp.bfloat16),
        "seq",
        split_axis=0,
        concat_axis=1,
        tiled=True,
    ).astype(jnp.float32)
    query_raw_grad, gain_query_grad = query_pull(
        query_grad_tokens.reshape(tok_rows, head_count, head_width)
    )
    key_raw_grad, gain_key_grad = key_pull(key_sum.reshape(tok_rows, 1, head_width))
    query_raw_b = query_raw_grad.reshape(tok_rows, head_count * head_width).astype(jnp.bfloat16)
    key_raw_b = key_raw_grad.reshape(tok_rows, head_width).astype(jnp.bfloat16)
    value_raw_b = value_sum.astype(jnp.bfloat16)
    query_w_grad_t = inner_rows(query_raw_b, normed_b)
    key_w_grad_t = inner_rows(key_raw_b, normed_b)
    value_w_grad_t = inner_rows(value_raw_b, normed_b)
    normed_grad = (
        outer_rows(query_raw_b, query_w)
        + outer_rows(key_raw_b, key_w)
        + outer_rows(value_raw_b, value_w)
    )
    residual_part, gain_pre_grad = pre_pull(normed_grad)
    input_grad = middle_grad + residual_part
    gains_grad = jnp.concatenate(
        [
            gain_pre_grad,
            gain_query_grad,
            gain_key_grad,
            gain_post_grad,
            gain_pre_ffn_grad,
            gain_post_ffn_grad,
        ]
    )
    shares = (
        lax.psum_scatter(gains_grad, ("fsdp", "seq"), scatter_dimension=0, tiled=True),
        lax.psum_scatter(query_w_grad_t, ("fsdp", "seq"), scatter_dimension=0, tiled=True),
        lax.psum_scatter(key_w_grad_t, ("fsdp", "seq"), scatter_dimension=0, tiled=True),
        lax.psum_scatter(value_w_grad_t, ("fsdp", "seq"), scatter_dimension=0, tiled=True),
        lax.psum_scatter(out_w_grad, ("fsdp", "seq"), scatter_dimension=0, tiled=True),
        lax.psum_scatter(gate_w_grad_t, ("fsdp", "seq"), scatter_dimension=0, tiled=True),
        lax.psum_scatter(up_w_grad_t, ("fsdp", "seq"), scatter_dimension=0, tiled=True),
        lax.psum_scatter(down_w_grad, ("fsdp", "seq"), scatter_dimension=0, tiled=True),
    )
    return (
        result,
        input_grad,
        shares[0],
        shares[1].T,
        shares[2].T,
        shares[3].T,
        shares[4],
        shares[5].T,
        shares[6].T,
        shares[7],
    )


gelu_c = 0.7978845608028654
MESH = pl.DeviceIdType.MESH
DMA = pltpu.SemaphoreType.DMA


def nt(former, latter):
    return lax.dot_general(
        former, latter, (((1,), (1,)), ((), ())), preferred_element_type=jnp.float32
    )


def nn(former, latter):
    return lax.dot_general(
        former, latter, (((1,), (0,)), ((), ())), preferred_element_type=jnp.float32
    )


def tn(former, latter):
    return lax.dot_general(
        former, latter, (((0,), (0,)), ((), ())), preferred_element_type=jnp.float32
    )


class Place:
    def __init__(self):
        self.f = lax.axis_index("fsdp")
        self.s = lax.axis_index("seq")
        self.z = self.f // 2
        self.y = lax.rem(self.f, 2)
        self.core = lax.rem(self.s, 2)
        self.high = self.z // 2
        self.inner = self.z * (3 - self.z) == 2
        self.outer = self.z * (3 - self.z) == 0
        self.sibling = (self.f, self.s + 1 - 2 * self.core)
        self.over_x = (self.f, lax.rem(self.s + 2, 4))
        self.over_y = (self.f + 1 - 2 * self.y, self.s)
        self.toward = 1 - 2 * self.high
        self.step_first = self.toward * (1 - self.z * (3 - self.z))

    def at_z(self, z):
        return (z * 2 + self.y, self.s)

    def source(self, j):
        last = j // 3
        middle = j // 2 - last
        none = (3 - j) // 3
        first = 1 - last - middle - none
        return (
            none * self.z
            + first * (1 - self.z + 4 * self.high)
            + middle * (2 - self.high)
            + last * (3 - 3 * self.high)
        )


def remote(source, target, send_sem, recv_sem, device):
    return pltpu.make_async_remote_copy(
        src_ref=source,
        dst_ref=target,
        send_sem=send_sem,
        recv_sem=recv_sem,
        device_id=device,
        device_id_type=MESH,
    )


def greet(partners):
    entry = pltpu.get_barrier_semaphore()
    for partner in partners:
        pl.semaphore_signal(entry, inc=1, device_id=partner, device_id_type=MESH)
    pl.semaphore_wait(entry, len(partners))


def exchange_pass(at, held, gather_sems, sum_sems, sum_bufs, part_own, compute, lag=0, ready=None, then=None):
    z_own, z_next, z_in, y_out, y_in, c_out, c_in = gather_sems
    t_out, t_in, v_out, v_in, w_out, w_in = sum_sems
    to_sib, from_sib, chip_sum, from_y, to_z, from_z = sum_bufs
    f, core = at.f, at.core

    def block(chip):
        return held.at[chip, core]

    def over(chip, outgoing, incoming, device):
        return remote(block(chip), block(chip), outgoing, incoming, device)

    def own_z(step, slot):
        return over(f, z_own.at[slot], z_in.at[at.z], at.at_z(at.z + step))

    def own_z_toward():
        return own_z(at.toward, 0)

    def own_z_away():
        return own_z(-at.toward, 1)

    def pass_z(src, step):
        return over(src * 2 + at.y, z_next.at[src], z_in.at[src], at.at_z(at.z + step))

    def pass_y(src):
        return over(src * 2 + at.y, y_out.at[src], y_in.at[src], at.over_y)

    def pass_sib(chip):
        return over(chip, c_out.at[chip], c_in.at[chip], at.sibling)

    own_z_toward().start()

    @pl.when(at.inner)
    def _():
        own_z_away().start()

    pass_y(at.z).start()
    pass_sib(f).start()

    def from_z_block(src):
        return over(src * 2 + at.y, z_next.at[src], z_in.at[src], at.at_z(src))

    def take_z(j, step):
        src = at.source(j)
        from_z_block(src).wait_recv()

        @pl.when(at.inner)
        def _():
            pass_z(src, step).start()

        pass_y(src).start()
        pass_sib(src * 2 + at.y).start()

    def chip_of(i):
        return at.source(i // 2) * 2 + lax.rem(at.y + lax.rem(i, 2), 2)

    def sib_sum(i):
        return remote(to_sib.at[i], from_sib.at[i], t_out.at[i], t_in.at[i], at.sibling)

    def y_sum(i):
        return remote(chip_sum.at[i], from_y.at[i // 2], v_out.at[i // 2], v_in.at[i // 2], at.over_y)

    def finish_chip(i):
        sib_sum(i).wait_recv()
        chip_sum[i] = (part_own[...] + from_sib[i].astype(jnp.float32)).astype(jnp.bfloat16)

    def arrivals(i):
        @pl.when(i == 1)
        def _():
            take_z(1, at.toward)

            @pl.when(at.inner)
            def _():
                take_z(2, -at.toward)

        @pl.when((i == 3) & at.outer)
        def _():
            take_z(2, -at.toward)

        @pl.when(((i == 3) & at.inner) | ((i == 5) & at.outer))
        def _():
            take_z(3, -at.toward)

        @pl.when(lax.rem(i, 2) == 1)
        def _():
            pass_y(at.source(i // 2)).wait_recv()
            pass_sib(chip_of(i)).start()

    def one_chip(i):
        chip = chip_of(i)
        pass_sib(chip).wait_recv()
        own_part, sib_part = compute(chip)
        to_sib[i] = sib_part.astype(jnp.bfloat16)
        sib_sum(i).start()

        @pl.when(i > 0)
        def _():
            finish_chip(i - 1)

        part_own[...] = own_part

    def step(i, carried):
        @pl.when(i < 8)
        def _():
            arrivals(i)

        if ready is not None:

            @pl.when(i == lag)
            def _():
                ready()

        @pl.when(i >= lag)
        def _():
            one_chip(i - lag)

        return carried

    lax.fori_loop(0, 8 + lag, step, 0)
    finish_chip(7)
    for j in (3, 2, 1, 0):
        y_sum(2 * j + 1).start()
    if then is not None:
        then()

    def z_sum(target, direction):
        slot = (direction + 1) // 2
        return remote(
            to_z.at[target],
            from_z.at[slot, target],
            w_out.at[target],
            w_in.at[slot, target],
            at.at_z(at.z + direction),
        )

    def z_arrival(target, direction):
        slot = (direction + 1) // 2
        return remote(
            to_z.at[target],
            from_z.at[slot, target],
            w_out.at[target],
            w_in.at[slot, target],
            at.at_z(lax.rem(at.z - direction + 4, 4)),
        )

    def direction_of(j):
        return at.step_first if j == 1 else at.toward

    for j in (3, 2, 1):
        target, direction = at.source(j), direction_of(j)
        y_sum(2 * j + 1).wait_recv()
        mine = chip_sum[2 * j].astype(jnp.float32) + from_y[j].astype(jnp.float32)

        @pl.when(at.outer)
        def _():
            to_z[target] = mine.astype(jnp.bfloat16)

        @pl.when(at.inner)
        def _():
            z_arrival(target, direction).wait_recv()
            ahead = from_z[(direction + 1) // 2, target].astype(jnp.float32)
            to_z[target] = (mine + ahead).astype(jnp.bfloat16)

        z_sum(target, direction).start()

    def finish():
        y_sum(1).wait_recv()
        part_own[...] = chip_sum[0].astype(jnp.float32) + from_y[0].astype(jnp.float32)
        z_arrival(at.z, -at.toward).wait_recv()
        part_own[...] += from_z[(1 - at.toward) // 2, at.z].astype(jnp.float32)

        @pl.when(at.inner)
        def _():
            z_arrival(at.z, at.toward).wait_recv()
            part_own[...] += from_z[(1 + at.toward) // 2, at.z].astype(jnp.float32)

        return part_own[...]

    def drain():
        own_z_toward().wait_send()

        @pl.when(at.inner)
        def _():
            own_z_away().wait_send()
            for j in (1, 2, 3):
                from_z_block(at.source(j)).wait_send()

        def drain_chip(i, carried):
            pass_sib(chip_of(i)).wait_send()
            sib_sum(i).wait_send()

            @pl.when(lax.rem(i, 2) == 1)
            def _():
                pass_y(at.source(i // 2)).wait_send()
                y_sum(i).wait_send()

            return carried

        lax.fori_loop(0, 8, drain_chip, 0)
        for j in (1, 2, 3):
            z_sum(at.source(j), direction_of(j)).wait_send()

    return finish, drain


gain_edges = (0, 1152, 1408, 1664, 2816, 3968, 5120)
score_step = 0.0625
hidden_score = -1e30


def shape_spec(shape, dtype):
    return jax.ShapeDtypeStruct(shape, dtype)


def rms_scale(values):
    return lax.rsqrt(jnp.mean(values * values, axis=-1, keepdims=True) + norm_eps)


def norm_back(values, gain, upstream):
    scale = rms_scale(values)
    weighted = upstream * gain
    inner = jnp.mean(weighted * values, axis=-1, keepdims=True)
    back = scale * weighted - values * (scale * scale * scale * inner)
    return back, jnp.sum(upstream * values * scale, axis=0, keepdims=True)


def pick(offset):
    row = lax.broadcasted_iota(jnp.int32, (256, 512), 0)
    column = lax.broadcasted_iota(jnp.int32, (256, 512), 1)
    wanted = row // 8 * 16 + lax.rem(row, 8) + offset
    return jnp.where(column == wanted, 1.0, 0.0).astype(jnp.bfloat16)


def rows_of_all(w_all, low, count):
    return jnp.concatenate(
        [w_all[d // 2, d % 2, low : low + count] for d in range(32)], axis=0
    )


def rows_of_head(w_all, head, low, count):
    return jnp.concatenate(
        [w_all[d // 2, d % 2, low : low + count] for d in range(8 * head, 8 * head + 8)], axis=0
    )


class GainGather:
    def __init__(self, at, held, sems):
        self.at, self.held = at, held
        self.out, self.inc, self.z_out, self.z_in = sems
        x = at.s // 2
        self.spans = (
            (at.f * 4 + at.s, 1, at.sibling),
            (at.f * 4 + 2 * x, 2, at.over_x),
            (at.f * 4, 4, at.over_y),
        )

    def stage(self, k):
        first, count, partner = self.spans[k]
        span = self.held.at[pl.ds(first, count)]
        return remote(span, span, self.out.at[k], self.inc.at[k], partner)

    def last(self, src, j, device):
        span = self.held.at[pl.ds(src * 8, 8)]
        return remote(span, span, self.z_out.at[j], self.z_in.at[src], device)

    def run(self):
        at = self.at
        for k in range(3):
            self.stage(k).start()
            self.stage(k).wait_recv()
        for j in (1, 2, 3):
            self.last(at.z, j, at.at_z(at.source(j))).start()
        for j in (1, 2, 3):
            self.last(at.source(j), j, at.at_z(at.source(j))).wait_recv()

    def drain(self):
        at = self.at
        for k in range(3):
            self.stage(k).wait_send()
        for j in (1, 2, 3):
            self.last(at.z, j, at.at_z(at.source(j))).wait_send()


class WeightGather:
    def __init__(self, at, w_all, sems, part, low, middle, high):
        self.at, self.w_all, self.part = at, w_all, part
        (
            self.z_own,
            self.z_next,
            self.z_in,
            self.yf_out,
            self.yf_in,
            self.xf_out,
            self.xf_in,
            self.yh_out,
            self.yh_in,
            self.xh_out,
            self.xh_in,
            self.s_out,
            self.s_in,
        ) = sems
        self.low, self.middle, self.high = low, middle, high
        self.x = at.s // 2

    def block(self, z, y, x, low, high):
        chip = (z * 2 + y) * 2 + x
        return self.w_all.at[chip, self.at.core, pl.ds(low, high - low)]

    def whole(self, z, outgoing, incoming, device):
        span = self.block(z, self.at.y, self.x, self.low, self.high)
        return remote(span, span, outgoing, incoming, device)

    def own(self, step, slot):
        at, p = self.at, self.part
        return self.whole(at.z, self.z_own.at[p, slot], self.z_in.at[p, at.z], at.at_z(at.z + step))

    def passed(self, src, device):
        p = self.part
        return self.whole(src, self.z_next.at[p, src], self.z_in.at[p, src], device)

    def y_full(self, src):
        p = self.part
        return self.whole(src, self.yf_out.at[p, src], self.yf_in.at[p, src], self.at.over_y)

    def x_full(self, src):
        p = self.part
        return self.whole(src, self.xf_out.at[p, src], self.xf_in.at[p, src], self.at.over_x)

    def x_half(self, src):
        span = self.block(src, 1 - self.at.y, self.x, self.low, self.middle)
        p = self.part
        return remote(span, span, self.xh_out.at[p, src], self.xh_in.at[p, src], self.at.over_x)

    def y_half(self, src):
        span = self.block(src, self.at.y, 1 - self.x, self.middle, self.high)
        p = self.part
        return remote(span, span, self.yh_out.at[p, src], self.yh_in.at[p, src], self.at.over_y)

    def sib(self, src):
        span = self.w_all.at[
            pl.ds(src * 4, 4), self.at.core, pl.ds(self.low, self.high - self.low)
        ]
        p = self.part
        return remote(span, span, self.s_out.at[p, src], self.s_in.at[p, src], self.at.sibling)

    def begin(self):
        at = self.at
        self.own(at.toward, 0).start()

        @pl.when(at.inner)
        def _():
            self.own(-at.toward, 1).start()

        self.y_full(at.z).start()
        self.x_full(at.z).start()

    def take(self, j):
        at = self.at
        src = at.source(j)
        self.passed(src, at.at_z(src)).wait_recv()

        @pl.when(at.inner)
        def _():
            self.passed(src, at.at_z(at.z + (at.toward if j == 1 else -at.toward))).start()

        self.y_full(src).start()
        self.x_full(src).start()

    def cross(self, j):
        src = self.at.source(j)
        self.y_full(src).wait_recv()
        self.x_half(src).start()
        self.x_full(src).wait_recv()
        self.y_half(src).start()

    def close(self, j):
        src = self.at.source(j)
        self.x_half(src).wait_recv()
        self.y_half(src).wait_recv()
        self.sib(src).start()

    def first_half(self):
        at = self.at
        self.take(1)

        @pl.when(at.inner)
        def _():
            self.take(2)

        self.cross(0)

        @pl.when(at.inner)
        def _():
            self.take(3)

        @pl.when(at.outer)
        def _():
            self.take(2)

        self.cross(1)
        self.close(0)

    def second_half(self):
        @pl.when(self.at.outer)
        def _():
            self.take(3)

        self.cross(2)
        self.close(1)
        self.cross(3)
        self.close(2)
        self.close(3)

    def settle(self):
        for j in range(4):
            self.sib(self.at.source(j)).wait_recv()

    def drain(self):
        at = self.at
        self.own(at.toward, 0).wait_send()

        @pl.when(at.inner)
        def _():
            self.own(-at.toward, 1).wait_send()
            for j in (1, 2, 3):
                self.passed(at.source(j), at.at_z(at.source(j))).wait_send()

        for j in range(4):
            src = at.source(j)
            for copy in (self.y_full, self.x_full, self.x_half, self.y_half, self.sib):
                copy(src).wait_send()


def gather_weight_sems():
    return [DMA((2, 2))] + [DMA((2, 4))] * 12


def gain_sems():
    return [DMA((3,)), DMA((3,)), DMA((4,)), DMA((4,))]


def turn(values, cos, sin):
    a, b = values[:, :128], values[:, 128:]
    return jnp.concatenate([a * cos - b * sin, b * cos + a * sin], axis=1)


def turn_back(values, cos, sin):
    a, b = values[:, :128], values[:, 128:]
    return jnp.concatenate([a * cos + b * sin, b * cos - a * sin], axis=1)


class WeightReturn:
    def __init__(self, at, held, bufs, sems, part, low, middle, high):
        self.at, self.held, self.part = at, held, part
        self.sib_in, self.xh_in, self.yh_in, self.xf_in, self.yf_in, self.z_in = bufs
        (
            self.so,
            self.si,
            self.xho,
            self.xhi,
            self.yho,
            self.yhi,
            self.xfo,
            self.xfi,
            self.yfo,
            self.yfi,
            self.zo,
            self.zi,
        ) = sems
        self.low, self.middle, self.high = low, middle, high
        self.x = at.s // 2
        self.rows = pl.ds(low, high - low)
        self.top = pl.ds(low, middle - low)
        self.bottom = pl.ds(middle, high - middle)

    def mine(self, z, y, x, rows):
        return self.held.at[self.at.core, z * 2 + y, x, rows]

    def sib(self, z):
        pair = pl.ds(z * 2, 2)
        p = self.part
        return remote(
            self.held.at[1 - self.at.core, pair, :, self.rows],
            self.sib_in.at[pair, :, self.rows],
            self.so.at[p, z],
            self.si.at[p, z],
            self.at.sibling,
        )

    def x_half(self, z):
        p = self.part
        source = self.mine(z, 1 - self.at.y, 1 - self.x, self.top)
        return remote(
            source, self.xh_in.at[z, self.top], self.xho.at[p, z], self.xhi.at[p, z], self.at.over_x
        )

    def y_half(self, z):
        p = self.part
        source = self.mine(z, 1 - self.at.y, 1 - self.x, self.bottom)
        return remote(
            source,
            self.yh_in.at[z, self.bottom],
            self.yho.at[p, z],
            self.yhi.at[p, z],
            self.at.over_y,
        )

    def x_full(self, z):
        p = self.part
        source = self.mine(z, self.at.y, 1 - self.x, self.rows)
        return remote(
            source,
            self.xf_in.at[z, self.rows],
            self.xfo.at[p, z],
            self.xfi.at[p, z],
            self.at.over_x,
        )

    def y_full(self, z):
        p = self.part
        source = self.mine(z, 1 - self.at.y, self.x, self.rows)
        return remote(
            source,
            self.yf_in.at[z, self.rows],
            self.yfo.at[p, z],
            self.yfi.at[p, z],
            self.at.over_y,
        )

    def z_part(self, z):
        p = self.part
        source = self.mine(z, self.at.y, self.x, self.rows)
        return remote(
            source,
            self.z_in.at[self.at.z, self.rows],
            self.zo.at[p, z],
            self.zi.at[p, self.at.z],
            self.at.at_z(z),
        )

    def z_arrival(self, z):
        p = self.part
        source = self.mine(z, self.at.y, self.x, self.rows)
        return remote(
            source,
            self.z_in.at[z, self.rows],
            self.zo.at[p, z],
            self.zi.at[p, z],
            self.at.at_z(z),
        )

    def add(self, z, y, x, rows, more):
        core, f = self.at.core, z * 2 + y
        self.held[core, f, x, rows] = (
            self.held[core, f, x, rows].astype(jnp.float32) + more.astype(jnp.float32)
        ).astype(jnp.bfloat16)

    def send_sib(self):
        for j in (3, 2, 1, 0):
            self.sib(self.at.source(j)).start()

    def merge(self):
        for j in (3, 2, 1, 0):
            z = self.at.source(j)
            self.sib(z).wait_recv()
            for y in (0, 1):
                for x in (0, 1):
                    self.add(z, y, x, self.rows, self.sib_in[z * 2 + y, x, self.rows])
            self.x_half(z).start()
            self.y_half(z).start()

    def pair_up(self):
        at = self.at
        for j in (3, 2, 1, 0):
            z = at.source(j)
            self.x_half(z).wait_recv()
            self.add(z, 1 - at.y, self.x, self.top, self.xh_in[z, self.top])
            self.y_full(z).start()
            self.y_half(z).wait_recv()
            self.add(z, at.y, 1 - self.x, self.bottom, self.yh_in[z, self.bottom])
            self.x_full(z).start()

    def collect(self):
        at = self.at
        for j in (3, 2, 1, 0):
            z = at.source(j)
            self.y_full(z).wait_recv()
            self.x_full(z).wait_recv()
            more = self.yf_in[z, self.rows].astype(jnp.float32) + self.xf_in[
                z, self.rows
            ].astype(jnp.float32)
            self.add(z, at.y, self.x, self.rows, more)
            if j > 0:
                self.z_part(z).start()

    def total(self):
        at = self.at
        value = self.held[at.core, at.f, self.x, self.rows].astype(jnp.float32)
        for j in (3, 2, 1):
            z = at.source(j)
            self.z_arrival(z).wait_recv()
            value = value + self.z_in[z, self.rows].astype(jnp.float32)
        return value

    def drain(self):
        for j in range(4):
            z = self.at.source(j)
            for copy in (self.sib, self.x_half, self.y_half, self.x_full, self.y_full):
                copy(z).wait_send()
            if j > 0:
                self.z_part(z).wait_send()


class GainSum:
    def __init__(self, at, row, outgoing, incoming, sems):
        self.at, self.row, self.outgoing, self.incoming = at, row, outgoing, incoming
        self.out, self.inc = sems
        self.partners = (at.sibling, at.over_x, at.over_y)

    def stage(self, k):
        return remote(
            self.outgoing.at[k],
            self.incoming.at[k],
            self.out.at[k],
            self.inc.at[k],
            self.partners[k],
        )

    def last(self, src, j, device):
        return remote(
            self.outgoing.at[3],
            self.incoming.at[3 + src],
            self.out.at[2 + j],
            self.inc.at[3 + src],
            device,
        )

    def send(self, k):
        self.outgoing[k] = self.row[...]
        if k < 3:
            self.stage(k).start()
        else:
            for j in (1, 2, 3):
                self.last(self.at.z, j, self.at.at_z(self.at.source(j))).start()

    def take(self, k):
        if k < 3:
            self.stage(k).wait_recv()
            self.row[...] += self.incoming[k]
        else:
            for j in (1, 2, 3):
                src = self.at.source(j)
                self.last(src, j, self.at.at_z(src)).wait_recv()
                self.row[...] += self.incoming[3 + src]

    def drain(self):
        for k in range(3):
            self.stage(k).wait_send()
        for j in (1, 2, 3):
            self.last(self.at.z, j, self.at.at_z(self.at.source(j))).wait_send()


class Refs:
    def __init__(self, names, refs):
        for name, ref in zip(names, refs):
            setattr(self, name, ref)


def columns_of(head):
    return slice(256 * head, 256 * head + 256)


def front_phase(at, r, sems):
    core, s = at.core, at.s
    gathered = GainGather(at, r.gain_all, sems[:4])
    w_sems = sems[4:17]
    kv_out, kv_in, x_out, x_in = sems[17:21]
    w_all, kv_all = r.w_all, r.kv_all
    early = WeightGather(at, w_all, w_sems, 0, 0, 16, 48)
    late = WeightGather(at, w_all, w_sems, 1, 48, 64, 80)
    chip = at.f * 2 + s // 2
    w_all[chip, core, 0:32] = r.own_q[...]
    w_all[chip, core, 32:48] = jnp.concatenate(
        [r.own_k[...].astype(jnp.float32), r.own_v[...].astype(jnp.float32)], axis=0
    ).astype(jnp.bfloat16)
    w_all[chip, core, 48:80] = r.own_o[...]
    r.gain_all[at.f * 4 + s] = r.gain_row[...]
    greet(
        [at.sibling, at.over_x, at.over_y]
        + [at.at_z(lax.rem(at.z + step, 4)) for step in (1, 2, 3)]
    )
    early.begin()
    gathered.run()
    placed = r.gain_all[...].reshape(32, 256)
    pieces = []
    for m in range(8):
        for k in range(5):
            piece = None
            if k < 4:
                piece = placed[4 * m + k : 4 * m + k + 1, :128]
            if k > 0:
                other = placed[4 * m + k - 1 : 4 * m + k, 128:]
                piece = other if piece is None else piece + other
            pieces.append(piece)
    r.gains[...] = jnp.concatenate(pieces, axis=1)
    gain = gain_parts(r)
    residual = r.tokens[...].astype(jnp.float32)
    r.normed[...] = (residual * rms_scale(residual) * gain[0]).astype(jnp.bfloat16)
    early.first_half()
    early.second_half()
    late.begin()
    early.settle()
    normed = r.normed[...]
    cos, sin = r.cos[...], r.sin[...]
    mixed_rows = rows_of_all(w_all, 32, 16)
    r.wk[...] = nn(pick(0), mixed_rows).astype(jnp.bfloat16)
    r.wv[...] = nn(pick(8), mixed_rows).astype(jnp.bfloat16)
    k_raw = nt(normed, r.wk[...])
    r.k_raw[...] = k_raw
    key = turn(k_raw * rms_scale(k_raw) * gain[2], cos, sin)
    kv_all[s, :, :256] = key.astype(jnp.bfloat16)
    kv_all[s, :, 256:] = nt(normed, r.wv[...]).astype(jnp.bfloat16)

    def kv_copy(which, slot, device):
        return remote(kv_all.at[slot], kv_all.at[slot], kv_out.at[which], kv_in.at[which], device)

    peer_slot = lax.rem(s + 2, 4)
    kv_copy(0, s, at.over_x).start()
    kv_copy(1, s, at.sibling).start()
    late.first_half()
    kv_copy(0, peer_slot, at.over_x).wait_recv()
    kv_copy(2, peer_slot, at.sibling).start()
    for head in range(4):
        q_raw = nt(normed, rows_of_head(w_all, head, 0, 32))
        r.q_raw[:, columns_of(head)] = q_raw
        query = turn(q_raw * rms_scale(q_raw) * gain[1], cos, sin)
        r.query[:, columns_of(head)] = query.astype(jnp.bfloat16)
    late.second_half()

    def x_weight(k):
        ref = (r.own_gate, r.own_up, r.own_down)[k]
        return remote(ref, r.peer_w.at[k], x_out.at[k], x_in.at[k], at.over_x)

    for k in range(3):
        x_weight(k).start()
    other = s + 1 - 2 * core
    kv_copy(1, other, at.sibling).wait_recv()
    kv_copy(2, lax.rem(other + 2, 4), at.sibling).wait_recv()
    keys, values = kv_parts(r)
    key_place = lax.broadcasted_iota(jnp.int32, (128, 512), 1)
    query_place = lax.broadcasted_iota(jnp.int32, (128, 512), 0) + s * 128
    allowed = (key_place >= r.doc[...]) & (key_place <= query_place)
    for head in range(4):
        raw = nt(r.query[:, columns_of(head)], keys) * score_step
        scores = jnp.where(allowed, raw, hidden_score)
        weights = jnp.exp(scores - jnp.max(scores, axis=1, keepdims=True))
        prob = weights / jnp.sum(weights, axis=1, keepdims=True)
        r.prob[head] = prob
        mixed = nn(prob.astype(jnp.bfloat16), values).astype(jnp.bfloat16)
        r.mixed[:, columns_of(head)] = mixed
    late.settle()
    attn = nn(r.mixed[...], rows_of_all(w_all, 48, 32))
    r.attn[...] = attn
    middle = r.tokens[...].astype(jnp.float32) + attn * rms_scale(attn) * gain[3]
    r.middle[...] = middle
    normed_ffn = (middle * rms_scale(middle) * gain[4]).astype(jnp.bfloat16)

    def drain():
        gathered.drain()
        early.drain()
        late.drain()
        kv_copy(0, s, at.over_x).wait_send()
        kv_copy(1, s, at.sibling).wait_send()
        kv_copy(2, peer_slot, at.sibling).wait_send()

    return normed_ffn, x_weight, drain


def gain_parts(r):
    return [r.gains[:, a:b] for a, b in zip(gain_edges[:-1], gain_edges[1:])]


def kv_parts(r):
    return r.kv_all[...].reshape(512, 512)[:, :256], r.kv_all[...].reshape(512, 512)[:, 256:]


def ffn_phase(at, r, sems, normed_ffn, x_weight):
    core = at.core
    fwd_gather, fwd_sum = sems[:7], sems[7:13]
    bwd_gather, bwd_sum = sems[13:20], sems[20:26]
    x_out, x_in = sems[26:28]
    sum_bufs = (r.to_sib, r.from_sib, r.chip_sum, r.from_y, r.to_z, r.from_z)
    normed_all, grad_all = r.held.at[0], r.held.at[1]
    gates = (r.own_gate, r.peer_w.at[0])
    ups = (r.own_up, r.peer_w.at[1])
    downs = (r.own_down, r.peer_w.at[2])
    r.held[0, at.f, core] = normed_ffn

    def rows_of(which, chip):
        return jnp.concatenate([r.held[which, chip, core], r.held[which, chip, 1 - core]], axis=0)

    def weights_here():
        for k in range(3):
            x_weight(k).wait()

    def forward(chip):
        rows = rows_of(0, chip)
        total = None
        for half in (0, 1):
            gate = nt(rows, gates[half][...])
            up = nt(rows, ups[half][...])
            r.gate_keep[half, chip] = gate.astype(jnp.bfloat16)
            r.up_keep[half, chip] = up.astype(jnp.bfloat16)
            bend = jnp.tanh(gelu_c * (gate + 0.044715 * gate * gate * gate))
            hidden = (0.5 * gate * (1.0 + bend) * up).astype(jnp.bfloat16)
            part = nn(hidden, downs[half][...])
            total = part if total is None else total + part
        return total[:128], total[128:]

    finish, drain = exchange_pass(
        at, normed_all, fwd_gather, fwd_sum, sum_bufs, r.part_own, forward, 4, weights_here
    )
    ffn_raw = finish()
    drain()
    gain = gain_parts(r)[5]
    scale = rms_scale(ffn_raw)
    r.result[...] = (r.middle[...] + ffn_raw * scale * gain).astype(jnp.bfloat16)
    ffn_grad, gain_grad = norm_back(ffn_raw, gain, r.cotangent[...].astype(jnp.float32))
    r.gain_sum[:, gain_edges[5] : gain_edges[6]] = gain_grad
    r.held[1, at.f, core] = ffn_grad.astype(jnp.bfloat16)
    own_grads = (r.gate_grad, r.up_grad, r.down_grad)
    grads = (own_grads, tuple(r.peer_sum.at[k] for k in range(3)))
    for half in (0, 1):
        for target in grads[half]:
            target[...] = jnp.zeros(target.shape, jnp.float32)

    def backward(chip):
        rows = rows_of(1, chip)
        ahead = rows_of(0, chip)
        total = None
        for half in (0, 1):
            dhidden = nt(rows, downs[half][...])
            gate = r.gate_keep[half, chip].astype(jnp.float32)
            up = r.up_keep[half, chip].astype(jnp.float32)
            square = gate * gate
            bend = jnp.tanh(gelu_c * (gate + 0.044715 * square * gate))
            unit = 0.5 * gate * (1.0 + bend)
            slope = 0.5 * (1.0 + bend) + 0.5 * gate * (1.0 - bend * bend) * (
                gelu_c * (1.0 + 3 * 0.044715 * square)
            )
            hidden = (unit * up).astype(jnp.bfloat16)
            dgate = (dhidden * up * slope).astype(jnp.bfloat16)
            dup = (dhidden * unit).astype(jnp.bfloat16)
            part = nn(dgate, gates[half][...]) + nn(dup, ups[half][...])
            total = part if total is None else total + part
            gate_sum, up_sum, down_sum = grads[half]
            gate_sum[...] += tn(dgate, ahead)
            up_sum[...] += tn(dup, ahead)
            down_sum[...] += tn(hidden, rows)
        return total[:128], total[128:]

    def x_copy(k):
        return remote(r.peer_w.at[k], r.from_x.at[k], x_out.at[k], x_in.at[k], at.over_x)

    def send_x():
        for k in range(3):
            r.peer_w[k] = r.peer_sum[k].astype(jnp.bfloat16)
            x_copy(k).start()

    finish, drain = exchange_pass(
        at, grad_all, bwd_gather, bwd_sum, sum_bufs, r.part_own, backward, 0, None, send_x
    )
    normed_grad = finish()
    drain()

    def complete():
        for k in range(3):
            x_copy(k).wait()
            own_grads[k][...] += r.from_x[k].astype(jnp.float32)

    return normed_grad, complete


def back_phase(at, r, sems, normed_grad, complete):
    core, s = at.core, at.s
    x = s // 2
    gain = gain_parts(r)
    cos, sin = r.cos[...], r.sin[...]
    bufs = (r.sib_in, r.half_in, r.half_in, r.xf_in, r.yf_in, r.zw_in)
    w_sems = sems[:12]
    kv_out, kv_in = sems[12:14]
    outer = WeightReturn(at, r.held, bufs, w_sems, 1, 48, 64, 80)
    inner = WeightReturn(at, r.held, bufs, w_sems, 0, 0, 16, 48)
    gain_total = GainSum(at, r.gain_sum, r.gain_out, r.gain_in, sems[14:16])

    def put_gain(k, value):
        r.gain_sum[:, gain_edges[k] : gain_edges[k + 1]] = value

    def put_rows(head, low, count, rows):
        split = rows.astype(jnp.bfloat16).reshape(4, 2, count, rows.shape[-1])
        for c in range(4):
            for k in (0, 1):
                r.held[k, 2 * head + c // 2, c % 2, low : low + count] = split[c, k]

    part, gain_grad = norm_back(r.middle[...], gain[4], normed_grad)
    put_gain(4, gain_grad)
    middle_grad = r.cotangent[...].astype(jnp.float32) + part
    r.middle[...] = middle_grad
    attn_grad, gain_grad = norm_back(r.attn[...], gain[3], middle_grad)
    put_gain(3, gain_grad)
    attn_grad = attn_grad.astype(jnp.bfloat16)
    for head in range(4):
        put_rows(head, 48, 32, tn(r.mixed[:, columns_of(head)], attn_grad))
    outer.send_sib()
    keys, values = kv_parts(r)
    for head in range(4):
        mixed_grad = nt(attn_grad, rows_of_head(r.w_all, head, 48, 32)).astype(jnp.bfloat16)
        prob = r.prob[head]
        prob_grad = nt(mixed_grad, values)
        delta = jnp.sum(prob * prob_grad, axis=1, keepdims=True)
        score_grad = (prob * (prob_grad - delta)).astype(jnp.bfloat16)
        key_part = tn(score_grad, r.query[:, columns_of(head)]) * score_step
        value_part = tn(prob.astype(jnp.bfloat16), mixed_grad)
        if head == 0:
            r.kv_sum[:, :256] = key_part
            r.kv_sum[:, 256:] = value_part
        else:
            r.kv_sum[:, :256] += key_part
            r.kv_sum[:, 256:] += value_part
        r.query_grad[:, columns_of(head)] = nn(score_grad, keys) * score_step
    r.kv_part[...] = r.kv_sum[...].astype(jnp.bfloat16).reshape(2, 2, 128, 512)
    kv_sib = remote(
        r.kv_part.at[:, 1 - core], r.kv_sib.at[...], kv_out.at[0], kv_in.at[0], at.sibling
    )
    kv_sib.start()
    outer.merge()
    kv_sib.wait_recv()
    r.kv_chip[...] = (
        r.kv_part[1 - x, core].astype(jnp.float32) + r.kv_sib[1 - x].astype(jnp.float32)
    ).astype(jnp.bfloat16)
    kv_x = remote(r.kv_chip, r.kv_far, kv_out.at[1], kv_in.at[1], at.over_x)
    kv_x.start()
    normed = r.normed[...]
    query_gain = None
    for head in range(4):
        turned = turn_back(r.query_grad[:, columns_of(head)], cos, sin)
        q_raw_grad, gain_grad = norm_back(r.q_raw[:, columns_of(head)], gain[1], turned)
        query_gain = gain_grad if query_gain is None else query_gain + gain_grad
        q_raw_grad = q_raw_grad.astype(jnp.bfloat16)
        r.query[:, columns_of(head)] = q_raw_grad
        put_rows(head, 0, 32, tn(q_raw_grad, normed))
    put_gain(1, query_gain)
    outer.pair_up()
    kv_x.wait_recv()
    kv_grad = (
        r.kv_part[x, core].astype(jnp.float32)
        + r.kv_sib[x].astype(jnp.float32)
        + r.kv_far[...].astype(jnp.float32)
    )
    k_raw_grad, gain_grad = norm_back(r.k_raw[...], gain[2], turn_back(kv_grad[:, :256], cos, sin))
    put_gain(2, gain_grad)
    k_raw_grad = k_raw_grad.astype(jnp.bfloat16)
    v_raw_grad = kv_grad[:, 256:].astype(jnp.bfloat16)
    woven = (nn(k_raw_grad, pick(0)) + nn(v_raw_grad, pick(8))).astype(jnp.bfloat16)
    for head in range(4):
        put_rows(head, 32, 16, tn(woven[:, 128 * head : 128 * head + 128], normed))
    inner.send_sib()
    normed_grad = nn(k_raw_grad, r.wk[...]) + nn(v_raw_grad, r.wv[...])
    for head in range(4):
        normed_grad += nn(r.query[:, columns_of(head)], rows_of_head(r.w_all, head, 0, 32))
    part, gain_grad = norm_back(r.tokens[...].astype(jnp.float32), gain[0], normed_grad)
    put_gain(0, gain_grad)
    gain_total.send(0)
    r.token_grad[...] = r.middle[...] + part
    inner.merge()
    gain_total.take(0)
    gain_total.send(1)
    outer.collect()
    inner.pair_up()
    gain_total.take(1)
    gain_total.send(2)
    inner.collect()
    gain_total.take(2)
    gain_total.send(3)
    r.o_grad[...] = outer.total()
    complete()
    total = inner.total()
    r.q_grad[...] = total[:32]
    r.k_grad[...] = total[32:40]
    r.v_grad[...] = total[40:48]
    gain_total.take(3)
    outer.drain()
    inner.drain()
    gain_total.drain()
    kv_sib.wait_send()
    kv_x.wait_send()


def layer_call(values):
    b16, f32 = jnp.bfloat16, jnp.float32
    rows, width = values["tokens"].shape
    units = values["own_gate"].shape[0]
    outs = {
        "result": ((rows, width), b16),
        "token_grad": ((rows, width), f32),
        "gain_sum": ((1, 5120), f32),
        "q_grad": ((32, width), f32),
        "k_grad": ((8, width), f32),
        "v_grad": ((8, width), f32),
        "o_grad": ((32, width), f32),
        "gate_grad": ((units, width), f32),
        "up_grad": ((units, width), f32),
        "down_grad": ((units, width), f32),
    }
    scratch = {
        "w_all": ((16, 2, 80, width), b16),
        "gain_all": ((32, 1, 256), f32),
        "gains": ((1, 5120), f32),
        "wk": ((256, width), b16),
        "wv": ((256, width), b16),
        "normed": ((rows, width), b16),
        "k_raw": ((rows, 256), f32),
        "q_raw": ((rows, 1024), f32),
        "query": ((rows, 1024), b16),
        "query_grad": ((rows, 1024), f32),
        "kv_all": ((4, rows, 512), b16),
        "prob": ((4, rows, 512), f32),
        "mixed": ((rows, 1024), b16),
        "attn": ((rows, width), f32),
        "middle": ((rows, width), f32),
        "peer_w": ((3, units, width), b16),
        "held": ((2, 8, 2, rows, width), b16),
        "gate_keep": ((2, 8, 2 * rows, units), b16),
        "up_keep": ((2, 8, 2 * rows, units), b16),
        "peer_sum": ((3, units, width), f32),
        "part_own": ((rows, width), f32),
        "to_sib": ((8, rows, width), b16),
        "from_sib": ((8, rows, width), b16),
        "chip_sum": ((8, rows, width), b16),
        "from_y": ((4, rows, width), b16),
        "to_z": ((4, rows, width), b16),
        "from_z": ((2, 4, rows, width), b16),
        "from_x": ((3, units, width), b16),
        "sib_in": ((8, 2, 80, width), b16),
        "half_in": ((4, 80, width), b16),
        "xf_in": ((4, 80, width), b16),
        "yf_in": ((4, 80, width), b16),
        "zw_in": ((4, 80, width), b16),
        "kv_sum": ((4 * rows, 512), f32),
        "kv_part": ((2, 2, rows, 512), b16),
        "kv_sib": ((2, rows, 512), b16),
        "kv_chip": ((rows, 512), b16),
        "kv_far": ((rows, 512), b16),
        "gain_out": ((4, 1, 5120), f32),
        "gain_in": ((7, 1, 5120), f32),
    }
    gather_sems = [DMA((2,)), DMA((4,)), DMA((4,)), DMA((4,)), DMA((4,)), DMA((8,)), DMA((8,))]
    sum_sems = [DMA((8,)), DMA((8,)), DMA((4,)), DMA((4,)), DMA((4,)), DMA((2, 4))]
    front_sems = gain_sems() + gather_weight_sems() + [DMA((3,))] * 4
    ffn_sems = (gather_sems + sum_sems) * 2 + [DMA((3,)), DMA((3,))]
    back_sems = [DMA((2, 4))] * 12 + [DMA((2,)), DMA((2,)), DMA((6,)), DMA((7,))]
    sems = front_sems + ffn_sems + back_sems
    names = tuple(values) + tuple(outs) + tuple(scratch)

    def kernel(*refs):
        at = Place()
        r = Refs(names, refs)
        held_sems = refs[len(names) :]
        first, second = len(front_sems), len(front_sems) + len(ffn_sems)
        normed_ffn, x_weight, drain = front_phase(at, r, held_sems[:first])
        normed_grad, complete = ffn_phase(at, r, held_sems[first:second], normed_ffn, x_weight)
        back_phase(at, r, held_sems[second:], normed_grad, complete)
        drain()

    vmem = pl.BlockSpec(memory_space=pltpu.VMEM)
    out = pl.pallas_call(
        kernel,
        out_shape=tuple(jax.ShapeDtypeStruct(*spec) for spec in outs.values()),
        in_specs=[vmem] * len(values),
        out_specs=tuple([vmem] * len(outs)),
        scratch_shapes=[pltpu.VMEM(*spec) for spec in scratch.values()] + sems,
        compiler_params=pltpu.CompilerParams(
            collective_id=1, has_side_effects=True, vmem_limit_bytes=63 << 20
        ),
        name="layer",
    )(*values.values())
    return dict(zip(outs, out))


def one_kernel(
    tokens, doc_start, gains, w_query, w_key, w_value, w_out, w_gate, w_up, w_down, cotangent
):
    rows = tokens.shape[0]
    device = lax.axis_index("fsdp") * lax.axis_size("seq") + lax.axis_index("seq")
    share = gains.shape[0]
    gain_row = lax.dynamic_update_slice(
        jnp.zeros((1, 256), jnp.float32),
        gains[None].astype(jnp.float32),
        (0, lax.rem(device, 4) * 32),
    )
    places = lax.axis_index("seq") * rows + jnp.arange(rows, dtype=jnp.int32) - doc_start
    cos, sin = rope_tables(places, 256)
    out = layer_call(
        {
            "tokens": tokens,
            "doc": doc_start[:, None],
            "gain_row": gain_row,
            "own_q": w_query.T,
            "own_k": w_key.T,
            "own_v": w_value.T,
            "own_o": w_out,
            "own_gate": w_gate.T,
            "own_up": w_up.T,
            "own_down": w_down,
            "cos": cos[:, 0],
            "sin": sin[:, 0],
            "cotangent": cotangent,
        }
    )
    return (
        out["result"],
        out["token_grad"],
        lax.dynamic_slice(out["gain_sum"][0], (device * share,), (share,)),
        out["q_grad"].T,
        out["k_grad"].T,
        out["v_grad"].T,
        out["o_grad"],
        out["gate_grad"].T,
        out["up_grad"].T,
        out["down_grad"],
    )


def solution(mesh):
    in_specs = (
        P(("fsdp", "seq"), None),
        P(("fsdp", "seq")),
        P(("fsdp", "seq")),
        P(None, ("fsdp", "seq")),
        P(None, ("fsdp", "seq")),
        P(None, ("fsdp", "seq")),
        P(("fsdp", "seq"), None),
        P(None, ("fsdp", "seq")),
        P(None, ("fsdp", "seq")),
        P(("fsdp", "seq"), None),
        P(("fsdp", "seq"), None),
    )
    out_specs = (
        P(("fsdp", "seq"), None),
        P(("fsdp", "seq"), None),
        P(("fsdp", "seq")),
        P(None, ("fsdp", "seq")),
        P(None, ("fsdp", "seq")),
        P(None, ("fsdp", "seq")),
        P(("fsdp", "seq"), None),
        P(None, ("fsdp", "seq")),
        P(None, ("fsdp", "seq")),
        P(("fsdp", "seq"), None),
    )
    body = one_kernel if dict(mesh.shape) == {"fsdp": 8, "seq": 4} else local
    return jax.shard_map(body, mesh=mesh, in_specs=in_specs, out_specs=out_specs, check_vma=False)
```

```python
from functools import partial

import jax
import jax.numpy as jnp
from jax import lax
from jax.experimental import pallas as pl
from jax.experimental.pallas import tpu as pltpu
from jax.sharding import PartitionSpec as P

norm_eps = 1e-06
rope_base = 1000000.0
score_scale = 0.0625
masked_value = -1e30


def product(former, latter):
    return jnp.dot(former, latter, preferred_element_type=jnp.float32)


def inner_rows(former, latter):
    return lax.dot_general(
        former, latter, (((0,), (0,)), ((), ())), preferred_element_type=jnp.float32
    )


def outer_rows(former, latter):
    return lax.dot_general(
        former, latter, (((1,), (1,)), ((), ())), preferred_element_type=jnp.float32
    )


def scaled_norm(values, factor):
    return values * lax.rsqrt(jnp.mean(values * values, axis=-1, keepdims=True) + norm_eps) * factor


def rotate(values, cos_table, sin_table):
    half_width = values.shape[-1] // 2
    leading = values[..., :half_width]
    trailing = values[..., half_width:]
    return jnp.concatenate(
        [leading * cos_table - trailing * sin_table, trailing * cos_table + leading * sin_table],
        axis=-1,
    )


def head_norm(values, factor, cos_table, sin_table):
    return rotate(scaled_norm(values, factor), cos_table, sin_table)


def gated_unit(gate_in, up_in):
    return jax.nn.gelu(gate_in, approximate=True) * up_in


def rope_tables(places, rot_width):
    half_width = rot_width // 2
    frequency = rope_base ** (-2.0 * jnp.arange(half_width, dtype=jnp.float32) / rot_width)
    angles = places.astype(jnp.float32)[:, None] * frequency[None, :]
    return (jnp.cos(angles)[:, None, :], jnp.sin(angles)[:, None, :])


def masked_scores(queries, key_rows, bounds, offset):
    raw_scores = outer_rows(queries, key_rows) * score_scale
    query_place = offset + jnp.arange(queries.shape[0], dtype=jnp.int32)
    key_place = jnp.arange(key_rows.shape[0], dtype=jnp.int32)
    allowed = (key_place[None, :] >= bounds[:, None]) & (key_place[None, :] <= query_place[:, None])
    return jnp.where(allowed, raw_scores, masked_value)


def local(
    tokens, doc_start, gains, w_query, w_key, w_value, w_out, w_gate, w_up, w_down, cotangent
):
    tok_rows = tokens.shape[0]
    model_width = tokens.shape[1]
    run_index = lax.axis_index("seq")
    gains_all, query_w, key_w, value_w, out_w = (
        lax.all_gather(gains, ("fsdp", "seq"), axis=0, tiled=True),
        lax.all_gather(w_query, ("fsdp", "seq"), axis=1, tiled=True),
        lax.all_gather(w_key, ("fsdp", "seq"), axis=1, tiled=True),
        lax.all_gather(w_value, ("fsdp", "seq"), axis=1, tiled=True),
        lax.all_gather(w_out, ("fsdp", "seq"), axis=0, tiled=True),
    )
    gate_w, up_w, down_w = (
        lax.all_gather(w_gate, ("fsdp", "seq"), axis=1, tiled=True),
        lax.all_gather(w_up, ("fsdp", "seq"), axis=1, tiled=True),
        lax.all_gather(w_down, ("fsdp", "seq"), axis=0, tiled=True),
    )
    head_width = key_w.shape[1]
    head_count = query_w.shape[1] // head_width
    gain_values = gains_all.astype(jnp.float32)
    gain_pre = gain_values[:model_width]
    gain_query = gain_values[model_width : model_width + head_width]
    gain_key = gain_values[model_width + head_width : model_width + 2 * head_width]
    gain_post = gain_values[model_width + 2 * head_width : 2 * model_width + 2 * head_width]
    gain_pre_ffn = gain_values[2 * model_width + 2 * head_width : 3 * model_width + 2 * head_width]
    gain_post_ffn = gain_values[3 * model_width + 2 * head_width :]
    residual = tokens.astype(jnp.float32)
    normed, pre_pull = jax.vjp(scaled_norm, residual, gain_pre)
    normed_b = normed.astype(jnp.bfloat16)
    query_raw = product(normed_b, query_w).reshape(tok_rows, head_count, head_width)
    key_raw = product(normed_b, key_w).reshape(tok_rows, 1, head_width)
    value_b = product(normed_b, value_w).astype(jnp.bfloat16)
    places = run_index * tok_rows + jnp.arange(tok_rows, dtype=jnp.int32) - doc_start
    cos_table, sin_table = rope_tables(places, head_width)
    rope_norm = partial(head_norm, cos_table=cos_table, sin_table=sin_table)
    query_rot, query_pull = jax.vjp(rope_norm, query_raw, gain_query)
    key_rot, key_pull = jax.vjp(rope_norm, key_raw, gain_key)
    query_b = query_rot.reshape(tok_rows, head_count * head_width).astype(jnp.bfloat16)
    key_b = key_rot.reshape(tok_rows, head_width).astype(jnp.bfloat16)
    query_heads = lax.all_to_all(query_b, "seq", split_axis=1, concat_axis=0, tiled=True)
    key_rows, value_rows = (
        lax.all_gather(key_b, "seq", axis=0, tiled=True),
        lax.all_gather(value_b, "seq", axis=0, tiled=True),
    )
    starts = lax.all_gather(doc_start, "seq", axis=0, tiled=True)
    seq_tokens = key_rows.shape[0]
    block_rows = min(512, seq_tokens)
    block_count = seq_tokens // block_rows
    query_blocks = query_heads.reshape(block_count, block_rows, head_width)
    start_blocks = starts.reshape(block_count, block_rows)
    block_ids = jnp.arange(block_count, dtype=jnp.int32)

    def attend(block_item):
        queries, bounds, block_index = block_item
        scores = masked_scores(queries, key_rows, bounds, block_index * block_rows)
        row_max = jnp.max(scores, axis=1, keepdims=True)
        weights = jnp.exp(scores - row_max)
        row_total = jnp.sum(weights, axis=1, keepdims=True)
        probability = (weights / row_total).astype(jnp.bfloat16)
        mixed_block = product(probability, value_rows).astype(jnp.bfloat16)
        return (mixed_block, (row_max + jnp.log(row_total))[:, 0])

    mixed_blocks, lse_blocks = lax.map(attend, (query_blocks, start_blocks, block_ids))
    mixed_heads = mixed_blocks.reshape(seq_tokens, head_width)
    mixed_tokens = lax.all_to_all(mixed_heads, "seq", split_axis=0, concat_axis=1, tiled=True)
    attn_raw = product(mixed_tokens, out_w)
    attn_out, post_pull = jax.vjp(scaled_norm, attn_raw, gain_post)
    middle = residual + attn_out
    normed_ffn, pre_ffn_pull = jax.vjp(scaled_norm, middle, gain_pre_ffn)
    normed_ffn_b = normed_ffn.astype(jnp.bfloat16)
    gate_act = product(normed_ffn_b, gate_w)
    up_act = product(normed_ffn_b, up_w)
    hidden, glu_pull = jax.vjp(gated_unit, gate_act, up_act)
    hidden_b = hidden.astype(jnp.bfloat16)
    ffn_raw = product(hidden_b, down_w)
    ffn_out, post_ffn_pull = jax.vjp(scaled_norm, ffn_raw, gain_post_ffn)
    result = (middle + ffn_out).astype(jnp.bfloat16)
    gate_w, up_w, down_w = (
        lax.all_gather(w_gate, ("fsdp", "seq"), axis=1, tiled=True),
        lax.all_gather(w_up, ("fsdp", "seq"), axis=1, tiled=True),
        lax.all_gather(w_down, ("fsdp", "seq"), axis=0, tiled=True),
    )
    query_w, key_w, value_w, out_w = (
        lax.all_gather(w_query, ("fsdp", "seq"), axis=1, tiled=True),
        lax.all_gather(w_key, ("fsdp", "seq"), axis=1, tiled=True),
        lax.all_gather(w_value, ("fsdp", "seq"), axis=1, tiled=True),
        lax.all_gather(w_out, ("fsdp", "seq"), axis=0, tiled=True),
    )
    upstream = cotangent.astype(jnp.float32)
    ffn_grad, gain_post_ffn_grad = post_ffn_pull(upstream)
    ffn_grad_b = ffn_grad.astype(jnp.bfloat16)
    down_w_grad = inner_rows(hidden_b, ffn_grad_b)
    hidden_grad = outer_rows(ffn_grad_b, down_w)
    gate_grad, up_grad = glu_pull(hidden_grad)
    gate_grad_b = gate_grad.astype(jnp.bfloat16)
    up_grad_b = up_grad.astype(jnp.bfloat16)
    gate_w_grad_t = inner_rows(gate_grad_b, normed_ffn_b)
    up_w_grad_t = inner_rows(up_grad_b, normed_ffn_b)
    normed_ffn_grad = outer_rows(gate_grad_b, gate_w) + outer_rows(up_grad_b, up_w)
    middle_part, gain_pre_ffn_grad = pre_ffn_pull(normed_ffn_grad)
    middle_grad = upstream + middle_part
    attn_grad, gain_post_grad = post_pull(middle_grad)
    attn_grad_b = attn_grad.astype(jnp.bfloat16)
    out_w_grad = inner_rows(mixed_tokens, attn_grad_b)
    mixed_grad = outer_rows(attn_grad_b, out_w).astype(jnp.bfloat16)
    mixed_grad_heads = lax.all_to_all(mixed_grad, "seq", split_axis=1, concat_axis=0, tiled=True)
    grad_blocks = mixed_grad_heads.reshape(block_count, block_rows, head_width)

    def attend_back(carried, block_item):
        key_accum, value_accum = carried
        queries, bounds, block_index, lse_row, block_grad = block_item
        scores = masked_scores(queries, key_rows, bounds, block_index * block_rows)
        probability = jnp.exp(scores - lse_row[:, None])
        prob_grad = outer_rows(block_grad, value_rows)
        value_accum = value_accum + inner_rows(probability.astype(jnp.bfloat16), block_grad)
        row_delta = jnp.sum(probability * prob_grad, axis=1, keepdims=True)
        score_grad = (probability * (prob_grad - row_delta)).astype(jnp.bfloat16)
        query_grad = product(score_grad, key_rows) * score_scale
        key_accum = key_accum + inner_rows(score_grad, queries) * score_scale
        return ((key_accum, value_accum), query_grad)

    zero_rows = jnp.zeros((seq_tokens, head_width), jnp.float32)
    (key_part, value_part), query_grad_blocks = lax.scan(
        attend_back,
        (zero_rows, zero_rows),
        (query_blocks, start_blocks, block_ids, lse_blocks, grad_blocks),
    )
    key_sum, value_sum = (
        lax.psum_scatter(
            key_part.astype(jnp.bfloat16), "seq", scatter_dimension=0, tiled=True
        ).astype(jnp.float32),
        lax.psum_scatter(
            value_part.astype(jnp.bfloat16), "seq", scatter_dimension=0, tiled=True
        ).astype(jnp.float32),
    )
    query_grad_tokens = lax.all_to_all(
        query_grad_blocks.reshape(seq_tokens, head_width).astype(jnp.bfloat16),
        "seq",
        split_axis=0,
        concat_axis=1,
        tiled=True,
    ).astype(jnp.float32)
    query_raw_grad, gain_query_grad = query_pull(
        query_grad_tokens.reshape(tok_rows, head_count, head_width)
    )
    key_raw_grad, gain_key_grad = key_pull(key_sum.reshape(tok_rows, 1, head_width))
    query_raw_b = query_raw_grad.reshape(tok_rows, head_count * head_width).astype(jnp.bfloat16)
    key_raw_b = key_raw_grad.reshape(tok_rows, head_width).astype(jnp.bfloat16)
    value_raw_b = value_sum.astype(jnp.bfloat16)
    query_w_grad_t = inner_rows(query_raw_b, normed_b)
    key_w_grad_t = inner_rows(key_raw_b, normed_b)
    value_w_grad_t = inner_rows(value_raw_b, normed_b)
    normed_grad = (
        outer_rows(query_raw_b, query_w)
        + outer_rows(key_raw_b, key_w)
        + outer_rows(value_raw_b, value_w)
    )
    residual_part, gain_pre_grad = pre_pull(normed_grad)
    input_grad = middle_grad + residual_part
    gains_grad = jnp.concatenate(
        [
            gain_pre_grad,
            gain_query_grad,
            gain_key_grad,
            gain_post_grad,
            gain_pre_ffn_grad,
            gain_post_ffn_grad,
        ]
    )
    shares = (
        lax.psum_scatter(gains_grad, ("fsdp", "seq"), scatter_dimension=0, tiled=True),
        lax.psum_scatter(query_w_grad_t, ("fsdp", "seq"), scatter_dimension=0, tiled=True),
        lax.psum_scatter(key_w_grad_t, ("fsdp", "seq"), scatter_dimension=0, tiled=True),
        lax.psum_scatter(value_w_grad_t, ("fsdp", "seq"), scatter_dimension=0, tiled=True),
        lax.psum_scatter(out_w_grad, ("fsdp", "seq"), scatter_dimension=0, tiled=True),
        lax.psum_scatter(gate_w_grad_t, ("fsdp", "seq"), scatter_dimension=0, tiled=True),
        lax.psum_scatter(up_w_grad_t, ("fsdp", "seq"), scatter_dimension=0, tiled=True),
        lax.psum_scatter(down_w_grad, ("fsdp", "seq"), scatter_dimension=0, tiled=True),
    )
    return (
        result,
        input_grad,
        shares[0],
        shares[1].T,
        shares[2].T,
        shares[3].T,
        shares[4],
        shares[5].T,
        shares[6].T,
        shares[7],
    )


gelu_c = 0.7978845608028654
MESH = pl.DeviceIdType.MESH
DMA = pltpu.SemaphoreType.DMA


def nt(former, latter):
    return lax.dot_general(
        former, latter, (((1,), (1,)), ((), ())), preferred_element_type=jnp.float32
    )


def nn(former, latter):
    return lax.dot_general(
        former, latter, (((1,), (0,)), ((), ())), preferred_element_type=jnp.float32
    )


def tn(former, latter):
    return lax.dot_general(
        former, latter, (((0,), (0,)), ((), ())), preferred_element_type=jnp.float32
    )


class Place:
    def __init__(self):
        self.f = lax.axis_index("fsdp")
        self.s = lax.axis_index("seq")
        self.z = self.f // 2
        self.y = lax.rem(self.f, 2)
        self.core = lax.rem(self.s, 2)
        self.high = self.z // 2
        self.inner = self.z * (3 - self.z) == 2
        self.outer = self.z * (3 - self.z) == 0
        self.sibling = (self.f, self.s + 1 - 2 * self.core)
        self.over_x = (self.f, lax.rem(self.s + 2, 4))
        self.over_y = (self.f + 1 - 2 * self.y, self.s)
        self.toward = 1 - 2 * self.high
        self.step_first = self.toward * (1 - self.z * (3 - self.z))

    def at_z(self, z):
        return (z * 2 + self.y, self.s)

    def source(self, j):
        last = j // 3
        middle = j // 2 - last
        none = (3 - j) // 3
        first = 1 - last - middle - none
        return (
            none * self.z
            + first * (1 - self.z + 4 * self.high)
            + middle * (2 - self.high)
            + last * (3 - 3 * self.high)
        )


def remote(source, target, send_sem, recv_sem, device):
    return pltpu.make_async_remote_copy(
        src_ref=source,
        dst_ref=target,
        send_sem=send_sem,
        recv_sem=recv_sem,
        device_id=device,
        device_id_type=MESH,
    )


def greet(partners):
    entry = pltpu.get_barrier_semaphore()
    for partner in partners:
        pl.semaphore_signal(entry, inc=1, device_id=partner, device_id_type=MESH)
    pl.semaphore_wait(entry, len(partners))


def exchange_pass(at, held, gather_sems, sum_sems, sum_bufs, part_own, compute, lag=0, ready=None, then=None):
    z_own, z_next, z_in, y_out, y_in, c_out, c_in = gather_sems
    t_out, t_in, v_out, v_in, w_out, w_in = sum_sems
    to_sib, from_sib, chip_sum, from_y, to_z, from_z = sum_bufs
    f, core = at.f, at.core

    def block(chip):
        return held.at[chip, core]

    def over(chip, outgoing, incoming, device):
        return remote(block(chip), block(chip), outgoing, incoming, device)

    def own_z(step, slot):
        return over(f, z_own.at[slot], z_in.at[at.z], at.at_z(at.z + step))

    def own_z_toward():
        return own_z(at.toward, 0)

    def own_z_away():
        return own_z(-at.toward, 1)

    def pass_z(src, step):
        return over(src * 2 + at.y, z_next.at[src], z_in.at[src], at.at_z(at.z + step))

    def pass_y(src):
        return over(src * 2 + at.y, y_out.at[src], y_in.at[src], at.over_y)

    def pass_sib(chip):
        return over(chip, c_out.at[chip], c_in.at[chip], at.sibling)

    own_z_toward().start()

    @pl.when(at.inner)
    def _():
        own_z_away().start()

    pass_y(at.z).start()
    pass_sib(f).start()

    def from_z_block(src):
        return over(src * 2 + at.y, z_next.at[src], z_in.at[src], at.at_z(src))

    def take_z(j, step):
        src = at.source(j)
        from_z_block(src).wait_recv()

        @pl.when(at.inner)
        def _():
            pass_z(src, step).start()

        pass_y(src).start()
        pass_sib(src * 2 + at.y).start()

    def chip_of(i):
        return at.source(i // 2) * 2 + lax.rem(at.y + lax.rem(i, 2), 2)

    def sib_sum(i):
        return remote(to_sib.at[i], from_sib.at[i], t_out.at[i], t_in.at[i], at.sibling)

    def y_sum(i):
        return remote(chip_sum.at[i], from_y.at[i // 2], v_out.at[i // 2], v_in.at[i // 2], at.over_y)

    def finish_chip(i):
        sib_sum(i).wait_recv()
        chip_sum[i] = (part_own[...] + from_sib[i].astype(jnp.float32)).astype(jnp.bfloat16)

    def arrivals(i):
        @pl.when(i == 1)
        def _():
            take_z(1, at.toward)

            @pl.when(at.inner)
            def _():
                take_z(2, -at.toward)

        @pl.when((i == 3) & at.outer)
        def _():
            take_z(2, -at.toward)

        @pl.when(((i == 3) & at.inner) | ((i == 5) & at.outer))
        def _():
            take_z(3, -at.toward)

        @pl.when(lax.rem(i, 2) == 1)
        def _():
            pass_y(at.source(i // 2)).wait_recv()
            pass_sib(chip_of(i)).start()

    def one_chip(i):
        chip = chip_of(i)
        pass_sib(chip).wait_recv()
        own_part, sib_part = compute(chip)
        to_sib[i] = sib_part.astype(jnp.bfloat16)
        sib_sum(i).start()

        @pl.when(i > 0)
        def _():
            finish_chip(i - 1)

        part_own[...] = own_part

    def step(i, carried):
        @pl.when(i < 8)
        def _():
            arrivals(i)

        if ready is not None:

            @pl.when(i == lag)
            def _():
                ready()

        @pl.when(i >= lag)
        def _():
            one_chip(i - lag)

        return carried

    lax.fori_loop(0, 8 + lag, step, 0)
    finish_chip(7)
    for j in (3, 2, 1, 0):
        y_sum(2 * j + 1).start()
    if then is not None:
        then()

    def z_sum(target, direction):
        slot = (direction + 1) // 2
        return remote(
            to_z.at[target],
            from_z.at[slot, target],
            w_out.at[target],
            w_in.at[slot, target],
            at.at_z(at.z + direction),
        )

    def z_arrival(target, direction):
        slot = (direction + 1) // 2
        return remote(
            to_z.at[target],
            from_z.at[slot, target],
            w_out.at[target],
            w_in.at[slot, target],
            at.at_z(lax.rem(at.z - direction + 4, 4)),
        )

    def direction_of(j):
        return at.step_first if j == 1 else at.toward

    for j in (3, 2, 1):
        target, direction = at.source(j), direction_of(j)
        y_sum(2 * j + 1).wait_recv()
        mine = chip_sum[2 * j].astype(jnp.float32) + from_y[j].astype(jnp.float32)

        @pl.when(at.outer)
        def _():
            to_z[target] = mine.astype(jnp.bfloat16)

        @pl.when(at.inner)
        def _():
            z_arrival(target, direction).wait_recv()
            ahead = from_z[(direction + 1) // 2, target].astype(jnp.float32)
            to_z[target] = (mine + ahead).astype(jnp.bfloat16)

        z_sum(target, direction).start()

    def finish():
        y_sum(1).wait_recv()
        part_own[...] = chip_sum[0].astype(jnp.float32) + from_y[0].astype(jnp.float32)
        z_arrival(at.z, -at.toward).wait_recv()
        part_own[...] += from_z[(1 - at.toward) // 2, at.z].astype(jnp.float32)

        @pl.when(at.inner)
        def _():
            z_arrival(at.z, at.toward).wait_recv()
            part_own[...] += from_z[(1 + at.toward) // 2, at.z].astype(jnp.float32)

        return part_own[...]

    def drain():
        own_z_toward().wait_send()

        @pl.when(at.inner)
        def _():
            own_z_away().wait_send()
            for j in (1, 2, 3):
                from_z_block(at.source(j)).wait_send()

        def drain_chip(i, carried):
            pass_sib(chip_of(i)).wait_send()
            sib_sum(i).wait_send()

            @pl.when(lax.rem(i, 2) == 1)
            def _():
                pass_y(at.source(i // 2)).wait_send()
                y_sum(i).wait_send()

            return carried

        lax.fori_loop(0, 8, drain_chip, 0)
        for j in (1, 2, 3):
            z_sum(at.source(j), direction_of(j)).wait_send()

    return finish, drain


gain_edges = (0, 1152, 1408, 1664, 2816, 3968, 5120)
score_step = 0.0625
hidden_score = -1e30


def shape_spec(shape, dtype):
    return jax.ShapeDtypeStruct(shape, dtype)


def rms_scale(values):
    return lax.rsqrt(jnp.mean(values * values, axis=-1, keepdims=True) + norm_eps)


def norm_back(values, gain, upstream):
    scale = rms_scale(values)
    weighted = upstream * gain
    inner = jnp.mean(weighted * values, axis=-1, keepdims=True)
    back = scale * weighted - values * (scale * scale * scale * inner)
    return back, jnp.sum(upstream * values * scale, axis=0, keepdims=True)


def pick(offset):
    row = lax.broadcasted_iota(jnp.int32, (256, 512), 0)
    column = lax.broadcasted_iota(jnp.int32, (256, 512), 1)
    wanted = row // 8 * 16 + lax.rem(row, 8) + offset
    return jnp.where(column == wanted, 1.0, 0.0).astype(jnp.bfloat16)


def rows_of_all(w_all, low, count):
    return jnp.concatenate(
        [w_all[d // 2, d % 2, low : low + count] for d in range(32)], axis=0
    )


def rows_of_head(w_all, head, low, count):
    return jnp.concatenate(
        [w_all[d // 2, d % 2, low : low + count] for d in range(8 * head, 8 * head + 8)], axis=0
    )


class GainGather:
    def __init__(self, at, held, sems):
        self.at, self.held = at, held
        self.out, self.inc, self.z_out, self.z_in = sems
        x = at.s // 2
        self.spans = (
            (at.f * 4 + at.s, 1, at.sibling),
            (at.f * 4 + 2 * x, 2, at.over_x),
            (at.f * 4, 4, at.over_y),
        )

    def stage(self, k):
        first, count, partner = self.spans[k]
        span = self.held.at[pl.ds(first, count)]
        return remote(span, span, self.out.at[k], self.inc.at[k], partner)

    def last(self, src, j, device):
        span = self.held.at[pl.ds(src * 8, 8)]
        return remote(span, span, self.z_out.at[j], self.z_in.at[src], device)

    def send(self, k):
        at = self.at
        if k < 3:
            self.stage(k).start()
        else:
            for j in (1, 2, 3):
                self.last(at.z, j, at.at_z(at.source(j))).start()

    def take(self, k):
        at = self.at
        if k < 3:
            self.stage(k).wait_recv()
        else:
            for j in (1, 2, 3):
                self.last(at.source(j), j, at.at_z(at.source(j))).wait_recv()

    def drain(self):
        at = self.at
        for k in range(3):
            self.stage(k).wait_send()
        for j in (1, 2, 3):
            self.last(at.z, j, at.at_z(at.source(j))).wait_send()


class WeightGather:
    def __init__(self, at, w_all, sems, part, low, high):
        self.at, self.w_all, self.part = at, w_all, part
        (
            self.x_out,
            self.x_in,
            self.first_out,
            self.first_in,
            self.z_own,
            self.z_next,
            self.z_in,
            self.y_out,
            self.y_in,
            self.s_out,
            self.s_in,
        ) = sems
        self.rows = pl.ds(low, high - low)
        self.x = at.s // 2

    def one(self, y, x, outgoing, incoming, device):
        span = self.w_all.at[(self.at.z * 2 + y) * 2 + x, self.at.core, self.rows]
        return remote(span, span, outgoing, incoming, device)

    def pair(self, z, y, outgoing, incoming, device):
        span = self.w_all.at[pl.ds((z * 2 + y) * 2, 2), self.at.core, self.rows]
        return remote(span, span, outgoing, incoming, device)

    def x_copy(self, x):
        p, at = self.part, self.at
        return self.one(at.y, x, self.x_out.at[p], self.x_in.at[p], at.over_x)

    def y_first(self, y, x):
        p, at = self.part, self.at
        return self.one(y, x, self.first_out.at[p, x], self.first_in.at[p, x], at.over_y)

    def own(self, step, slot):
        p, at = self.part, self.at
        return self.pair(
            at.z, at.y, self.z_own.at[p, slot], self.z_in.at[p, at.z], at.at_z(at.z + step)
        )

    def passed(self, src, device):
        p = self.part
        return self.pair(src, self.at.y, self.z_next.at[p, src], self.z_in.at[p, src], device)

    def y_pair(self, src, y):
        p = self.part
        return self.pair(src, y, self.y_out.at[p, src], self.y_in.at[p, src], self.at.over_y)

    def sib(self, src):
        span = self.w_all.at[pl.ds(src * 4, 4), self.at.core, self.rows]
        p = self.part
        return remote(span, span, self.s_out.at[p, src], self.s_in.at[p, src], self.at.sibling)

    def begin(self):
        self.x_copy(self.x).start()

    def spread(self):
        at = self.at
        self.y_first(at.y, self.x).start()
        self.x_copy(1 - self.x).wait_recv()
        self.own(at.toward, 0).start()

        @pl.when(at.inner)
        def _():
            self.own(-at.toward, 1).start()

        self.y_first(at.y, 1 - self.x).start()

    def take(self, j):
        at = self.at
        src = at.source(j)
        self.passed(src, at.at_z(src)).wait_recv()

        @pl.when(at.inner)
        def _():
            self.passed(src, at.at_z(at.z + (at.toward if j == 1 else -at.toward))).start()

        self.y_pair(src, at.y).start()

    def close(self, j):
        src = self.at.source(j)
        if j == 0:
            for x in (0, 1):
                self.y_first(1 - self.at.y, x).wait_recv()
        else:
            self.y_pair(src, 1 - self.at.y).wait_recv()
        self.sib(src).start()

    def walk(self, between=()):
        at = self.at
        extra = list(between) + [lambda: None] * 3
        self.take(1)

        @pl.when(at.inner)
        def _():
            self.take(2)

        extra[0]()
        self.close(0)

        @pl.when(at.inner)
        def _():
            self.take(3)

        @pl.when(at.outer)
        def _():
            self.take(2)

        extra[1]()
        self.close(1)

        @pl.when(at.outer)
        def _():
            self.take(3)

        extra[2]()
        self.close(2)
        self.close(3)

    def settle(self):
        for j in range(4):
            self.sib(self.at.source(j)).wait_recv()

    def drain(self):
        at = self.at
        self.x_copy(self.x).wait_send()
        for x in (0, 1):
            self.y_first(at.y, x).wait_send()
        self.own(at.toward, 0).wait_send()

        @pl.when(at.inner)
        def _():
            self.own(-at.toward, 1).wait_send()
            for j in (1, 2, 3):
                self.passed(at.source(j), at.at_z(at.source(j))).wait_send()

        for j in range(4):
            src = at.source(j)
            if j > 0:
                self.y_pair(src, at.y).wait_send()
            self.sib(src).wait_send()


def gather_weight_sems():
    return [DMA((2,)), DMA((2,))] + [DMA((2, 2))] * 3 + [DMA((2, 4))] * 6


def gain_sems():
    return [DMA((3,)), DMA((3,)), DMA((4,)), DMA((4,))]


def turn(values, cos, sin):
    a, b = values[:, :128], values[:, 128:]
    return jnp.concatenate([a * cos - b * sin, b * cos + a * sin], axis=1)


def turn_back(values, cos, sin):
    a, b = values[:, :128], values[:, 128:]
    return jnp.concatenate([a * cos + b * sin, b * cos - a * sin], axis=1)


class WeightReturn:
    def __init__(self, at, held, bufs, sems, part, low, middle, high):
        self.at, self.held, self.part = at, held, part
        self.sib_in, self.xh_in, self.yh_in, self.xf_in, self.yf_in, self.z_in = bufs
        (
            self.so,
            self.si,
            self.xho,
            self.xhi,
            self.yho,
            self.yhi,
            self.xfo,
            self.xfi,
            self.yfo,
            self.yfi,
            self.zo,
            self.zi,
        ) = sems
        self.low, self.middle, self.high = low, middle, high
        self.x = at.s // 2
        self.rows = pl.ds(low, high - low)
        self.top = pl.ds(low, middle - low)
        self.bottom = pl.ds(middle, high - middle)

    def mine(self, z, y, x, rows):
        return self.held.at[self.at.core, z * 2 + y, x, rows]

    def sib(self, z):
        pair = pl.ds(z * 2, 2)
        p = self.part
        return remote(
            self.held.at[1 - self.at.core, pair, :, self.rows],
            self.sib_in.at[pair, :, self.rows],
            self.so.at[p, z],
            self.si.at[p, z],
            self.at.sibling,
        )

    def x_half(self, z):
        p = self.part
        source = self.mine(z, 1 - self.at.y, 1 - self.x, self.top)
        return remote(
            source, self.xh_in.at[z, self.top], self.xho.at[p, z], self.xhi.at[p, z], self.at.over_x
        )

    def y_half(self, z):
        p = self.part
        source = self.mine(z, 1 - self.at.y, 1 - self.x, self.bottom)
        return remote(
            source,
            self.yh_in.at[z, self.bottom],
            self.yho.at[p, z],
            self.yhi.at[p, z],
            self.at.over_y,
        )

    def x_full(self, z):
        p = self.part
        source = self.mine(z, self.at.y, 1 - self.x, self.rows)
        return remote(
            source,
            self.xf_in.at[z, self.rows],
            self.xfo.at[p, z],
            self.xfi.at[p, z],
            self.at.over_x,
        )

    def y_full(self, z):
        p = self.part
        source = self.mine(z, 1 - self.at.y, self.x, self.rows)
        return remote(
            source,
            self.yf_in.at[z, self.rows],
            self.yfo.at[p, z],
            self.yfi.at[p, z],
            self.at.over_y,
        )

    def z_part(self, z):
        p = self.part
        source = self.mine(z, self.at.y, self.x, self.rows)
        return remote(
            source,
            self.z_in.at[self.at.z, self.rows],
            self.zo.at[p, z],
            self.zi.at[p, self.at.z],
            self.at.at_z(z),
        )

    def z_arrival(self, z):
        p = self.part
        source = self.mine(z, self.at.y, self.x, self.rows)
        return remote(
            source,
            self.z_in.at[z, self.rows],
            self.zo.at[p, z],
            self.zi.at[p, z],
            self.at.at_z(z),
        )

    def add(self, z, y, x, rows, more):
        core, f = self.at.core, z * 2 + y
        self.held[core, f, x, rows] = (
            self.held[core, f, x, rows].astype(jnp.float32) + more.astype(jnp.float32)
        ).astype(jnp.bfloat16)

    def send_sib(self):
        for j in (3, 2, 1, 0):
            self.sib(self.at.source(j)).start()

    def merge(self):
        for j in (3, 2, 1, 0):
            z = self.at.source(j)
            self.sib(z).wait_recv()
            for y in (0, 1):
                for x in (0, 1):
                    self.add(z, y, x, self.rows, self.sib_in[z * 2 + y, x, self.rows])
            self.x_half(z).start()
            self.y_half(z).start()

    def pair_up(self):
        at = self.at
        for j in (3, 2, 1, 0):
            z = at.source(j)
            self.x_half(z).wait_recv()
            self.add(z, 1 - at.y, self.x, self.top, self.xh_in[z, self.top])
            self.y_full(z).start()
            self.y_half(z).wait_recv()
            self.add(z, at.y, 1 - self.x, self.bottom, self.yh_in[z, self.bottom])
            self.x_full(z).start()

    def collect(self):
        at = self.at
        for j in (3, 2, 1, 0):
            z = at.source(j)
            self.y_full(z).wait_recv()
            self.x_full(z).wait_recv()
            more = self.yf_in[z, self.rows].astype(jnp.float32) + self.xf_in[
                z, self.rows
            ].astype(jnp.float32)
            self.add(z, at.y, self.x, self.rows, more)
            if j > 0:
                self.z_part(z).start()

    def total(self):
        at = self.at
        value = self.held[at.core, at.f, self.x, self.rows].astype(jnp.float32)
        for j in (3, 2, 1):
            z = at.source(j)
            self.z_arrival(z).wait_recv()
            value = value + self.z_in[z, self.rows].astype(jnp.float32)
        return value

    def drain(self):
        for j in range(4):
            z = self.at.source(j)
            for copy in (self.sib, self.x_half, self.y_half, self.x_full, self.y_full):
                copy(z).wait_send()
            if j > 0:
                self.z_part(z).wait_send()


class GainSum:
    def __init__(self, at, row, outgoing, incoming, sems):
        self.at, self.row, self.outgoing, self.incoming = at, row, outgoing, incoming
        self.out, self.inc = sems
        self.partners = (at.sibling, at.over_x, at.over_y)

    def stage(self, k):
        return remote(
            self.outgoing.at[k],
            self.incoming.at[k],
            self.out.at[k],
            self.inc.at[k],
            self.partners[k],
        )

    def last(self, src, j, device):
        return remote(
            self.outgoing.at[3],
            self.incoming.at[3 + src],
            self.out.at[2 + j],
            self.inc.at[3 + src],
            device,
        )

    def send(self, k):
        self.outgoing[k] = self.row[...]
        if k < 3:
            self.stage(k).start()
        else:
            for j in (1, 2, 3):
                self.last(self.at.z, j, self.at.at_z(self.at.source(j))).start()

    def take(self, k):
        if k < 3:
            self.stage(k).wait_recv()
            self.row[...] += self.incoming[k]
        else:
            for j in (1, 2, 3):
                src = self.at.source(j)
                self.last(src, j, self.at.at_z(src)).wait_recv()
                self.row[...] += self.incoming[3 + src]

    def drain(self):
        for k in range(3):
            self.stage(k).wait_send()
        for j in (1, 2, 3):
            self.last(self.at.z, j, self.at.at_z(self.at.source(j))).wait_send()


class Refs:
    def __init__(self, names, refs):
        for name, ref in zip(names, refs):
            setattr(self, name, ref)


def columns_of(head):
    return slice(256 * head, 256 * head + 256)


def front_phase(at, r, sems):
    core, s = at.core, at.s
    gathered = GainGather(at, r.gain_all, sems[:4])
    w_sems = sems[4:15]
    kv_out, kv_in, x_out, x_in = sems[15:19]
    w_all, kv_all = r.w_all, r.kv_all
    early = WeightGather(at, w_all, w_sems, 0, 0, 48)
    late = WeightGather(at, w_all, w_sems, 1, 48, 80)
    chip = at.f * 2 + s // 2
    w_all[chip, core, 0:32] = r.own_q[...]
    w_all[chip, core, 32:48] = jnp.concatenate(
        [r.own_k[...].astype(jnp.float32), r.own_v[...].astype(jnp.float32)], axis=0
    ).astype(jnp.bfloat16)
    w_all[chip, core, 48:80] = r.own_o[...]
    r.gain_all[at.f * 4 + s] = r.gain_row[...]
    greet(
        [at.sibling, at.over_x, at.over_y]
        + [at.at_z(lax.rem(at.z + step, 4)) for step in (1, 2, 3)]
    )
    def x_weight(k):
        ref = (r.own_gate, r.own_up, r.own_down)[k]
        return remote(ref, r.peer_w.at[k], x_out.at[k], x_in.at[k], at.over_x)

    def gain_step(k):
        def step():
            gathered.take(k)
            if k < 3:
                gathered.send(k + 1)

        return step

    gathered.send(0)
    early.begin()
    late.begin()
    gain_step(0)()
    early.spread()
    x_weight(0).start()
    x_weight(1).start()
    gain_step(1)()
    early.walk((gain_step(2), gain_step(3), late.spread))
    placed = r.gain_all[...].reshape(32, 256)
    pieces = []
    for m in range(8):
        for k in range(5):
            piece = None
            if k < 4:
                piece = placed[4 * m + k : 4 * m + k + 1, :128]
            if k > 0:
                other = placed[4 * m + k - 1 : 4 * m + k, 128:]
                piece = other if piece is None else piece + other
            pieces.append(piece)
    r.gains[...] = jnp.concatenate(pieces, axis=1)
    gain = gain_parts(r)
    residual = r.tokens[...].astype(jnp.float32)
    r.normed[...] = (residual * rms_scale(residual) * gain[0]).astype(jnp.bfloat16)
    early.settle()
    normed = r.normed[...]
    cos, sin = r.cos[...], r.sin[...]
    mixed_rows = rows_of_all(w_all, 32, 16)
    r.wk[...] = nn(pick(0), mixed_rows).astype(jnp.bfloat16)
    r.wv[...] = nn(pick(8), mixed_rows).astype(jnp.bfloat16)
    k_raw = nt(normed, r.wk[...])
    r.k_raw[...] = k_raw
    key = turn(k_raw * rms_scale(k_raw) * gain[2], cos, sin)
    kv_all[s, :, :256] = key.astype(jnp.bfloat16)
    kv_all[s, :, 256:] = nt(normed, r.wv[...]).astype(jnp.bfloat16)

    def kv_copy(which, slot, device):
        return remote(kv_all.at[slot], kv_all.at[slot], kv_out.at[which], kv_in.at[which], device)

    peer_slot = lax.rem(s + 2, 4)
    kv_copy(0, s, at.over_x).start()
    kv_copy(1, s, at.sibling).start()

    def one_query(head):
        q_raw = nt(normed, rows_of_head(w_all, head, 0, 32))
        r.q_raw[:, columns_of(head)] = q_raw
        query = turn(q_raw * rms_scale(q_raw) * gain[1], cos, sin)
        r.query[:, columns_of(head)] = query.astype(jnp.bfloat16)

    def pass_kv():
        one_query(0)
        kv_copy(0, peer_slot, at.over_x).wait_recv()
        kv_copy(2, peer_slot, at.sibling).start()
        x_weight(2).start()
        one_query(1)

    late.walk((pass_kv, lambda: one_query(2), lambda: one_query(3)))
    other = s + 1 - 2 * core
    kv_copy(1, other, at.sibling).wait_recv()
    kv_copy(2, lax.rem(other + 2, 4), at.sibling).wait_recv()
    keys, values = kv_parts(r)
    key_place = lax.broadcasted_iota(jnp.int32, (128, 512), 1)
    query_place = lax.broadcasted_iota(jnp.int32, (128, 512), 0) + s * 128
    allowed = (key_place >= r.doc[...]) & (key_place <= query_place)
    for head in range(4):
        raw = nt(r.query[:, columns_of(head)], keys) * score_step
        scores = jnp.where(allowed, raw, hidden_score)
        weights = jnp.exp(scores - jnp.max(scores, axis=1, keepdims=True))
        prob = weights / jnp.sum(weights, axis=1, keepdims=True)
        r.prob[head] = prob
        mixed = nn(prob.astype(jnp.bfloat16), values).astype(jnp.bfloat16)
        r.mixed[:, columns_of(head)] = mixed
    late.settle()
    attn = nn(r.mixed[...], rows_of_all(w_all, 48, 32))
    r.attn[...] = attn
    middle = r.tokens[...].astype(jnp.float32) + attn * rms_scale(attn) * gain[3]
    r.middle[...] = middle
    normed_ffn = (middle * rms_scale(middle) * gain[4]).astype(jnp.bfloat16)

    def drain():
        gathered.drain()
        early.drain()
        late.drain()
        kv_copy(0, s, at.over_x).wait_send()
        kv_copy(1, s, at.sibling).wait_send()
        kv_copy(2, peer_slot, at.sibling).wait_send()

    return normed_ffn, x_weight, drain


def gain_parts(r):
    return [r.gains[:, a:b] for a, b in zip(gain_edges[:-1], gain_edges[1:])]


def kv_parts(r):
    return r.kv_all[...].reshape(512, 512)[:, :256], r.kv_all[...].reshape(512, 512)[:, 256:]


def ffn_phase(at, r, sems, normed_ffn, x_weight):
    core = at.core
    fwd_gather, fwd_sum = sems[:7], sems[7:13]
    bwd_gather, bwd_sum = sems[13:20], sems[20:26]
    x_out, x_in = sems[26:28]
    sum_bufs = (r.to_sib, r.from_sib, r.chip_sum, r.from_y, r.to_z, r.from_z)
    normed_all, grad_all = r.held.at[0], r.held.at[1]
    gates = (r.own_gate, r.peer_w.at[0])
    ups = (r.own_up, r.peer_w.at[1])
    downs = (r.own_down, r.peer_w.at[2])
    r.held[0, at.f, core] = normed_ffn

    def rows_of(which, chip):
        return jnp.concatenate([r.held[which, chip, core], r.held[which, chip, 1 - core]], axis=0)

    def weights_here():
        for k in range(3):
            x_weight(k).wait()

    def forward(chip):
        rows = rows_of(0, chip)
        total = None
        for half in (0, 1):
            gate = nt(rows, gates[half][...])
            up = nt(rows, ups[half][...])
            r.gate_keep[half, chip] = gate.astype(jnp.bfloat16)
            r.up_keep[half, chip] = up.astype(jnp.bfloat16)
            bend = jnp.tanh(gelu_c * (gate + 0.044715 * gate * gate * gate))
            hidden = (0.5 * gate * (1.0 + bend) * up).astype(jnp.bfloat16)
            part = nn(hidden, downs[half][...])
            total = part if total is None else total + part
        return total[:128], total[128:]

    finish, drain = exchange_pass(
        at, normed_all, fwd_gather, fwd_sum, sum_bufs, r.part_own, forward, 0, weights_here
    )
    ffn_raw = finish()
    drain()
    gain = gain_parts(r)[5]
    scale = rms_scale(ffn_raw)
    r.result[...] = (r.middle[...] + ffn_raw * scale * gain).astype(jnp.bfloat16)
    ffn_grad, gain_grad = norm_back(ffn_raw, gain, r.cotangent[...].astype(jnp.float32))
    r.gain_sum[:, gain_edges[5] : gain_edges[6]] = gain_grad
    r.held[1, at.f, core] = ffn_grad.astype(jnp.bfloat16)
    own_grads = (r.gate_grad, r.up_grad, r.down_grad)
    grads = (own_grads, tuple(r.peer_sum.at[k] for k in range(3)))
    for half in (0, 1):
        for target in grads[half]:
            target[...] = jnp.zeros(target.shape, jnp.float32)

    def backward(chip):
        rows = rows_of(1, chip)
        ahead = rows_of(0, chip)
        total = None
        for half in (0, 1):
            dhidden = nt(rows, downs[half][...])
            gate = r.gate_keep[half, chip].astype(jnp.float32)
            up = r.up_keep[half, chip].astype(jnp.float32)
            square = gate * gate
            bend = jnp.tanh(gelu_c * (gate + 0.044715 * square * gate))
            unit = 0.5 * gate * (1.0 + bend)
            slope = 0.5 * (1.0 + bend) + 0.5 * gate * (1.0 - bend * bend) * (
                gelu_c * (1.0 + 3 * 0.044715 * square)
            )
            hidden = (unit * up).astype(jnp.bfloat16)
            dgate = (dhidden * up * slope).astype(jnp.bfloat16)
            dup = (dhidden * unit).astype(jnp.bfloat16)
            part = nn(dgate, gates[half][...]) + nn(dup, ups[half][...])
            total = part if total is None else total + part
            gate_sum, up_sum, down_sum = grads[half]
            gate_sum[...] += tn(dgate, ahead)
            up_sum[...] += tn(dup, ahead)
            down_sum[...] += tn(hidden, rows)
        return total[:128], total[128:]

    def x_copy(k):
        return remote(r.peer_w.at[k], r.from_x.at[k], x_out.at[k], x_in.at[k], at.over_x)

    def send_x():
        for k in range(3):
            r.peer_w[k] = r.peer_sum[k].astype(jnp.bfloat16)
            x_copy(k).start()

    finish, drain = exchange_pass(
        at, grad_all, bwd_gather, bwd_sum, sum_bufs, r.part_own, backward, 0, None, send_x
    )
    normed_grad = finish()
    drain()

    def complete():
        for k in range(3):
            x_copy(k).wait()
            own_grads[k][...] += r.from_x[k].astype(jnp.float32)

    return normed_grad, complete


def back_phase(at, r, sems, normed_grad, complete):
    core, s = at.core, at.s
    x = s // 2
    gain = gain_parts(r)
    cos, sin = r.cos[...], r.sin[...]
    bufs = (r.sib_in, r.half_in, r.half_in, r.xf_in, r.yf_in, r.zw_in)
    w_sems = sems[:12]
    kv_out, kv_in = sems[12:14]
    outer = WeightReturn(at, r.held, bufs, w_sems, 1, 48, 64, 80)
    inner = WeightReturn(at, r.held, bufs, w_sems, 0, 0, 16, 48)
    gain_total = GainSum(at, r.gain_sum, r.gain_out, r.gain_in, sems[14:16])

    def put_gain(k, value):
        r.gain_sum[:, gain_edges[k] : gain_edges[k + 1]] = value

    def put_rows(head, low, count, rows):
        split = rows.astype(jnp.bfloat16).reshape(4, 2, count, rows.shape[-1])
        for c in range(4):
            for k in (0, 1):
                r.held[k, 2 * head + c // 2, c % 2, low : low + count] = split[c, k]

    part, gain_grad = norm_back(r.middle[...], gain[4], normed_grad)
    put_gain(4, gain_grad)
    middle_grad = r.cotangent[...].astype(jnp.float32) + part
    r.middle[...] = middle_grad
    attn_grad, gain_grad = norm_back(r.attn[...], gain[3], middle_grad)
    put_gain(3, gain_grad)
    attn_grad = attn_grad.astype(jnp.bfloat16)
    for head in range(4):
        put_rows(head, 48, 32, tn(r.mixed[:, columns_of(head)], attn_grad))
    outer.send_sib()
    keys, values = kv_parts(r)
    for head in range(4):
        mixed_grad = nt(attn_grad, rows_of_head(r.w_all, head, 48, 32)).astype(jnp.bfloat16)
        prob = r.prob[head]
        prob_grad = nt(mixed_grad, values)
        delta = jnp.sum(prob * prob_grad, axis=1, keepdims=True)
        score_grad = (prob * (prob_grad - delta)).astype(jnp.bfloat16)
        key_part = tn(score_grad, r.query[:, columns_of(head)]) * score_step
        value_part = tn(prob.astype(jnp.bfloat16), mixed_grad)
        if head == 0:
            r.kv_sum[:, :256] = key_part
            r.kv_sum[:, 256:] = value_part
        else:
            r.kv_sum[:, :256] += key_part
            r.kv_sum[:, 256:] += value_part
        r.query_grad[:, columns_of(head)] = nn(score_grad, keys) * score_step
    r.kv_part[...] = r.kv_sum[...].astype(jnp.bfloat16).reshape(2, 2, 128, 512)
    kv_sib = remote(
        r.kv_part.at[:, 1 - core], r.kv_sib.at[...], kv_out.at[0], kv_in.at[0], at.sibling
    )
    kv_sib.start()
    outer.merge()
    kv_sib.wait_recv()
    r.kv_chip[...] = (
        r.kv_part[1 - x, core].astype(jnp.float32) + r.kv_sib[1 - x].astype(jnp.float32)
    ).astype(jnp.bfloat16)
    kv_x = remote(r.kv_chip, r.kv_far, kv_out.at[1], kv_in.at[1], at.over_x)
    kv_x.start()
    normed = r.normed[...]
    query_gain = None
    for head in range(4):
        turned = turn_back(r.query_grad[:, columns_of(head)], cos, sin)
        q_raw_grad, gain_grad = norm_back(r.q_raw[:, columns_of(head)], gain[1], turned)
        query_gain = gain_grad if query_gain is None else query_gain + gain_grad
        q_raw_grad = q_raw_grad.astype(jnp.bfloat16)
        r.query[:, columns_of(head)] = q_raw_grad
        put_rows(head, 0, 32, tn(q_raw_grad, normed))
    put_gain(1, query_gain)
    outer.pair_up()
    kv_x.wait_recv()
    kv_grad = (
        r.kv_part[x, core].astype(jnp.float32)
        + r.kv_sib[x].astype(jnp.float32)
        + r.kv_far[...].astype(jnp.float32)
    )
    k_raw_grad, gain_grad = norm_back(r.k_raw[...], gain[2], turn_back(kv_grad[:, :256], cos, sin))
    put_gain(2, gain_grad)
    k_raw_grad = k_raw_grad.astype(jnp.bfloat16)
    v_raw_grad = kv_grad[:, 256:].astype(jnp.bfloat16)
    woven = (nn(k_raw_grad, pick(0)) + nn(v_raw_grad, pick(8))).astype(jnp.bfloat16)
    for head in range(4):
        put_rows(head, 32, 16, tn(woven[:, 128 * head : 128 * head + 128], normed))
    inner.send_sib()
    normed_grad = nn(k_raw_grad, r.wk[...]) + nn(v_raw_grad, r.wv[...])
    for head in range(4):
        normed_grad += nn(r.query[:, columns_of(head)], rows_of_head(r.w_all, head, 0, 32))
    part, gain_grad = norm_back(r.tokens[...].astype(jnp.float32), gain[0], normed_grad)
    put_gain(0, gain_grad)
    gain_total.send(0)
    r.token_grad[...] = r.middle[...] + part
    inner.merge()
    gain_total.take(0)
    gain_total.send(1)
    outer.collect()
    inner.pair_up()
    gain_total.take(1)
    gain_total.send(2)
    inner.collect()
    gain_total.take(2)
    gain_total.send(3)
    r.o_grad[...] = outer.total()
    complete()
    total = inner.total()
    r.q_grad[...] = total[:32]
    r.k_grad[...] = total[32:40]
    r.v_grad[...] = total[40:48]
    gain_total.take(3)
    device = at.f * 4 + s
    first = pl.multiple_of(device * 160 // 128 * 128, 128)
    r.gain_grad[...] = pltpu.roll(
        r.gain_sum[:, pl.ds(first, 256)], 256 - lax.rem(device, 4) * 32, 1
    )
    outer.drain()
    inner.drain()
    gain_total.drain()
    kv_sib.wait_send()
    kv_x.wait_send()


def layer_call(values):
    b16, f32 = jnp.bfloat16, jnp.float32
    rows, width = values["tokens"].shape
    units = values["own_gate"].shape[0]
    outs = {
        "result": ((rows, width), b16),
        "token_grad": ((rows, width), f32),
        "gain_grad": ((1, 256), f32),
        "q_grad": ((32, width), f32),
        "k_grad": ((8, width), f32),
        "v_grad": ((8, width), f32),
        "o_grad": ((32, width), f32),
        "gate_grad": ((units, width), f32),
        "up_grad": ((units, width), f32),
        "down_grad": ((units, width), f32),
    }
    scratch = {
        "gain_sum": ((1, 5120), f32),
        "w_all": ((16, 2, 80, width), b16),
        "gain_all": ((32, 1, 256), f32),
        "gains": ((1, 5120), f32),
        "wk": ((256, width), b16),
        "wv": ((256, width), b16),
        "normed": ((rows, width), b16),
        "k_raw": ((rows, 256), f32),
        "q_raw": ((rows, 1024), f32),
        "query": ((rows, 1024), b16),
        "query_grad": ((rows, 1024), f32),
        "kv_all": ((4, rows, 512), b16),
        "prob": ((4, rows, 512), f32),
        "mixed": ((rows, 1024), b16),
        "attn": ((rows, width), f32),
        "middle": ((rows, width), f32),
        "peer_w": ((3, units, width), b16),
        "held": ((2, 8, 2, rows, width), b16),
        "gate_keep": ((2, 8, 2 * rows, units), b16),
        "up_keep": ((2, 8, 2 * rows, units), b16),
        "peer_sum": ((3, units, width), f32),
        "part_own": ((rows, width), f32),
        "to_sib": ((8, rows, width), b16),
        "from_sib": ((8, rows, width), b16),
        "chip_sum": ((8, rows, width), b16),
        "from_y": ((4, rows, width), b16),
        "to_z": ((4, rows, width), b16),
        "from_z": ((2, 4, rows, width), b16),
        "from_x": ((3, units, width), b16),
        "sib_in": ((8, 2, 80, width), b16),
        "half_in": ((4, 80, width), b16),
        "xf_in": ((4, 80, width), b16),
        "yf_in": ((4, 80, width), b16),
        "zw_in": ((4, 80, width), b16),
        "kv_sum": ((4 * rows, 512), f32),
        "kv_part": ((2, 2, rows, 512), b16),
        "kv_sib": ((2, rows, 512), b16),
        "kv_chip": ((rows, 512), b16),
        "kv_far": ((rows, 512), b16),
        "gain_out": ((4, 1, 5120), f32),
        "gain_in": ((7, 1, 5120), f32),
    }
    gather_sems = [DMA((2,)), DMA((4,)), DMA((4,)), DMA((4,)), DMA((4,)), DMA((8,)), DMA((8,))]
    sum_sems = [DMA((8,)), DMA((8,)), DMA((4,)), DMA((4,)), DMA((4,)), DMA((2, 4))]
    front_sems = gain_sems() + gather_weight_sems() + [DMA((3,))] * 4
    ffn_sems = (gather_sems + sum_sems) * 2 + [DMA((3,)), DMA((3,))]
    back_sems = [DMA((2, 4))] * 12 + [DMA((2,)), DMA((2,)), DMA((6,)), DMA((7,))]
    sems = front_sems + ffn_sems + back_sems
    names = tuple(values) + tuple(outs) + tuple(scratch)

    def kernel(*refs):
        at = Place()
        r = Refs(names, refs)
        held_sems = refs[len(names) :]
        first, second = len(front_sems), len(front_sems) + len(ffn_sems)
        normed_ffn, x_weight, drain = front_phase(at, r, held_sems[:first])
        normed_grad, complete = ffn_phase(at, r, held_sems[first:second], normed_ffn, x_weight)
        back_phase(at, r, held_sems[second:], normed_grad, complete)
        drain()

    vmem = pl.BlockSpec(memory_space=pltpu.VMEM)
    out = pl.pallas_call(
        kernel,
        out_shape=tuple(jax.ShapeDtypeStruct(*spec) for spec in outs.values()),
        in_specs=[vmem] * len(values),
        out_specs=tuple([vmem] * len(outs)),
        scratch_shapes=[pltpu.VMEM(*spec) for spec in scratch.values()] + sems,
        compiler_params=pltpu.CompilerParams(
            collective_id=1, has_side_effects=True, vmem_limit_bytes=63 << 20
        ),
        name="layer",
    )(*values.values())
    return dict(zip(outs, out))


def settle_kernel(count, *refs):
    ins, outs, held, sems = refs[:count], refs[count : 2 * count], refs[2 * count : -1], refs[-1]
    loads = [pltpu.make_async_copy(ins[k], held[k], sems.at[0, k]) for k in range(count)]
    stores = [pltpu.make_async_copy(held[k], outs[k], sems.at[1, k]) for k in range(count)]
    for copy in loads:
        copy.start()
    for load, store in zip(loads, stores):
        load.wait()
        store.start()
    for copy in stores:
        copy.wait()


def settle(arrays):
    anywhere = pl.BlockSpec(memory_space=pl.ANY)
    return pl.pallas_call(
        partial(settle_kernel, len(arrays)),
        out_shape=tuple(jax.ShapeDtypeStruct(a.shape, a.dtype) for a in arrays),
        in_specs=[anywhere] * len(arrays),
        out_specs=tuple([anywhere] * len(arrays)),
        scratch_shapes=[pltpu.VMEM(a.shape, a.dtype) for a in arrays] + [DMA((2, len(arrays)))],
        name="settle",
    )(*arrays)


def one_kernel(
    tokens, doc_start, gains, w_query, w_key, w_value, w_out, w_gate, w_up, w_down, cotangent
):
    rows = tokens.shape[0]
    device = lax.axis_index("fsdp") * lax.axis_size("seq") + lax.axis_index("seq")
    share = gains.shape[0]
    gain_row = lax.dynamic_update_slice(
        jnp.zeros((1, 256), jnp.float32),
        gains[None].astype(jnp.float32),
        (0, lax.rem(device, 4) * 32),
    )
    places = lax.axis_index("seq") * rows + jnp.arange(rows, dtype=jnp.int32) - doc_start
    cos, sin = rope_tables(places, 256)
    out = layer_call(
        {
            "tokens": tokens,
            "doc": doc_start[:, None],
            "gain_row": gain_row,
            "own_q": w_query.T,
            "own_k": w_key.T,
            "own_v": w_value.T,
            "own_o": w_out,
            "own_gate": w_gate.T,
            "own_up": w_up.T,
            "own_down": w_down,
            "cos": cos[:, 0],
            "sin": sin[:, 0],
            "cotangent": cotangent,
        }
    )
    names = ("result", "token_grad", "gain_grad", "q_grad", "k_grad", "v_grad", "o_grad")
    names += ("gate_grad", "up_grad", "down_grad")
    out = dict(zip(names, settle([out[name] for name in names])))
    return (
        out["result"],
        out["token_grad"],
        out["gain_grad"][0, :share],
        out["q_grad"].T,
        out["k_grad"].T,
        out["v_grad"].T,
        out["o_grad"],
        out["gate_grad"].T,
        out["up_grad"].T,
        out["down_grad"],
    )


def solution(mesh):
    in_specs = (
        P(("fsdp", "seq"), None),
        P(("fsdp", "seq")),
        P(("fsdp", "seq")),
        P(None, ("fsdp", "seq")),
        P(None, ("fsdp", "seq")),
        P(None, ("fsdp", "seq")),
        P(("fsdp", "seq"), None),
        P(None, ("fsdp", "seq")),
        P(None, ("fsdp", "seq")),
        P(("fsdp", "seq"), None),
        P(("fsdp", "seq"), None),
    )
    out_specs = (
        P(("fsdp", "seq"), None),
        P(("fsdp", "seq"), None),
        P(("fsdp", "seq")),
        P(None, ("fsdp", "seq")),
        P(None, ("fsdp", "seq")),
        P(None, ("fsdp", "seq")),
        P(("fsdp", "seq"), None),
        P(None, ("fsdp", "seq")),
        P(None, ("fsdp", "seq")),
        P(("fsdp", "seq"), None),
    )
    body = one_kernel if dict(mesh.shape) == {"fsdp": 8, "seq": 4} else local
    return jax.shard_map(body, mesh=mesh, in_specs=in_specs, out_specs=out_specs, check_vma=False)
```

```python
from functools import partial

import jax
import jax.numpy as jnp
from jax import lax
from jax.experimental import pallas as pl
from jax.experimental.pallas import tpu as pltpu
from jax.sharding import PartitionSpec as P

norm_eps = 1e-06
rope_base = 1000000.0
score_scale = 0.0625
masked_value = -1e30


def product(former, latter):
    return jnp.dot(former, latter, preferred_element_type=jnp.float32)


def inner_rows(former, latter):
    return lax.dot_general(
        former, latter, (((0,), (0,)), ((), ())), preferred_element_type=jnp.float32
    )


def outer_rows(former, latter):
    return lax.dot_general(
        former, latter, (((1,), (1,)), ((), ())), preferred_element_type=jnp.float32
    )


def scaled_norm(values, factor):
    return values * lax.rsqrt(jnp.mean(values * values, axis=-1, keepdims=True) + norm_eps) * factor


def rotate(values, cos_table, sin_table):
    half_width = values.shape[-1] // 2
    leading = values[..., :half_width]
    trailing = values[..., half_width:]
    return jnp.concatenate(
        [leading * cos_table - trailing * sin_table, trailing * cos_table + leading * sin_table],
        axis=-1,
    )


def head_norm(values, factor, cos_table, sin_table):
    return rotate(scaled_norm(values, factor), cos_table, sin_table)


def gated_unit(gate_in, up_in):
    return jax.nn.gelu(gate_in, approximate=True) * up_in


def rope_tables(places, rot_width):
    half_width = rot_width // 2
    frequency = rope_base ** (-2.0 * jnp.arange(half_width, dtype=jnp.float32) / rot_width)
    angles = places.astype(jnp.float32)[:, None] * frequency[None, :]
    return (jnp.cos(angles)[:, None, :], jnp.sin(angles)[:, None, :])


def masked_scores(queries, key_rows, bounds, offset):
    raw_scores = outer_rows(queries, key_rows) * score_scale
    query_place = offset + jnp.arange(queries.shape[0], dtype=jnp.int32)
    key_place = jnp.arange(key_rows.shape[0], dtype=jnp.int32)
    allowed = (key_place[None, :] >= bounds[:, None]) & (key_place[None, :] <= query_place[:, None])
    return jnp.where(allowed, raw_scores, masked_value)


def local(
    tokens, doc_start, gains, w_query, w_key, w_value, w_out, w_gate, w_up, w_down, cotangent
):
    tok_rows = tokens.shape[0]
    model_width = tokens.shape[1]
    run_index = lax.axis_index("seq")
    gains_all, query_w, key_w, value_w, out_w = (
        lax.all_gather(gains, ("fsdp", "seq"), axis=0, tiled=True),
        lax.all_gather(w_query, ("fsdp", "seq"), axis=1, tiled=True),
        lax.all_gather(w_key, ("fsdp", "seq"), axis=1, tiled=True),
        lax.all_gather(w_value, ("fsdp", "seq"), axis=1, tiled=True),
        lax.all_gather(w_out, ("fsdp", "seq"), axis=0, tiled=True),
    )
    gate_w, up_w, down_w = (
        lax.all_gather(w_gate, ("fsdp", "seq"), axis=1, tiled=True),
        lax.all_gather(w_up, ("fsdp", "seq"), axis=1, tiled=True),
        lax.all_gather(w_down, ("fsdp", "seq"), axis=0, tiled=True),
    )
    head_width = key_w.shape[1]
    head_count = query_w.shape[1] // head_width
    gain_values = gains_all.astype(jnp.float32)
    gain_pre = gain_values[:model_width]
    gain_query = gain_values[model_width : model_width + head_width]
    gain_key = gain_values[model_width + head_width : model_width + 2 * head_width]
    gain_post = gain_values[model_width + 2 * head_width : 2 * model_width + 2 * head_width]
    gain_pre_ffn = gain_values[2 * model_width + 2 * head_width : 3 * model_width + 2 * head_width]
    gain_post_ffn = gain_values[3 * model_width + 2 * head_width :]
    residual = tokens.astype(jnp.float32)
    normed, pre_pull = jax.vjp(scaled_norm, residual, gain_pre)
    normed_b = normed.astype(jnp.bfloat16)
    query_raw = product(normed_b, query_w).reshape(tok_rows, head_count, head_width)
    key_raw = product(normed_b, key_w).reshape(tok_rows, 1, head_width)
    value_b = product(normed_b, value_w).astype(jnp.bfloat16)
    places = run_index * tok_rows + jnp.arange(tok_rows, dtype=jnp.int32) - doc_start
    cos_table, sin_table = rope_tables(places, head_width)
    rope_norm = partial(head_norm, cos_table=cos_table, sin_table=sin_table)
    query_rot, query_pull = jax.vjp(rope_norm, query_raw, gain_query)
    key_rot, key_pull = jax.vjp(rope_norm, key_raw, gain_key)
    query_b = query_rot.reshape(tok_rows, head_count * head_width).astype(jnp.bfloat16)
    key_b = key_rot.reshape(tok_rows, head_width).astype(jnp.bfloat16)
    query_heads = lax.all_to_all(query_b, "seq", split_axis=1, concat_axis=0, tiled=True)
    key_rows, value_rows = (
        lax.all_gather(key_b, "seq", axis=0, tiled=True),
        lax.all_gather(value_b, "seq", axis=0, tiled=True),
    )
    starts = lax.all_gather(doc_start, "seq", axis=0, tiled=True)
    seq_tokens = key_rows.shape[0]
    block_rows = min(512, seq_tokens)
    block_count = seq_tokens // block_rows
    query_blocks = query_heads.reshape(block_count, block_rows, head_width)
    start_blocks = starts.reshape(block_count, block_rows)
    block_ids = jnp.arange(block_count, dtype=jnp.int32)

    def attend(block_item):
        queries, bounds, block_index = block_item
        scores = masked_scores(queries, key_rows, bounds, block_index * block_rows)
        row_max = jnp.max(scores, axis=1, keepdims=True)
        weights = jnp.exp(scores - row_max)
        row_total = jnp.sum(weights, axis=1, keepdims=True)
        probability = (weights / row_total).astype(jnp.bfloat16)
        mixed_block = product(probability, value_rows).astype(jnp.bfloat16)
        return (mixed_block, (row_max + jnp.log(row_total))[:, 0])

    mixed_blocks, lse_blocks = lax.map(attend, (query_blocks, start_blocks, block_ids))
    mixed_heads = mixed_blocks.reshape(seq_tokens, head_width)
    mixed_tokens = lax.all_to_all(mixed_heads, "seq", split_axis=0, concat_axis=1, tiled=True)
    attn_raw = product(mixed_tokens, out_w)
    attn_out, post_pull = jax.vjp(scaled_norm, attn_raw, gain_post)
    middle = residual + attn_out
    normed_ffn, pre_ffn_pull = jax.vjp(scaled_norm, middle, gain_pre_ffn)
    normed_ffn_b = normed_ffn.astype(jnp.bfloat16)
    gate_act = product(normed_ffn_b, gate_w)
    up_act = product(normed_ffn_b, up_w)
    hidden, glu_pull = jax.vjp(gated_unit, gate_act, up_act)
    hidden_b = hidden.astype(jnp.bfloat16)
    ffn_raw = product(hidden_b, down_w)
    ffn_out, post_ffn_pull = jax.vjp(scaled_norm, ffn_raw, gain_post_ffn)
    result = (middle + ffn_out).astype(jnp.bfloat16)
    gate_w, up_w, down_w = (
        lax.all_gather(w_gate, ("fsdp", "seq"), axis=1, tiled=True),
        lax.all_gather(w_up, ("fsdp", "seq"), axis=1, tiled=True),
        lax.all_gather(w_down, ("fsdp", "seq"), axis=0, tiled=True),
    )
    query_w, key_w, value_w, out_w = (
        lax.all_gather(w_query, ("fsdp", "seq"), axis=1, tiled=True),
        lax.all_gather(w_key, ("fsdp", "seq"), axis=1, tiled=True),
        lax.all_gather(w_value, ("fsdp", "seq"), axis=1, tiled=True),
        lax.all_gather(w_out, ("fsdp", "seq"), axis=0, tiled=True),
    )
    upstream = cotangent.astype(jnp.float32)
    ffn_grad, gain_post_ffn_grad = post_ffn_pull(upstream)
    ffn_grad_b = ffn_grad.astype(jnp.bfloat16)
    down_w_grad = inner_rows(hidden_b, ffn_grad_b)
    hidden_grad = outer_rows(ffn_grad_b, down_w)
    gate_grad, up_grad = glu_pull(hidden_grad)
    gate_grad_b = gate_grad.astype(jnp.bfloat16)
    up_grad_b = up_grad.astype(jnp.bfloat16)
    gate_w_grad_t = inner_rows(gate_grad_b, normed_ffn_b)
    up_w_grad_t = inner_rows(up_grad_b, normed_ffn_b)
    normed_ffn_grad = outer_rows(gate_grad_b, gate_w) + outer_rows(up_grad_b, up_w)
    middle_part, gain_pre_ffn_grad = pre_ffn_pull(normed_ffn_grad)
    middle_grad = upstream + middle_part
    attn_grad, gain_post_grad = post_pull(middle_grad)
    attn_grad_b = attn_grad.astype(jnp.bfloat16)
    out_w_grad = inner_rows(mixed_tokens, attn_grad_b)
    mixed_grad = outer_rows(attn_grad_b, out_w).astype(jnp.bfloat16)
    mixed_grad_heads = lax.all_to_all(mixed_grad, "seq", split_axis=1, concat_axis=0, tiled=True)
    grad_blocks = mixed_grad_heads.reshape(block_count, block_rows, head_width)

    def attend_back(carried, block_item):
        key_accum, value_accum = carried
        queries, bounds, block_index, lse_row, block_grad = block_item
        scores = masked_scores(queries, key_rows, bounds, block_index * block_rows)
        probability = jnp.exp(scores - lse_row[:, None])
        prob_grad = outer_rows(block_grad, value_rows)
        value_accum = value_accum + inner_rows(probability.astype(jnp.bfloat16), block_grad)
        row_delta = jnp.sum(probability * prob_grad, axis=1, keepdims=True)
        score_grad = (probability * (prob_grad - row_delta)).astype(jnp.bfloat16)
        query_grad = product(score_grad, key_rows) * score_scale
        key_accum = key_accum + inner_rows(score_grad, queries) * score_scale
        return ((key_accum, value_accum), query_grad)

    zero_rows = jnp.zeros((seq_tokens, head_width), jnp.float32)
    (key_part, value_part), query_grad_blocks = lax.scan(
        attend_back,
        (zero_rows, zero_rows),
        (query_blocks, start_blocks, block_ids, lse_blocks, grad_blocks),
    )
    key_sum, value_sum = (
        lax.psum_scatter(
            key_part.astype(jnp.bfloat16), "seq", scatter_dimension=0, tiled=True
        ).astype(jnp.float32),
        lax.psum_scatter(
            value_part.astype(jnp.bfloat16), "seq", scatter_dimension=0, tiled=True
        ).astype(jnp.float32),
    )
    query_grad_tokens = lax.all_to_all(
        query_grad_blocks.reshape(seq_tokens, head_width).astype(jnp.bfloat16),
        "seq",
        split_axis=0,
        concat_axis=1,
        tiled=True,
    ).astype(jnp.float32)
    query_raw_grad, gain_query_grad = query_pull(
        query_grad_tokens.reshape(tok_rows, head_count, head_width)
    )
    key_raw_grad, gain_key_grad = key_pull(key_sum.reshape(tok_rows, 1, head_width))
    query_raw_b = query_raw_grad.reshape(tok_rows, head_count * head_width).astype(jnp.bfloat16)
    key_raw_b = key_raw_grad.reshape(tok_rows, head_width).astype(jnp.bfloat16)
    value_raw_b = value_sum.astype(jnp.bfloat16)
    query_w_grad_t = inner_rows(query_raw_b, normed_b)
    key_w_grad_t = inner_rows(key_raw_b, normed_b)
    value_w_grad_t = inner_rows(value_raw_b, normed_b)
    normed_grad = (
        outer_rows(query_raw_b, query_w)
        + outer_rows(key_raw_b, key_w)
        + outer_rows(value_raw_b, value_w)
    )
    residual_part, gain_pre_grad = pre_pull(normed_grad)
    input_grad = middle_grad + residual_part
    gains_grad = jnp.concatenate(
        [
            gain_pre_grad,
            gain_query_grad,
            gain_key_grad,
            gain_post_grad,
            gain_pre_ffn_grad,
            gain_post_ffn_grad,
        ]
    )
    shares = (
        lax.psum_scatter(gains_grad, ("fsdp", "seq"), scatter_dimension=0, tiled=True),
        lax.psum_scatter(query_w_grad_t, ("fsdp", "seq"), scatter_dimension=0, tiled=True),
        lax.psum_scatter(key_w_grad_t, ("fsdp", "seq"), scatter_dimension=0, tiled=True),
        lax.psum_scatter(value_w_grad_t, ("fsdp", "seq"), scatter_dimension=0, tiled=True),
        lax.psum_scatter(out_w_grad, ("fsdp", "seq"), scatter_dimension=0, tiled=True),
        lax.psum_scatter(gate_w_grad_t, ("fsdp", "seq"), scatter_dimension=0, tiled=True),
        lax.psum_scatter(up_w_grad_t, ("fsdp", "seq"), scatter_dimension=0, tiled=True),
        lax.psum_scatter(down_w_grad, ("fsdp", "seq"), scatter_dimension=0, tiled=True),
    )
    return (
        result,
        input_grad,
        shares[0],
        shares[1].T,
        shares[2].T,
        shares[3].T,
        shares[4],
        shares[5].T,
        shares[6].T,
        shares[7],
    )


gelu_c = 0.7978845608028654
MESH = pl.DeviceIdType.MESH
DMA = pltpu.SemaphoreType.DMA


def nt(former, latter):
    return lax.dot_general(
        former, latter, (((1,), (1,)), ((), ())), preferred_element_type=jnp.float32
    )


def nn(former, latter):
    return lax.dot_general(
        former, latter, (((1,), (0,)), ((), ())), preferred_element_type=jnp.float32
    )


def tn(former, latter):
    return lax.dot_general(
        former, latter, (((0,), (0,)), ((), ())), preferred_element_type=jnp.float32
    )


class Place:
    def __init__(self):
        self.f = lax.axis_index("fsdp")
        self.s = lax.axis_index("seq")
        self.z = self.f // 2
        self.y = lax.rem(self.f, 2)
        self.core = lax.rem(self.s, 2)
        self.high = self.z // 2
        self.inner = self.z * (3 - self.z) == 2
        self.outer = self.z * (3 - self.z) == 0
        self.sibling = (self.f, self.s + 1 - 2 * self.core)
        self.over_x = (self.f, lax.rem(self.s + 2, 4))
        self.over_y = (self.f + 1 - 2 * self.y, self.s)
        self.toward = 1 - 2 * self.high
        self.step_first = self.toward * (1 - self.z * (3 - self.z))

    def at_z(self, z):
        return (z * 2 + self.y, self.s)

    def source(self, j):
        last = j // 3
        middle = j // 2 - last
        none = (3 - j) // 3
        first = 1 - last - middle - none
        return (
            none * self.z
            + first * (1 - self.z + 4 * self.high)
            + middle * (2 - self.high)
            + last * (3 - 3 * self.high)
        )


def remote(source, target, send_sem, recv_sem, device):
    return pltpu.make_async_remote_copy(
        src_ref=source,
        dst_ref=target,
        send_sem=send_sem,
        recv_sem=recv_sem,
        device_id=device,
        device_id_type=MESH,
    )


def greet(partners):
    entry = pltpu.get_barrier_semaphore()
    for partner in partners:
        pl.semaphore_signal(entry, inc=1, device_id=partner, device_id_type=MESH)
    pl.semaphore_wait(entry, len(partners))


def exchange_pass(at, held, gather_sems, sum_sems, sum_bufs, part_own, compute, lag=0, ready=None, then=()):
    z_own, z_next, z_in, y_out, y_in, c_out, c_in = gather_sems
    t_out, t_in, v_out, v_in, w_out, w_in = sum_sems
    to_sib, from_sib, chip_sum, from_y, to_z, from_z = sum_bufs
    f, core = at.f, at.core

    def block(chip):
        return held.at[chip, core]

    def over(chip, outgoing, incoming, device):
        return remote(block(chip), block(chip), outgoing, incoming, device)

    def own_z(step, slot):
        return over(f, z_own.at[slot], z_in.at[at.z], at.at_z(at.z + step))

    def own_z_toward():
        return own_z(at.toward, 0)

    def own_z_away():
        return own_z(-at.toward, 1)

    def pass_z(src, step):
        return over(src * 2 + at.y, z_next.at[src], z_in.at[src], at.at_z(at.z + step))

    def pass_y(src):
        return over(src * 2 + at.y, y_out.at[src], y_in.at[src], at.over_y)

    def pass_sib(chip):
        return over(chip, c_out.at[chip], c_in.at[chip], at.sibling)

    own_z_toward().start()

    @pl.when(at.inner)
    def _():
        own_z_away().start()

    pass_y(at.z).start()
    pass_sib(f).start()

    def from_z_block(src):
        return over(src * 2 + at.y, z_next.at[src], z_in.at[src], at.at_z(src))

    def take_z(j, step):
        src = at.source(j)
        from_z_block(src).wait_recv()

        @pl.when(at.inner)
        def _():
            pass_z(src, step).start()

        pass_y(src).start()
        pass_sib(src * 2 + at.y).start()

    def chip_of(i):
        return at.source(i // 2) * 2 + lax.rem(at.y + lax.rem(i, 2), 2)

    def sib_sum(i):
        return remote(to_sib.at[i], from_sib.at[i], t_out.at[i], t_in.at[i], at.sibling)

    rows = part_own.shape[0] // 4
    pieces = [pl.ds(k * rows, rows) for k in range(4)]

    def y_sum(i, k):
        return remote(
            chip_sum.at[i, pieces[k]],
            from_y.at[i // 2, pieces[k]],
            v_out.at[i // 2, k],
            v_in.at[i // 2, k],
            at.over_y,
        )

    def send_y(i):
        for k in range(4):
            y_sum(i, k).start()

    def finish_chip(i):
        sib_sum(i).wait_recv()
        chip_sum[i] = (part_own[...] + from_sib[i].astype(jnp.float32)).astype(jnp.bfloat16)

    def arrivals(i):
        @pl.when(i == 1)
        def _():
            take_z(1, at.toward)

            @pl.when(at.inner)
            def _():
                take_z(2, -at.toward)

        @pl.when((i == 3) & at.outer)
        def _():
            take_z(2, -at.toward)

        @pl.when(((i == 3) & at.inner) | ((i == 5) & at.outer))
        def _():
            take_z(3, -at.toward)

        @pl.when(lax.rem(i, 2) == 1)
        def _():
            pass_y(at.source(i // 2)).wait_recv()
            pass_sib(chip_of(i)).start()

    def one_chip(i):
        chip = chip_of(i)
        pass_sib(chip).wait_recv()
        own_part, sib_part = compute(chip)
        to_sib[i] = sib_part.astype(jnp.bfloat16)
        sib_sum(i).start()

        @pl.when(i > 0)
        def _():
            finish_chip(i - 1)

        part_own[...] = own_part

    def step(i, carried):
        @pl.when(i < 8)
        def _():
            arrivals(i)

        @pl.when(i == 7 + lag)
        def _():
            send_y(5)

        if ready is not None:

            @pl.when(i == lag)
            def _():
                ready()

        @pl.when(i >= lag)
        def _():
            one_chip(i - lag)

        return carried

    lax.fori_loop(0, 8 + lag, step, 0)
    finish_chip(7)
    for j in (3, 1, 0):
        send_y(2 * j + 1)
    later = list(then) + [lambda: None] * 4
    later[0]()

    def z_sum(target, direction, k, device=None):
        slot = (direction + 1) // 2
        return remote(
            to_z.at[target, pieces[k]],
            from_z.at[slot, target, pieces[k]],
            w_out.at[target, k],
            w_in.at[slot, target, k],
            at.at_z(at.z + direction) if device is None else device,
        )

    def z_arrival(target, direction, k):
        return z_sum(target, direction, k, at.at_z(lax.rem(at.z - direction + 4, 4)))

    def direction_of(j):
        return at.step_first if j == 1 else at.toward

    for place, j in enumerate((2, 3, 1)):
        target, direction = at.source(j), direction_of(j)
        for k, piece in enumerate(pieces):
            y_sum(2 * j + 1, k).wait_recv()
            mine = chip_sum[2 * j, piece].astype(jnp.float32) + from_y[j, piece].astype(
                jnp.float32
            )

            @pl.when(at.outer)
            def _():
                to_z[target, piece] = mine.astype(jnp.bfloat16)

            @pl.when(at.inner)
            def _():
                z_arrival(target, direction, k).wait_recv()
                ahead = from_z[(direction + 1) // 2, target, piece].astype(jnp.float32)
                to_z[target, piece] = (mine + ahead).astype(jnp.bfloat16)

            z_sum(target, direction, k).start()
        later[1 + place]()

    def finish():
        for k, piece in enumerate(pieces):
            y_sum(1, k).wait_recv()
            part_own[piece] = chip_sum[0, piece].astype(jnp.float32) + from_y[0, piece].astype(
                jnp.float32
            )
            z_arrival(at.z, -at.toward, k).wait_recv()
            part_own[piece] += from_z[(1 - at.toward) // 2, at.z, piece].astype(jnp.float32)

            @pl.when(at.inner)
            def _():
                z_arrival(at.z, at.toward, k).wait_recv()
                part_own[piece] += from_z[(1 + at.toward) // 2, at.z, piece].astype(jnp.float32)

        return part_own[...]

    def drain():
        own_z_toward().wait_send()

        @pl.when(at.inner)
        def _():
            own_z_away().wait_send()
            for j in (1, 2, 3):
                from_z_block(at.source(j)).wait_send()

        def drain_chip(i, carried):
            pass_sib(chip_of(i)).wait_send()
            sib_sum(i).wait_send()

            @pl.when(lax.rem(i, 2) == 1)
            def _():
                pass_y(at.source(i // 2)).wait_send()
                for k in range(4):
                    y_sum(i, k).wait_send()

            return carried

        lax.fori_loop(0, 8, drain_chip, 0)
        for j in (1, 2, 3):
            for k in range(4):
                z_sum(at.source(j), direction_of(j), k).wait_send()

    return finish, drain


gain_edges = (0, 1152, 1408, 1664, 2816, 3968, 5120)
score_step = 0.0625
hidden_score = -1e30


def shape_spec(shape, dtype):
    return jax.ShapeDtypeStruct(shape, dtype)


def rms_scale(values):
    return lax.rsqrt(jnp.mean(values * values, axis=-1, keepdims=True) + norm_eps)


def norm_back(values, gain, upstream):
    scale = rms_scale(values)
    weighted = upstream * gain
    inner = jnp.mean(weighted * values, axis=-1, keepdims=True)
    back = scale * weighted - values * (scale * scale * scale * inner)
    return back, jnp.sum(upstream * values * scale, axis=0, keepdims=True)


def pick(offset):
    row = lax.broadcasted_iota(jnp.int32, (256, 512), 0)
    column = lax.broadcasted_iota(jnp.int32, (256, 512), 1)
    wanted = row // 8 * 16 + lax.rem(row, 8) + offset
    return jnp.where(column == wanted, 1.0, 0.0).astype(jnp.bfloat16)


def rows_of_all(w_all, low, count):
    return jnp.concatenate(
        [w_all[d // 2, d % 2, low : low + count] for d in range(32)], axis=0
    )


def rows_of_head(w_all, head, low, count):
    return jnp.concatenate(
        [w_all[d // 2, d % 2, low : low + count] for d in range(8 * head, 8 * head + 8)], axis=0
    )


class GainGather:
    def __init__(self, at, held, sems):
        self.at, self.held = at, held
        self.out, self.inc, self.z_out, self.z_in = sems
        x = at.s // 2
        self.spans = (
            (at.f * 4 + at.s, 1, at.sibling),
            (at.f * 4 + 2 * x, 2, at.over_x),
            (at.f * 4, 4, at.over_y),
        )

    def stage(self, k):
        first, count, partner = self.spans[k]
        span = self.held.at[pl.ds(first, count)]
        return remote(span, span, self.out.at[k], self.inc.at[k], partner)

    def last(self, src, j, device):
        span = self.held.at[pl.ds(src * 8, 8)]
        return remote(span, span, self.z_out.at[j], self.z_in.at[src], device)

    def send(self, k):
        at = self.at
        if k < 3:
            self.stage(k).start()
        else:
            for j in (1, 2, 3):
                self.last(at.z, j, at.at_z(at.source(j))).start()

    def take(self, k):
        at = self.at
        if k < 3:
            self.stage(k).wait_recv()
        else:
            for j in (1, 2, 3):
                self.last(at.source(j), j, at.at_z(at.source(j))).wait_recv()

    def drain(self):
        at = self.at
        for k in range(3):
            self.stage(k).wait_send()
        for j in (1, 2, 3):
            self.last(at.z, j, at.at_z(at.source(j))).wait_send()


class WeightGather:
    def __init__(self, at, w_all, sems, part, low, high):
        self.at, self.w_all, self.part = at, w_all, part
        (
            self.x_out,
            self.x_in,
            self.first_out,
            self.first_in,
            self.z_own,
            self.z_next,
            self.z_in,
            self.y_out,
            self.y_in,
            self.s_out,
            self.s_in,
        ) = sems
        self.rows = pl.ds(low, high - low)
        self.x = at.s // 2

    def one(self, y, x, outgoing, incoming, device):
        span = self.w_all.at[(self.at.z * 2 + y) * 2 + x, self.at.core, self.rows]
        return remote(span, span, outgoing, incoming, device)

    def pair(self, z, y, outgoing, incoming, device):
        span = self.w_all.at[pl.ds((z * 2 + y) * 2, 2), self.at.core, self.rows]
        return remote(span, span, outgoing, incoming, device)

    def x_copy(self, x):
        p, at = self.part, self.at
        return self.one(at.y, x, self.x_out.at[p], self.x_in.at[p], at.over_x)

    def y_first(self, y, x):
        p, at = self.part, self.at
        return self.one(y, x, self.first_out.at[p, x], self.first_in.at[p, x], at.over_y)

    def own(self, step, slot):
        p, at = self.part, self.at
        return self.pair(
            at.z, at.y, self.z_own.at[p, slot], self.z_in.at[p, at.z], at.at_z(at.z + step)
        )

    def passed(self, src, device):
        p = self.part
        return self.pair(src, self.at.y, self.z_next.at[p, src], self.z_in.at[p, src], device)

    def y_pair(self, src, y):
        p = self.part
        return self.pair(src, y, self.y_out.at[p, src], self.y_in.at[p, src], self.at.over_y)

    def sib(self, src):
        span = self.w_all.at[pl.ds(src * 4, 4), self.at.core, self.rows]
        p = self.part
        return remote(span, span, self.s_out.at[p, src], self.s_in.at[p, src], self.at.sibling)

    def begin(self):
        self.x_copy(self.x).start()

    def spread(self):
        at = self.at
        self.y_first(at.y, self.x).start()
        self.x_copy(1 - self.x).wait_recv()
        self.own(at.toward, 0).start()

        @pl.when(at.inner)
        def _():
            self.own(-at.toward, 1).start()

        self.y_first(at.y, 1 - self.x).start()

    def take(self, j):
        at = self.at
        src = at.source(j)
        self.passed(src, at.at_z(src)).wait_recv()

        @pl.when(at.inner)
        def _():
            self.passed(src, at.at_z(at.z + (at.toward if j == 1 else -at.toward))).start()

        self.y_pair(src, at.y).start()

    def close(self, j):
        src = self.at.source(j)
        if j == 0:
            for x in (0, 1):
                self.y_first(1 - self.at.y, x).wait_recv()
        else:
            self.y_pair(src, 1 - self.at.y).wait_recv()
        self.sib(src).start()

    def walk(self, between=()):
        at = self.at
        extra = list(between) + [lambda: None] * 3
        self.take(1)

        @pl.when(at.inner)
        def _():
            self.take(2)

        extra[0]()
        self.close(0)

        @pl.when(at.inner)
        def _():
            self.take(3)

        @pl.when(at.outer)
        def _():
            self.take(2)

        extra[1]()
        self.close(1)

        @pl.when(at.outer)
        def _():
            self.take(3)

        extra[2]()
        self.close(2)
        self.close(3)

    def settle(self):
        for j in range(4):
            self.sib(self.at.source(j)).wait_recv()

    def drain(self):
        at = self.at
        self.x_copy(self.x).wait_send()
        for x in (0, 1):
            self.y_first(at.y, x).wait_send()
        self.own(at.toward, 0).wait_send()

        @pl.when(at.inner)
        def _():
            self.own(-at.toward, 1).wait_send()
            for j in (1, 2, 3):
                self.passed(at.source(j), at.at_z(at.source(j))).wait_send()

        for j in range(4):
            src = at.source(j)
            if j > 0:
                self.y_pair(src, at.y).wait_send()
            self.sib(src).wait_send()


def gather_weight_sems():
    return [DMA((2,)), DMA((2,))] + [DMA((2, 2))] * 3 + [DMA((2, 4))] * 6


def gain_sems():
    return [DMA((3,)), DMA((3,)), DMA((4,)), DMA((4,))]


def turn(values, cos, sin):
    a, b = values[:, :128], values[:, 128:]
    return jnp.concatenate([a * cos - b * sin, b * cos + a * sin], axis=1)


def turn_back(values, cos, sin):
    a, b = values[:, :128], values[:, 128:]
    return jnp.concatenate([a * cos + b * sin, b * cos - a * sin], axis=1)


class WeightReturn:
    def __init__(self, at, held, bufs, sems, part, low, middle, high):
        self.at, self.held, self.part = at, held, part
        self.sib_in, self.xh_in, self.yh_in, self.xf_in, self.yf_in, self.z_in = bufs
        (
            self.so,
            self.si,
            self.xho,
            self.xhi,
            self.yho,
            self.yhi,
            self.xfo,
            self.xfi,
            self.yfo,
            self.yfi,
            self.zo,
            self.zi,
        ) = sems
        self.low, self.middle, self.high = low, middle, high
        self.x = at.s // 2
        self.rows = pl.ds(low, high - low)
        self.top = pl.ds(low, middle - low)
        self.bottom = pl.ds(middle, high - middle)
        self.by_x, self.by_y = middle > low, high > middle

    def mine(self, z, y, x, rows):
        return self.held.at[self.at.core, z * 2 + y, x, rows]

    def sib(self, z):
        pair = pl.ds(z * 2, 2)
        p = self.part
        return remote(
            self.held.at[1 - self.at.core, pair, :, self.rows],
            self.sib_in.at[pair, :, self.rows],
            self.so.at[p, z],
            self.si.at[p, z],
            self.at.sibling,
        )

    def x_half(self, z):
        p = self.part
        source = self.mine(z, 1 - self.at.y, 1 - self.x, self.top)
        return remote(
            source, self.xh_in.at[z, self.top], self.xho.at[p, z], self.xhi.at[p, z], self.at.over_x
        )

    def y_half(self, z):
        p = self.part
        source = self.mine(z, 1 - self.at.y, 1 - self.x, self.bottom)
        return remote(
            source,
            self.yh_in.at[z, self.bottom],
            self.yho.at[p, z],
            self.yhi.at[p, z],
            self.at.over_y,
        )

    def x_full(self, z):
        p = self.part
        source = self.mine(z, self.at.y, 1 - self.x, self.rows)
        return remote(
            source,
            self.xf_in.at[z, self.rows],
            self.xfo.at[p, z],
            self.xfi.at[p, z],
            self.at.over_x,
        )

    def y_full(self, z):
        p = self.part
        source = self.mine(z, 1 - self.at.y, self.x, self.rows)
        return remote(
            source,
            self.yf_in.at[z, self.rows],
            self.yfo.at[p, z],
            self.yfi.at[p, z],
            self.at.over_y,
        )

    def z_part(self, z):
        p = self.part
        source = self.mine(z, self.at.y, self.x, self.rows)
        return remote(
            source,
            self.z_in.at[self.at.z, self.rows],
            self.zo.at[p, z],
            self.zi.at[p, self.at.z],
            self.at.at_z(z),
        )

    def z_arrival(self, z):
        p = self.part
        source = self.mine(z, self.at.y, self.x, self.rows)
        return remote(
            source,
            self.z_in.at[z, self.rows],
            self.zo.at[p, z],
            self.zi.at[p, z],
            self.at.at_z(z),
        )

    def add(self, z, y, x, rows, more):
        core, f = self.at.core, z * 2 + y
        self.held[core, f, x, rows] = (
            self.held[core, f, x, rows].astype(jnp.float32) + more.astype(jnp.float32)
        ).astype(jnp.bfloat16)

    def send_sib(self):
        for j in (3, 2, 1, 0):
            self.sib(self.at.source(j)).start()

    def merge(self):
        for j in (3, 2, 1, 0):
            z = self.at.source(j)
            self.sib(z).wait_recv()
            for y in (0, 1):
                for x in (0, 1):
                    self.add(z, y, x, self.rows, self.sib_in[z * 2 + y, x, self.rows])
            (self.x_half if self.by_x else self.y_full)(z).start()
            (self.y_half if self.by_y else self.x_full)(z).start()

    def pair_up(self):
        at = self.at
        for j in (3, 2, 1, 0):
            z = at.source(j)
            if self.by_x:
                self.x_half(z).wait_recv()
                self.add(z, 1 - at.y, self.x, self.top, self.xh_in[z, self.top])
                self.y_full(z).start()
            if self.by_y:
                self.y_half(z).wait_recv()
                self.add(z, at.y, 1 - self.x, self.bottom, self.yh_in[z, self.bottom])
                self.x_full(z).start()

    def collect(self):
        at = self.at
        for j in (3, 2, 1, 0):
            z = at.source(j)
            self.y_full(z).wait_recv()
            self.x_full(z).wait_recv()
            more = self.yf_in[z, self.rows].astype(jnp.float32) + self.xf_in[
                z, self.rows
            ].astype(jnp.float32)
            self.add(z, at.y, self.x, self.rows, more)
            if j > 0:
                self.z_part(z).start()

    def total(self):
        at = self.at
        value = self.held[at.core, at.f, self.x, self.rows].astype(jnp.float32)
        for j in (3, 2, 1):
            z = at.source(j)
            self.z_arrival(z).wait_recv()
            value = value + self.z_in[z, self.rows].astype(jnp.float32)
        return value

    def drain(self):
        for j in range(4):
            z = self.at.source(j)
            for copy in (self.sib, self.x_full, self.y_full):
                copy(z).wait_send()
            if self.by_x:
                self.x_half(z).wait_send()
            if self.by_y:
                self.y_half(z).wait_send()
            if j > 0:
                self.z_part(z).wait_send()


class GainSum:
    def __init__(self, at, row, outgoing, incoming, sems):
        self.at, self.row, self.outgoing, self.incoming = at, row, outgoing, incoming
        self.out, self.inc = sems
        self.partners = (at.sibling, at.over_x, at.over_y)

    def stage(self, k):
        return remote(
            self.outgoing.at[k],
            self.incoming.at[k],
            self.out.at[k],
            self.inc.at[k],
            self.partners[k],
        )

    def last(self, src, j, device):
        return remote(
            self.outgoing.at[3],
            self.incoming.at[3 + src],
            self.out.at[2 + j],
            self.inc.at[3 + src],
            device,
        )

    def send(self, k):
        self.outgoing[k] = self.row[...]
        if k < 3:
            self.stage(k).start()
        else:
            for j in (1, 2, 3):
                self.last(self.at.z, j, self.at.at_z(self.at.source(j))).start()

    def take(self, k):
        if k < 3:
            self.stage(k).wait_recv()
            self.row[...] += self.incoming[k]
        else:
            for j in (1, 2, 3):
                src = self.at.source(j)
                self.last(src, j, self.at.at_z(src)).wait_recv()
                self.row[...] += self.incoming[3 + src]

    def drain(self):
        for k in range(3):
            self.stage(k).wait_send()
        for j in (1, 2, 3):
            self.last(self.at.z, j, self.at.at_z(self.at.source(j))).wait_send()


class Refs:
    def __init__(self, names, refs):
        for name, ref in zip(names, refs):
            setattr(self, name, ref)


def columns_of(head):
    return slice(256 * head, 256 * head + 256)


def front_phase(at, r, sems):
    core, s = at.core, at.s
    gathered = GainGather(at, r.gain_all, sems[:4])
    w_sems = sems[4:15]
    kv_out, kv_in, x_out, x_in = sems[15:19]
    w_all, kv_all = r.w_all, r.kv_all
    early = WeightGather(at, w_all, w_sems, 0, 0, 48)
    late = WeightGather(at, w_all, w_sems, 1, 48, 80)
    chip = at.f * 2 + s // 2
    w_all[chip, core, 0:32] = r.own_q[...]
    w_all[chip, core, 32:48] = jnp.concatenate(
        [r.own_k[...].astype(jnp.float32), r.own_v[...].astype(jnp.float32)], axis=0
    ).astype(jnp.bfloat16)
    w_all[chip, core, 48:80] = r.own_o[...]
    r.gain_all[at.f * 4 + s] = r.gain_row[...]
    greet(
        [at.sibling, at.over_x, at.over_y]
        + [at.at_z(lax.rem(at.z + step, 4)) for step in (1, 2, 3)]
    )
    def x_weight(k):
        ref = (r.own_gate, r.own_up, r.own_down)[k]
        return remote(ref, r.peer_w.at[k], x_out.at[k], x_in.at[k], at.over_x)

    def gain_step(k):
        def step():
            gathered.take(k)
            if k < 3:
                gathered.send(k + 1)

        return step

    gathered.send(0)
    early.begin()
    late.begin()
    gain_step(0)()
    early.spread()
    x_weight(0).start()
    x_weight(1).start()
    gain_step(1)()
    early.walk((gain_step(2), gain_step(3), late.spread))
    placed = r.gain_all[...].reshape(32, 256)
    pieces = []
    for m in range(8):
        for k in range(5):
            piece = None
            if k < 4:
                piece = placed[4 * m + k : 4 * m + k + 1, :128]
            if k > 0:
                other = placed[4 * m + k - 1 : 4 * m + k, 128:]
                piece = other if piece is None else piece + other
            pieces.append(piece)
    r.gains[...] = jnp.concatenate(pieces, axis=1)
    gain = gain_parts(r)
    residual = r.tokens[...].astype(jnp.float32)
    r.normed[...] = (residual * rms_scale(residual) * gain[0]).astype(jnp.bfloat16)
    early.settle()
    normed = r.normed[...]
    cos, sin = r.cos[...], r.sin[...]
    mixed_rows = rows_of_all(w_all, 32, 16)
    r.wk[...] = nn(pick(0), mixed_rows).astype(jnp.bfloat16)
    r.wv[...] = nn(pick(8), mixed_rows).astype(jnp.bfloat16)
    k_raw = nt(normed, r.wk[...])
    r.k_raw[...] = k_raw
    key = turn(k_raw * rms_scale(k_raw) * gain[2], cos, sin)
    kv_all[s, :, :256] = key.astype(jnp.bfloat16)
    kv_all[s, :, 256:] = nt(normed, r.wv[...]).astype(jnp.bfloat16)

    def kv_copy(which, slot, device):
        return remote(kv_all.at[slot], kv_all.at[slot], kv_out.at[which], kv_in.at[which], device)

    peer_slot = lax.rem(s + 2, 4)
    kv_copy(0, s, at.over_x).start()
    kv_copy(1, s, at.sibling).start()

    def one_query(head):
        q_raw = nt(normed, rows_of_head(w_all, head, 0, 32))
        r.q_raw[:, columns_of(head)] = q_raw
        query = turn(q_raw * rms_scale(q_raw) * gain[1], cos, sin)
        r.query[:, columns_of(head)] = query.astype(jnp.bfloat16)

    def pass_kv():
        one_query(0)
        kv_copy(0, peer_slot, at.over_x).wait_recv()
        kv_copy(2, peer_slot, at.sibling).start()
        x_weight(2).start()
        one_query(1)

    late.walk((pass_kv, lambda: one_query(2), lambda: one_query(3)))
    other = s + 1 - 2 * core
    kv_copy(1, other, at.sibling).wait_recv()
    kv_copy(2, lax.rem(other + 2, 4), at.sibling).wait_recv()
    keys, values = kv_parts(r)
    key_place = lax.broadcasted_iota(jnp.int32, (128, 512), 1)
    query_place = lax.broadcasted_iota(jnp.int32, (128, 512), 0) + s * 128
    allowed = (key_place >= r.doc[...]) & (key_place <= query_place)
    for head in range(4):
        raw = nt(r.query[:, columns_of(head)], keys) * score_step
        scores = jnp.where(allowed, raw, hidden_score)
        weights = jnp.exp(scores - jnp.max(scores, axis=1, keepdims=True))
        prob = weights / jnp.sum(weights, axis=1, keepdims=True)
        r.prob[head] = prob
        mixed = nn(prob.astype(jnp.bfloat16), values).astype(jnp.bfloat16)
        r.mixed[:, columns_of(head)] = mixed
    late.settle()
    attn = nn(r.mixed[...], rows_of_all(w_all, 48, 32))
    r.attn[...] = attn
    middle = r.tokens[...].astype(jnp.float32) + attn * rms_scale(attn) * gain[3]
    r.middle[...] = middle
    normed_ffn = (middle * rms_scale(middle) * gain[4]).astype(jnp.bfloat16)

    def drain():
        gathered.drain()
        early.drain()
        late.drain()
        kv_copy(0, s, at.over_x).wait_send()
        kv_copy(1, s, at.sibling).wait_send()
        kv_copy(2, peer_slot, at.sibling).wait_send()

    return normed_ffn, x_weight, drain


def gain_parts(r):
    return [r.gains[:, a:b] for a, b in zip(gain_edges[:-1], gain_edges[1:])]


def kv_parts(r):
    return r.kv_all[...].reshape(512, 512)[:, :256], r.kv_all[...].reshape(512, 512)[:, 256:]


def ffn_phase(at, r, sems, normed_ffn, x_weight):
    core = at.core
    fwd_gather, fwd_sum = sems[:7], sems[7:13]
    bwd_gather, bwd_sum = sems[13:20], sems[20:26]
    x_out, x_in = sems[26:28]
    sum_bufs = (r.to_sib, r.from_sib, r.chip_sum, r.from_y, r.to_z, r.from_z)
    normed_all, grad_all = r.held.at[0], r.held.at[1]
    gates = (r.own_gate, r.peer_w.at[0])
    ups = (r.own_up, r.peer_w.at[1])
    downs = (r.own_down, r.peer_w.at[2])
    r.held[0, at.f, core] = normed_ffn

    def rows_of(which, chip):
        return jnp.concatenate([r.held[which, chip, core], r.held[which, chip, 1 - core]], axis=0)

    def weights_here():
        for k in range(3):
            x_weight(k).wait()

    def forward(chip):
        rows = rows_of(0, chip)
        total = None
        for half in (0, 1):
            gate = nt(rows, gates[half][...])
            up = nt(rows, ups[half][...])
            r.gate_keep[half, chip] = gate.astype(jnp.bfloat16)
            r.up_keep[half, chip] = up.astype(jnp.bfloat16)
            bend = jnp.tanh(gelu_c * (gate + 0.044715 * gate * gate * gate))
            hidden = (0.5 * gate * (1.0 + bend) * up).astype(jnp.bfloat16)
            r.hidden_keep[half, chip] = hidden
            part = nn(hidden, downs[half][...])
            total = part if total is None else total + part
        return total[:128], total[128:]

    finish, drain = exchange_pass(
        at, normed_all, fwd_gather, fwd_sum, sum_bufs, r.part_own, forward, 0, weights_here
    )
    ffn_raw = finish()
    drain()
    gain = gain_parts(r)[5]
    scale = rms_scale(ffn_raw)
    r.result[...] = (r.middle[...] + ffn_raw * scale * gain).astype(jnp.bfloat16)
    ffn_grad, gain_grad = norm_back(ffn_raw, gain, r.cotangent[...].astype(jnp.float32))
    r.gain_sum[:, gain_edges[5] : gain_edges[6]] = gain_grad
    r.held[1, at.f, core] = ffn_grad.astype(jnp.bfloat16)
    own_grads = (r.gate_grad, r.up_grad, r.down_grad)

    def backward(chip):
        rows = rows_of(1, chip)
        total = None
        for half in (0, 1):
            dhidden = nt(rows, downs[half][...])
            gate = r.gate_keep[half, chip].astype(jnp.float32)
            up = r.up_keep[half, chip].astype(jnp.float32)
            square = gate * gate
            bend = jnp.tanh(gelu_c * (gate + 0.044715 * square * gate))
            unit = 0.5 * gate * (1.0 + bend)
            slope = 0.5 * (1.0 + bend) + 0.5 * gate * (1.0 - bend * bend) * (
                gelu_c * (1.0 + 3 * 0.044715 * square)
            )
            dgate = (dhidden * up * slope).astype(jnp.bfloat16)
            dup = (dhidden * unit).astype(jnp.bfloat16)
            part = nn(dgate, gates[half][...]) + nn(dup, ups[half][...])
            total = part if total is None else total + part
            r.gate_keep[half, chip] = dgate
            r.up_keep[half, chip] = dup
        return total[:128], total[128:]

    def x_copy(k):
        return remote(r.peer_w.at[k], r.from_x.at[k], x_out.at[k], x_in.at[k], at.over_x)

    kept = ((r.gate_keep, 0), (r.up_keep, 0), (r.hidden_keep, 1))

    def weight_grad(k, half):
        left, which = kept[k]
        total = None
        for chip in range(8):
            part = tn(left[half, chip], rows_of(which, chip))
            total = part if total is None else total + part
        return total

    def peers():
        for k in range(3):
            r.peer_w[k] = weight_grad(k, 1).astype(jnp.bfloat16)
            x_copy(k).start()

    def own(k):
        def step():
            own_grads[k][...] = weight_grad(k, 0)

        return step

    finish, drain = exchange_pass(
        at,
        grad_all,
        bwd_gather,
        bwd_sum,
        sum_bufs,
        r.part_own,
        backward,
        0,
        None,
        (peers, own(0), own(1), own(2)),
    )
    normed_grad = finish()
    drain()

    def complete():
        for k in range(3):
            x_copy(k).wait()
            own_grads[k][...] += r.from_x[k].astype(jnp.float32)

    return normed_grad, complete


def back_phase(at, r, sems, normed_grad, complete):
    core, s = at.core, at.s
    x = s // 2
    gain = gain_parts(r)
    cos, sin = r.cos[...], r.sin[...]
    bufs = (r.sib_in, r.half_in, r.half_in, r.xf_in, r.yf_in, r.zw_in)
    w_sems = sems[:12]
    kv_out, kv_in = sems[12:14]
    outer = WeightReturn(at, r.held, bufs, w_sems, 1, 48, 64, 80)
    inner = WeightReturn(at, r.held, bufs, w_sems, 0, 0, 16, 48)
    gain_total = GainSum(at, r.gain_sum, r.gain_out, r.gain_in, sems[14:16])

    def put_gain(k, value):
        r.gain_sum[:, gain_edges[k] : gain_edges[k + 1]] = value

    def put_rows(head, low, count, rows):
        split = rows.astype(jnp.bfloat16).reshape(4, 2, count, rows.shape[-1])
        for c in range(4):
            for k in (0, 1):
                r.held[k, 2 * head + c // 2, c % 2, low : low + count] = split[c, k]

    part, gain_grad = norm_back(r.middle[...], gain[4], normed_grad)
    put_gain(4, gain_grad)
    middle_grad = r.cotangent[...].astype(jnp.float32) + part
    r.middle[...] = middle_grad
    attn_grad, gain_grad = norm_back(r.attn[...], gain[3], middle_grad)
    put_gain(3, gain_grad)
    attn_grad = attn_grad.astype(jnp.bfloat16)
    for head in range(4):
        put_rows(head, 48, 32, tn(r.mixed[:, columns_of(head)], attn_grad))
    outer.send_sib()
    keys, values = kv_parts(r)
    for head in range(4):
        mixed_grad = nt(attn_grad, rows_of_head(r.w_all, head, 48, 32)).astype(jnp.bfloat16)
        prob = r.prob[head]
        prob_grad = nt(mixed_grad, values)
        delta = jnp.sum(prob * prob_grad, axis=1, keepdims=True)
        score_grad = (prob * (prob_grad - delta)).astype(jnp.bfloat16)
        key_part = tn(score_grad, r.query[:, columns_of(head)]) * score_step
        value_part = tn(prob.astype(jnp.bfloat16), mixed_grad)
        if head == 0:
            r.kv_sum[:, :256] = key_part
            r.kv_sum[:, 256:] = value_part
        else:
            r.kv_sum[:, :256] += key_part
            r.kv_sum[:, 256:] += value_part
        r.query_grad[:, columns_of(head)] = nn(score_grad, keys) * score_step
    r.kv_part[...] = r.kv_sum[...].astype(jnp.bfloat16).reshape(2, 2, 128, 512)
    kv_sib = remote(
        r.kv_part.at[:, 1 - core], r.kv_sib.at[...], kv_out.at[0], kv_in.at[0], at.sibling
    )
    kv_sib.start()
    outer.merge()
    kv_sib.wait_recv()
    r.kv_chip[...] = (
        r.kv_part[1 - x, core].astype(jnp.float32) + r.kv_sib[1 - x].astype(jnp.float32)
    ).astype(jnp.bfloat16)
    kv_x = remote(r.kv_chip, r.kv_far, kv_out.at[1], kv_in.at[1], at.over_x)
    kv_x.start()
    normed = r.normed[...]
    query_gain = None
    for head in range(4):
        turned = turn_back(r.query_grad[:, columns_of(head)], cos, sin)
        q_raw_grad, gain_grad = norm_back(r.q_raw[:, columns_of(head)], gain[1], turned)
        query_gain = gain_grad if query_gain is None else query_gain + gain_grad
        q_raw_grad = q_raw_grad.astype(jnp.bfloat16)
        r.query[:, columns_of(head)] = q_raw_grad
        put_rows(head, 0, 32, tn(q_raw_grad, normed))
    put_gain(1, query_gain)
    outer.pair_up()
    kv_x.wait_recv()
    kv_grad = (
        r.kv_part[x, core].astype(jnp.float32)
        + r.kv_sib[x].astype(jnp.float32)
        + r.kv_far[...].astype(jnp.float32)
    )
    k_raw_grad, gain_grad = norm_back(r.k_raw[...], gain[2], turn_back(kv_grad[:, :256], cos, sin))
    put_gain(2, gain_grad)
    k_raw_grad = k_raw_grad.astype(jnp.bfloat16)
    v_raw_grad = kv_grad[:, 256:].astype(jnp.bfloat16)
    woven = (nn(k_raw_grad, pick(0)) + nn(v_raw_grad, pick(8))).astype(jnp.bfloat16)
    for head in range(4):
        put_rows(head, 32, 16, tn(woven[:, 128 * head : 128 * head + 128], normed))
    inner.send_sib()
    normed_grad = nn(k_raw_grad, r.wk[...]) + nn(v_raw_grad, r.wv[...])
    for head in range(4):
        normed_grad += nn(r.query[:, columns_of(head)], rows_of_head(r.w_all, head, 0, 32))
    part, gain_grad = norm_back(r.tokens[...].astype(jnp.float32), gain[0], normed_grad)
    put_gain(0, gain_grad)
    gain_total.send(0)
    r.token_grad[...] = r.middle[...] + part
    inner.merge()
    gain_total.take(0)
    gain_total.send(1)
    outer.collect()
    inner.pair_up()
    gain_total.take(1)
    gain_total.send(2)
    inner.collect()
    gain_total.take(2)
    gain_total.send(3)
    r.o_grad[...] = outer.total()
    complete()
    total = inner.total()
    r.q_grad[...] = total[:32]
    r.k_grad[...] = total[32:40]
    r.v_grad[...] = total[40:48]
    gain_total.take(3)
    device = at.f * 4 + s
    first = pl.multiple_of(device * 160 // 128 * 128, 128)
    r.gain_grad[...] = pltpu.roll(
        r.gain_sum[:, pl.ds(first, 256)], 256 - lax.rem(device, 4) * 32, 1
    )
    outer.drain()
    inner.drain()
    gain_total.drain()
    kv_sib.wait_send()
    kv_x.wait_send()


def layer_call(values):
    b16, f32 = jnp.bfloat16, jnp.float32
    rows, width = values["tokens"].shape
    units = values["own_gate"].shape[0]
    outs = {
        "result": ((rows, width), b16),
        "token_grad": ((rows, width), f32),
        "gain_grad": ((1, 256), f32),
        "q_grad": ((32, width), f32),
        "k_grad": ((8, width), f32),
        "v_grad": ((8, width), f32),
        "o_grad": ((32, width), f32),
        "gate_grad": ((units, width), f32),
        "up_grad": ((units, width), f32),
        "down_grad": ((units, width), f32),
    }
    scratch = {
        "gain_sum": ((1, 5120), f32),
        "w_all": ((16, 2, 80, width), b16),
        "gain_all": ((32, 1, 256), f32),
        "gains": ((1, 5120), f32),
        "wk": ((256, width), b16),
        "wv": ((256, width), b16),
        "normed": ((rows, width), b16),
        "k_raw": ((rows, 256), f32),
        "q_raw": ((rows, 1024), f32),
        "query": ((rows, 1024), b16),
        "query_grad": ((rows, 1024), f32),
        "kv_all": ((4, rows, 512), b16),
        "prob": ((4, rows, 512), f32),
        "mixed": ((rows, 1024), b16),
        "attn": ((rows, width), f32),
        "middle": ((rows, width), f32),
        "peer_w": ((3, units, width), b16),
        "held": ((2, 8, 2, rows, width), b16),
        "gate_keep": ((2, 8, 2 * rows, units), b16),
        "up_keep": ((2, 8, 2 * rows, units), b16),
        "hidden_keep": ((2, 8, 2 * rows, units), b16),
        "part_own": ((rows, width), f32),
        "to_sib": ((8, rows, width), b16),
        "from_sib": ((8, rows, width), b16),
        "chip_sum": ((8, rows, width), b16),
        "from_y": ((4, rows, width), b16),
        "to_z": ((4, rows, width), b16),
        "from_z": ((2, 4, rows, width), b16),
        "from_x": ((3, units, width), b16),
        "sib_in": ((8, 2, 80, width), b16),
        "half_in": ((4, 80, width), b16),
        "xf_in": ((4, 80, width), b16),
        "yf_in": ((4, 80, width), b16),
        "zw_in": ((4, 80, width), b16),
        "kv_sum": ((4 * rows, 512), f32),
        "kv_part": ((2, 2, rows, 512), b16),
        "kv_sib": ((2, rows, 512), b16),
        "kv_chip": ((rows, 512), b16),
        "kv_far": ((rows, 512), b16),
        "gain_out": ((4, 1, 5120), f32),
        "gain_in": ((7, 1, 5120), f32),
    }
    gather_sems = [DMA((2,)), DMA((4,)), DMA((4,)), DMA((4,)), DMA((4,)), DMA((8,)), DMA((8,))]
    sum_sems = [DMA((8,)), DMA((8,)), DMA((4, 4)), DMA((4, 4)), DMA((4, 4)), DMA((2, 4, 4))]
    front_sems = gain_sems() + gather_weight_sems() + [DMA((3,))] * 4
    ffn_sems = (gather_sems + sum_sems) * 2 + [DMA((3,)), DMA((3,))]
    back_sems = [DMA((2, 4))] * 12 + [DMA((2,)), DMA((2,)), DMA((6,)), DMA((7,))]
    sems = front_sems + ffn_sems + back_sems
    names = tuple(values) + tuple(outs) + tuple(scratch)

    def kernel(*refs):
        at = Place()
        r = Refs(names, refs)
        held_sems = refs[len(names) :]
        first, second = len(front_sems), len(front_sems) + len(ffn_sems)
        normed_ffn, x_weight, drain = front_phase(at, r, held_sems[:first])
        normed_grad, complete = ffn_phase(at, r, held_sems[first:second], normed_ffn, x_weight)
        back_phase(at, r, held_sems[second:], normed_grad, complete)
        drain()

    vmem = pl.BlockSpec(memory_space=pltpu.VMEM)
    out = pl.pallas_call(
        kernel,
        out_shape=tuple(jax.ShapeDtypeStruct(*spec) for spec in outs.values()),
        in_specs=[vmem] * len(values),
        out_specs=tuple([vmem] * len(outs)),
        scratch_shapes=[pltpu.VMEM(*spec) for spec in scratch.values()] + sems,
        compiler_params=pltpu.CompilerParams(
            collective_id=1, has_side_effects=True, vmem_limit_bytes=63 << 20
        ),
        name="layer",
    )(*values.values())
    return dict(zip(outs, out))


def settle_kernel(count, *refs):
    ins, outs, held, sems = refs[:count], refs[count : 2 * count], refs[2 * count : -1], refs[-1]
    loads = [pltpu.make_async_copy(ins[k], held[k], sems.at[0, k]) for k in range(count)]
    stores = [pltpu.make_async_copy(held[k], outs[k], sems.at[1, k]) for k in range(count)]
    for copy in loads:
        copy.start()
    for load, store in zip(loads, stores):
        load.wait()
        store.start()
    for copy in stores:
        copy.wait()


def settle(arrays):
    anywhere = pl.BlockSpec(memory_space=pl.ANY)
    return pl.pallas_call(
        partial(settle_kernel, len(arrays)),
        out_shape=tuple(jax.ShapeDtypeStruct(a.shape, a.dtype) for a in arrays),
        in_specs=[anywhere] * len(arrays),
        out_specs=tuple([anywhere] * len(arrays)),
        scratch_shapes=[pltpu.VMEM(a.shape, a.dtype) for a in arrays] + [DMA((2, len(arrays)))],
        name="settle",
    )(*arrays)


def one_kernel(
    tokens, doc_start, gains, w_query, w_key, w_value, w_out, w_gate, w_up, w_down, cotangent
):
    rows = tokens.shape[0]
    device = lax.axis_index("fsdp") * lax.axis_size("seq") + lax.axis_index("seq")
    share = gains.shape[0]
    gain_row = lax.dynamic_update_slice(
        jnp.zeros((1, 256), jnp.float32),
        gains[None].astype(jnp.float32),
        (0, lax.rem(device, 4) * 32),
    )
    places = lax.axis_index("seq") * rows + jnp.arange(rows, dtype=jnp.int32) - doc_start
    cos, sin = rope_tables(places, 256)
    out = layer_call(
        {
            "tokens": tokens,
            "doc": doc_start[:, None],
            "gain_row": gain_row,
            "own_q": w_query.T,
            "own_k": w_key.T,
            "own_v": w_value.T,
            "own_o": w_out,
            "own_gate": w_gate.T,
            "own_up": w_up.T,
            "own_down": w_down,
            "cos": cos[:, 0],
            "sin": sin[:, 0],
            "cotangent": cotangent,
        }
    )
    names = ("result", "token_grad", "gain_grad", "q_grad", "k_grad", "v_grad", "o_grad")
    names += ("gate_grad", "up_grad", "down_grad")
    out = dict(zip(names, settle([out[name] for name in names])))
    return (
        out["result"],
        out["token_grad"],
        out["gain_grad"][0, :share],
        out["q_grad"].T,
        out["k_grad"].T,
        out["v_grad"].T,
        out["o_grad"],
        out["gate_grad"].T,
        out["up_grad"].T,
        out["down_grad"],
    )


def solution(mesh):
    in_specs = (
        P(("fsdp", "seq"), None),
        P(("fsdp", "seq")),
        P(("fsdp", "seq")),
        P(None, ("fsdp", "seq")),
        P(None, ("fsdp", "seq")),
        P(None, ("fsdp", "seq")),
        P(("fsdp", "seq"), None),
        P(None, ("fsdp", "seq")),
        P(None, ("fsdp", "seq")),
        P(("fsdp", "seq"), None),
        P(("fsdp", "seq"), None),
    )
    out_specs = (
        P(("fsdp", "seq"), None),
        P(("fsdp", "seq"), None),
        P(("fsdp", "seq")),
        P(None, ("fsdp", "seq")),
        P(None, ("fsdp", "seq")),
        P(None, ("fsdp", "seq")),
        P(("fsdp", "seq"), None),
        P(None, ("fsdp", "seq")),
        P(None, ("fsdp", "seq")),
        P(("fsdp", "seq"), None),
    )
    body = one_kernel if dict(mesh.shape) == {"fsdp": 8, "seq": 4} else local
    return jax.shard_map(body, mesh=mesh, in_specs=in_specs, out_specs=out_specs, check_vma=False)
```

```python
from functools import partial

import jax
import jax.numpy as jnp
from jax import lax
from jax.experimental import pallas as pl
from jax.experimental.pallas import tpu as pltpu
from jax.sharding import PartitionSpec as P

norm_eps = 1e-06
rope_base = 1000000.0
score_scale = 0.0625
masked_value = -1e30


def product(former, latter):
    return jnp.dot(former, latter, preferred_element_type=jnp.float32)


def inner_rows(former, latter):
    return lax.dot_general(
        former, latter, (((0,), (0,)), ((), ())), preferred_element_type=jnp.float32
    )


def outer_rows(former, latter):
    return lax.dot_general(
        former, latter, (((1,), (1,)), ((), ())), preferred_element_type=jnp.float32
    )


def scaled_norm(values, factor):
    return values * lax.rsqrt(jnp.mean(values * values, axis=-1, keepdims=True) + norm_eps) * factor


def rotate(values, cos_table, sin_table):
    half_width = values.shape[-1] // 2
    leading = values[..., :half_width]
    trailing = values[..., half_width:]
    return jnp.concatenate(
        [leading * cos_table - trailing * sin_table, trailing * cos_table + leading * sin_table],
        axis=-1,
    )


def head_norm(values, factor, cos_table, sin_table):
    return rotate(scaled_norm(values, factor), cos_table, sin_table)


def gated_unit(gate_in, up_in):
    return jax.nn.gelu(gate_in, approximate=True) * up_in


def rope_tables(places, rot_width):
    half_width = rot_width // 2
    frequency = rope_base ** (-2.0 * jnp.arange(half_width, dtype=jnp.float32) / rot_width)
    angles = places.astype(jnp.float32)[:, None] * frequency[None, :]
    return (jnp.cos(angles)[:, None, :], jnp.sin(angles)[:, None, :])


def masked_scores(queries, key_rows, bounds, offset):
    raw_scores = outer_rows(queries, key_rows) * score_scale
    query_place = offset + jnp.arange(queries.shape[0], dtype=jnp.int32)
    key_place = jnp.arange(key_rows.shape[0], dtype=jnp.int32)
    allowed = (key_place[None, :] >= bounds[:, None]) & (key_place[None, :] <= query_place[:, None])
    return jnp.where(allowed, raw_scores, masked_value)


def local(
    tokens, doc_start, gains, w_query, w_key, w_value, w_out, w_gate, w_up, w_down, cotangent
):
    tok_rows = tokens.shape[0]
    model_width = tokens.shape[1]
    run_index = lax.axis_index("seq")
    gains_all, query_w, key_w, value_w, out_w = (
        lax.all_gather(gains, ("fsdp", "seq"), axis=0, tiled=True),
        lax.all_gather(w_query, ("fsdp", "seq"), axis=1, tiled=True),
        lax.all_gather(w_key, ("fsdp", "seq"), axis=1, tiled=True),
        lax.all_gather(w_value, ("fsdp", "seq"), axis=1, tiled=True),
        lax.all_gather(w_out, ("fsdp", "seq"), axis=0, tiled=True),
    )
    gate_w, up_w, down_w = (
        lax.all_gather(w_gate, ("fsdp", "seq"), axis=1, tiled=True),
        lax.all_gather(w_up, ("fsdp", "seq"), axis=1, tiled=True),
        lax.all_gather(w_down, ("fsdp", "seq"), axis=0, tiled=True),
    )
    head_width = key_w.shape[1]
    head_count = query_w.shape[1] // head_width
    gain_values = gains_all.astype(jnp.float32)
    gain_pre = gain_values[:model_width]
    gain_query = gain_values[model_width : model_width + head_width]
    gain_key = gain_values[model_width + head_width : model_width + 2 * head_width]
    gain_post = gain_values[model_width + 2 * head_width : 2 * model_width + 2 * head_width]
    gain_pre_ffn = gain_values[2 * model_width + 2 * head_width : 3 * model_width + 2 * head_width]
    gain_post_ffn = gain_values[3 * model_width + 2 * head_width :]
    residual = tokens.astype(jnp.float32)
    normed, pre_pull = jax.vjp(scaled_norm, residual, gain_pre)
    normed_b = normed.astype(jnp.bfloat16)
    query_raw = product(normed_b, query_w).reshape(tok_rows, head_count, head_width)
    key_raw = product(normed_b, key_w).reshape(tok_rows, 1, head_width)
    value_b = product(normed_b, value_w).astype(jnp.bfloat16)
    places = run_index * tok_rows + jnp.arange(tok_rows, dtype=jnp.int32) - doc_start
    cos_table, sin_table = rope_tables(places, head_width)
    rope_norm = partial(head_norm, cos_table=cos_table, sin_table=sin_table)
    query_rot, query_pull = jax.vjp(rope_norm, query_raw, gain_query)
    key_rot, key_pull = jax.vjp(rope_norm, key_raw, gain_key)
    query_b = query_rot.reshape(tok_rows, head_count * head_width).astype(jnp.bfloat16)
    key_b = key_rot.reshape(tok_rows, head_width).astype(jnp.bfloat16)
    query_heads = lax.all_to_all(query_b, "seq", split_axis=1, concat_axis=0, tiled=True)
    key_rows, value_rows = (
        lax.all_gather(key_b, "seq", axis=0, tiled=True),
        lax.all_gather(value_b, "seq", axis=0, tiled=True),
    )
    starts = lax.all_gather(doc_start, "seq", axis=0, tiled=True)
    seq_tokens = key_rows.shape[0]
    block_rows = min(512, seq_tokens)
    block_count = seq_tokens // block_rows
    query_blocks = query_heads.reshape(block_count, block_rows, head_width)
    start_blocks = starts.reshape(block_count, block_rows)
    block_ids = jnp.arange(block_count, dtype=jnp.int32)

    def attend(block_item):
        queries, bounds, block_index = block_item
        scores = masked_scores(queries, key_rows, bounds, block_index * block_rows)
        row_max = jnp.max(scores, axis=1, keepdims=True)
        weights = jnp.exp(scores - row_max)
        row_total = jnp.sum(weights, axis=1, keepdims=True)
        probability = (weights / row_total).astype(jnp.bfloat16)
        mixed_block = product(probability, value_rows).astype(jnp.bfloat16)
        return (mixed_block, (row_max + jnp.log(row_total))[:, 0])

    mixed_blocks, lse_blocks = lax.map(attend, (query_blocks, start_blocks, block_ids))
    mixed_heads = mixed_blocks.reshape(seq_tokens, head_width)
    mixed_tokens = lax.all_to_all(mixed_heads, "seq", split_axis=0, concat_axis=1, tiled=True)
    attn_raw = product(mixed_tokens, out_w)
    attn_out, post_pull = jax.vjp(scaled_norm, attn_raw, gain_post)
    middle = residual + attn_out
    normed_ffn, pre_ffn_pull = jax.vjp(scaled_norm, middle, gain_pre_ffn)
    normed_ffn_b = normed_ffn.astype(jnp.bfloat16)
    gate_act = product(normed_ffn_b, gate_w)
    up_act = product(normed_ffn_b, up_w)
    hidden, glu_pull = jax.vjp(gated_unit, gate_act, up_act)
    hidden_b = hidden.astype(jnp.bfloat16)
    ffn_raw = product(hidden_b, down_w)
    ffn_out, post_ffn_pull = jax.vjp(scaled_norm, ffn_raw, gain_post_ffn)
    result = (middle + ffn_out).astype(jnp.bfloat16)
    gate_w, up_w, down_w = (
        lax.all_gather(w_gate, ("fsdp", "seq"), axis=1, tiled=True),
        lax.all_gather(w_up, ("fsdp", "seq"), axis=1, tiled=True),
        lax.all_gather(w_down, ("fsdp", "seq"), axis=0, tiled=True),
    )
    query_w, key_w, value_w, out_w = (
        lax.all_gather(w_query, ("fsdp", "seq"), axis=1, tiled=True),
        lax.all_gather(w_key, ("fsdp", "seq"), axis=1, tiled=True),
        lax.all_gather(w_value, ("fsdp", "seq"), axis=1, tiled=True),
        lax.all_gather(w_out, ("fsdp", "seq"), axis=0, tiled=True),
    )
    upstream = cotangent.astype(jnp.float32)
    ffn_grad, gain_post_ffn_grad = post_ffn_pull(upstream)
    ffn_grad_b = ffn_grad.astype(jnp.bfloat16)
    down_w_grad = inner_rows(hidden_b, ffn_grad_b)
    hidden_grad = outer_rows(ffn_grad_b, down_w)
    gate_grad, up_grad = glu_pull(hidden_grad)
    gate_grad_b = gate_grad.astype(jnp.bfloat16)
    up_grad_b = up_grad.astype(jnp.bfloat16)
    gate_w_grad_t = inner_rows(gate_grad_b, normed_ffn_b)
    up_w_grad_t = inner_rows(up_grad_b, normed_ffn_b)
    normed_ffn_grad = outer_rows(gate_grad_b, gate_w) + outer_rows(up_grad_b, up_w)
    middle_part, gain_pre_ffn_grad = pre_ffn_pull(normed_ffn_grad)
    middle_grad = upstream + middle_part
    attn_grad, gain_post_grad = post_pull(middle_grad)
    attn_grad_b = attn_grad.astype(jnp.bfloat16)
    out_w_grad = inner_rows(mixed_tokens, attn_grad_b)
    mixed_grad = outer_rows(attn_grad_b, out_w).astype(jnp.bfloat16)
    mixed_grad_heads = lax.all_to_all(mixed_grad, "seq", split_axis=1, concat_axis=0, tiled=True)
    grad_blocks = mixed_grad_heads.reshape(block_count, block_rows, head_width)

    def attend_back(carried, block_item):
        key_accum, value_accum = carried
        queries, bounds, block_index, lse_row, block_grad = block_item
        scores = masked_scores(queries, key_rows, bounds, block_index * block_rows)
        probability = jnp.exp(scores - lse_row[:, None])
        prob_grad = outer_rows(block_grad, value_rows)
        value_accum = value_accum + inner_rows(probability.astype(jnp.bfloat16), block_grad)
        row_delta = jnp.sum(probability * prob_grad, axis=1, keepdims=True)
        score_grad = (probability * (prob_grad - row_delta)).astype(jnp.bfloat16)
        query_grad = product(score_grad, key_rows) * score_scale
        key_accum = key_accum + inner_rows(score_grad, queries) * score_scale
        return ((key_accum, value_accum), query_grad)

    zero_rows = jnp.zeros((seq_tokens, head_width), jnp.float32)
    (key_part, value_part), query_grad_blocks = lax.scan(
        attend_back,
        (zero_rows, zero_rows),
        (query_blocks, start_blocks, block_ids, lse_blocks, grad_blocks),
    )
    key_sum, value_sum = (
        lax.psum_scatter(
            key_part.astype(jnp.bfloat16), "seq", scatter_dimension=0, tiled=True
        ).astype(jnp.float32),
        lax.psum_scatter(
            value_part.astype(jnp.bfloat16), "seq", scatter_dimension=0, tiled=True
        ).astype(jnp.float32),
    )
    query_grad_tokens = lax.all_to_all(
        query_grad_blocks.reshape(seq_tokens, head_width).astype(jnp.bfloat16),
        "seq",
        split_axis=0,
        concat_axis=1,
        tiled=True,
    ).astype(jnp.float32)
    query_raw_grad, gain_query_grad = query_pull(
        query_grad_tokens.reshape(tok_rows, head_count, head_width)
    )
    key_raw_grad, gain_key_grad = key_pull(key_sum.reshape(tok_rows, 1, head_width))
    query_raw_b = query_raw_grad.reshape(tok_rows, head_count * head_width).astype(jnp.bfloat16)
    key_raw_b = key_raw_grad.reshape(tok_rows, head_width).astype(jnp.bfloat16)
    value_raw_b = value_sum.astype(jnp.bfloat16)
    query_w_grad_t = inner_rows(query_raw_b, normed_b)
    key_w_grad_t = inner_rows(key_raw_b, normed_b)
    value_w_grad_t = inner_rows(value_raw_b, normed_b)
    normed_grad = (
        outer_rows(query_raw_b, query_w)
        + outer_rows(key_raw_b, key_w)
        + outer_rows(value_raw_b, value_w)
    )
    residual_part, gain_pre_grad = pre_pull(normed_grad)
    input_grad = middle_grad + residual_part
    gains_grad = jnp.concatenate(
        [
            gain_pre_grad,
            gain_query_grad,
            gain_key_grad,
            gain_post_grad,
            gain_pre_ffn_grad,
            gain_post_ffn_grad,
        ]
    )
    shares = (
        lax.psum_scatter(gains_grad, ("fsdp", "seq"), scatter_dimension=0, tiled=True),
        lax.psum_scatter(query_w_grad_t, ("fsdp", "seq"), scatter_dimension=0, tiled=True),
        lax.psum_scatter(key_w_grad_t, ("fsdp", "seq"), scatter_dimension=0, tiled=True),
        lax.psum_scatter(value_w_grad_t, ("fsdp", "seq"), scatter_dimension=0, tiled=True),
        lax.psum_scatter(out_w_grad, ("fsdp", "seq"), scatter_dimension=0, tiled=True),
        lax.psum_scatter(gate_w_grad_t, ("fsdp", "seq"), scatter_dimension=0, tiled=True),
        lax.psum_scatter(up_w_grad_t, ("fsdp", "seq"), scatter_dimension=0, tiled=True),
        lax.psum_scatter(down_w_grad, ("fsdp", "seq"), scatter_dimension=0, tiled=True),
    )
    return (
        result,
        input_grad,
        shares[0],
        shares[1].T,
        shares[2].T,
        shares[3].T,
        shares[4],
        shares[5].T,
        shares[6].T,
        shares[7],
    )


gelu_c = 0.7978845608028654
MESH = pl.DeviceIdType.MESH
DMA = pltpu.SemaphoreType.DMA


def nt(former, latter):
    return lax.dot_general(
        former, latter, (((1,), (1,)), ((), ())), preferred_element_type=jnp.float32
    )


def nn(former, latter):
    return lax.dot_general(
        former, latter, (((1,), (0,)), ((), ())), preferred_element_type=jnp.float32
    )


def tn(former, latter):
    return lax.dot_general(
        former, latter, (((0,), (0,)), ((), ())), preferred_element_type=jnp.float32
    )


class Place:
    def __init__(self):
        self.f = lax.axis_index("fsdp")
        self.s = lax.axis_index("seq")
        self.z = self.f // 2
        self.y = lax.rem(self.f, 2)
        self.core = lax.rem(self.s, 2)
        self.high = self.z // 2
        self.inner = self.z * (3 - self.z) == 2
        self.outer = self.z * (3 - self.z) == 0
        self.sibling = (self.f, self.s + 1 - 2 * self.core)
        self.over_x = (self.f, lax.rem(self.s + 2, 4))
        self.over_y = (self.f + 1 - 2 * self.y, self.s)
        self.toward = 1 - 2 * self.high
        self.step_first = self.toward * (1 - self.z * (3 - self.z))

    def at_z(self, z):
        return (z * 2 + self.y, self.s)

    def source(self, j):
        last = j // 3
        middle = j // 2 - last
        none = (3 - j) // 3
        first = 1 - last - middle - none
        return (
            none * self.z
            + first * (1 - self.z + 4 * self.high)
            + middle * (2 - self.high)
            + last * (3 - 3 * self.high)
        )


def remote(source, target, send_sem, recv_sem, device):
    return pltpu.make_async_remote_copy(
        src_ref=source,
        dst_ref=target,
        send_sem=send_sem,
        recv_sem=recv_sem,
        device_id=device,
        device_id_type=MESH,
    )


def greet(partners):
    entry = pltpu.get_barrier_semaphore()
    for partner in partners:
        pl.semaphore_signal(entry, inc=1, device_id=partner, device_id_type=MESH)
    return entry


def exchange_pass(at, held, gather_sems, sum_sems, sum_bufs, part_own, compute, lag=0, ready=None, then=()):
    z_own, z_next, z_in, y_out, y_in, c_out, c_in = gather_sems
    t_out, t_in, v_out, v_in, w_out, w_in = sum_sems
    to_sib, from_sib, chip_sum, from_y, to_z, from_z = sum_bufs
    f, core = at.f, at.core

    def block(chip):
        return held.at[chip, core]

    def over(chip, outgoing, incoming, device):
        return remote(block(chip), block(chip), outgoing, incoming, device)

    def own_z(step, slot):
        return over(f, z_own.at[slot], z_in.at[at.z], at.at_z(at.z + step))

    def own_z_toward():
        return own_z(at.toward, 0)

    def own_z_away():
        return own_z(-at.toward, 1)

    def pass_z(src, step):
        return over(src * 2 + at.y, z_next.at[src], z_in.at[src], at.at_z(at.z + step))

    def pass_y(src):
        return over(src * 2 + at.y, y_out.at[src], y_in.at[src], at.over_y)

    def pass_sib(chip):
        return over(chip, c_out.at[chip], c_in.at[chip], at.sibling)

    own_z_toward().start()

    @pl.when(at.inner)
    def _():
        own_z_away().start()

    pass_y(at.z).start()
    pass_sib(f).start()

    def from_z_block(src):
        return over(src * 2 + at.y, z_next.at[src], z_in.at[src], at.at_z(src))

    def take_z(j, step):
        src = at.source(j)
        from_z_block(src).wait_recv()

        @pl.when(at.inner)
        def _():
            pass_z(src, step).start()

        pass_y(src).start()
        pass_sib(src * 2 + at.y).start()

    def chip_of(i):
        return at.source(i // 2) * 2 + lax.rem(at.y + lax.rem(i, 2), 2)

    def sib_sum(i):
        return remote(to_sib.at[i], from_sib.at[i], t_out.at[i], t_in.at[i], at.sibling)

    rows = part_own.shape[0] // 2
    pieces = [pl.ds(k * rows, rows) for k in range(2)]

    def y_sum(i, k):
        return remote(
            chip_sum.at[i, pieces[k]],
            from_y.at[i // 2, pieces[k]],
            v_out.at[i // 2, k],
            v_in.at[i // 2, k],
            at.over_y,
        )

    def send_y(i):
        for k in range(2):
            y_sum(i, k).start()

    def finish_chip(i):
        sib_sum(i).wait_recv()
        chip_sum[i] = (part_own[...] + from_sib[i].astype(jnp.float32)).astype(jnp.bfloat16)

    def arrivals(i):
        @pl.when(i == 1)
        def _():
            take_z(1, at.toward)

            @pl.when(at.inner)
            def _():
                take_z(2, -at.toward)

        @pl.when((i == 3) & at.outer)
        def _():
            take_z(2, -at.toward)

        @pl.when(((i == 3) & at.inner) | ((i == 5) & at.outer))
        def _():
            take_z(3, -at.toward)

        @pl.when(lax.rem(i, 2) == 1)
        def _():
            pass_y(at.source(i // 2)).wait_recv()
            pass_sib(chip_of(i)).start()

    def one_chip(i):
        chip = chip_of(i)
        pass_sib(chip).wait_recv()
        own_part, sib_part = compute(chip)
        to_sib[i] = sib_part.astype(jnp.bfloat16)
        sib_sum(i).start()

        @pl.when(i > 0)
        def _():
            finish_chip(i - 1)

        part_own[...] = own_part

    def step(i, carried):
        @pl.when(i < 8)
        def _():
            arrivals(i)

        @pl.when(i == 7 + lag)
        def _():
            send_y(5)

        if ready is not None:

            @pl.when(i == lag)
            def _():
                ready()

        @pl.when(i >= lag)
        def _():
            one_chip(i - lag)

        return carried

    lax.fori_loop(0, 8 + lag, step, 0)
    finish_chip(7)
    for j in (3, 1, 0):
        send_y(2 * j + 1)
    later = list(then) + [lambda: None] * 4
    later[0]()

    def z_sum(target, direction, k, device=None):
        slot = (direction + 1) // 2
        return remote(
            to_z.at[target, pieces[k]],
            from_z.at[slot, target, pieces[k]],
            w_out.at[target, k],
            w_in.at[slot, target, k],
            at.at_z(at.z + direction) if device is None else device,
        )

    def z_arrival(target, direction, k):
        return z_sum(target, direction, k, at.at_z(lax.rem(at.z - direction + 4, 4)))

    def direction_of(j):
        return at.step_first if j == 1 else at.toward

    for place, j in enumerate((2, 3, 1)):
        target, direction = at.source(j), direction_of(j)
        for k, piece in enumerate(pieces):
            y_sum(2 * j + 1, k).wait_recv()
            mine = chip_sum[2 * j, piece].astype(jnp.float32) + from_y[j, piece].astype(
                jnp.float32
            )

            @pl.when(at.outer)
            def _():
                to_z[target, piece] = mine.astype(jnp.bfloat16)

            @pl.when(at.inner)
            def _():
                z_arrival(target, direction, k).wait_recv()
                ahead = from_z[(direction + 1) // 2, target, piece].astype(jnp.float32)
                to_z[target, piece] = (mine + ahead).astype(jnp.bfloat16)

            z_sum(target, direction, k).start()
        later[1 + place]()

    def finish():
        for k, piece in enumerate(pieces):
            y_sum(1, k).wait_recv()
            part_own[piece] = chip_sum[0, piece].astype(jnp.float32) + from_y[0, piece].astype(
                jnp.float32
            )
            z_arrival(at.z, -at.toward, k).wait_recv()
            part_own[piece] += from_z[(1 - at.toward) // 2, at.z, piece].astype(jnp.float32)

            @pl.when(at.inner)
            def _():
                z_arrival(at.z, at.toward, k).wait_recv()
                part_own[piece] += from_z[(1 + at.toward) // 2, at.z, piece].astype(jnp.float32)

        return part_own[...]

    def drain():
        own_z_toward().wait_send()

        @pl.when(at.inner)
        def _():
            own_z_away().wait_send()
            for j in (1, 2, 3):
                from_z_block(at.source(j)).wait_send()

        def drain_chip(i, carried):
            pass_sib(chip_of(i)).wait_send()
            sib_sum(i).wait_send()

            @pl.when(lax.rem(i, 2) == 1)
            def _():
                pass_y(at.source(i // 2)).wait_send()
                for k in range(2):
                    y_sum(i, k).wait_send()

            return carried

        lax.fori_loop(0, 8, drain_chip, 0)
        for j in (1, 2, 3):
            for k in range(2):
                z_sum(at.source(j), direction_of(j), k).wait_send()

    return finish, drain


gain_edges = (0, 1152, 1408, 1664, 2816, 3968, 5120)
score_step = 0.0625
log_base = 13.815510557964274
hidden_score = -1e30


def shape_spec(shape, dtype):
    return jax.ShapeDtypeStruct(shape, dtype)


def rms_scale(values):
    return lax.rsqrt(jnp.mean(values * values, axis=-1, keepdims=True) + norm_eps)


def norm_back(values, gain, upstream):
    scale = rms_scale(values)
    weighted = upstream * gain
    inner = jnp.mean(weighted * values, axis=-1, keepdims=True)
    back = scale * weighted - values * (scale * scale * scale * inner)
    return back, jnp.sum(upstream * values * scale, axis=0, keepdims=True)


def pick(offset):
    row = lax.broadcasted_iota(jnp.int32, (256, 512), 0)
    column = lax.broadcasted_iota(jnp.int32, (256, 512), 1)
    wanted = row // 8 * 16 + lax.rem(row, 8) + offset
    return jnp.where(column == wanted, 1.0, 0.0).astype(jnp.bfloat16)


def rows_of_all(w_all, low, count):
    return jnp.concatenate(
        [w_all[d // 2, d % 2, low : low + count] for d in range(32)], axis=0
    )


def rows_of_head(w_all, head, low, count):
    return jnp.concatenate(
        [w_all[d // 2, d % 2, low : low + count] for d in range(8 * head, 8 * head + 8)], axis=0
    )


class GainGather:
    def __init__(self, at, held, sems):
        self.at, self.held = at, held
        self.out, self.inc, self.z_out, self.z_in = sems
        x = at.s // 2
        self.spans = (
            (at.f * 4 + at.s, 1, at.sibling),
            (at.f * 4 + 2 * x, 2, at.over_x),
            (at.f * 4, 4, at.over_y),
        )

    def stage(self, k):
        first, count, partner = self.spans[k]
        span = self.held.at[pl.ds(first, count)]
        return remote(span, span, self.out.at[k], self.inc.at[k], partner)

    def last(self, src, j, device):
        span = self.held.at[pl.ds(src * 8, 8)]
        return remote(span, span, self.z_out.at[j], self.z_in.at[src], device)

    def send(self, k):
        at = self.at
        if k < 3:
            self.stage(k).start()
        else:
            for j in (1, 2, 3):
                self.last(at.z, j, at.at_z(at.source(j))).start()

    def take(self, k):
        at = self.at
        if k < 3:
            self.stage(k).wait_recv()
        else:
            for j in (1, 2, 3):
                self.last(at.source(j), j, at.at_z(at.source(j))).wait_recv()

    def drain(self):
        at = self.at
        for k in range(3):
            self.stage(k).wait_send()
        for j in (1, 2, 3):
            self.last(at.z, j, at.at_z(at.source(j))).wait_send()


class WeightGather:
    def __init__(self, at, w_all, sems, part, low, high):
        self.at, self.w_all, self.part = at, w_all, part
        (
            self.x_out,
            self.x_in,
            self.first_out,
            self.first_in,
            self.z_own,
            self.z_next,
            self.z_in,
            self.y_out,
            self.y_in,
            self.s_out,
            self.s_in,
        ) = sems
        self.rows = pl.ds(low, high - low)
        self.x = at.s // 2

    def one(self, y, x, outgoing, incoming, device):
        span = self.w_all.at[(self.at.z * 2 + y) * 2 + x, self.at.core, self.rows]
        return remote(span, span, outgoing, incoming, device)

    def pair(self, z, y, outgoing, incoming, device):
        span = self.w_all.at[pl.ds((z * 2 + y) * 2, 2), self.at.core, self.rows]
        return remote(span, span, outgoing, incoming, device)

    def x_copy(self, x):
        p, at = self.part, self.at
        return self.one(at.y, x, self.x_out.at[p], self.x_in.at[p], at.over_x)

    def y_first(self, y, x):
        p, at = self.part, self.at
        return self.one(y, x, self.first_out.at[p, x], self.first_in.at[p, x], at.over_y)

    def own(self, step, slot):
        p, at = self.part, self.at
        return self.pair(
            at.z, at.y, self.z_own.at[p, slot], self.z_in.at[p, at.z], at.at_z(at.z + step)
        )

    def passed(self, src, device):
        p = self.part
        return self.pair(src, self.at.y, self.z_next.at[p, src], self.z_in.at[p, src], device)

    def y_pair(self, src, y):
        p = self.part
        return self.pair(src, y, self.y_out.at[p, src], self.y_in.at[p, src], self.at.over_y)

    def sib(self, src):
        span = self.w_all.at[pl.ds(src * 4, 4), self.at.core, self.rows]
        p = self.part
        return remote(span, span, self.s_out.at[p, src], self.s_in.at[p, src], self.at.sibling)

    def begin(self):
        self.x_copy(self.x).start()
        self.y_first(self.at.y, self.x).start()

    def spread(self):
        at = self.at
        self.x_copy(1 - self.x).wait_recv()
        self.own(at.toward, 0).start()

        @pl.when(at.inner)
        def _():
            self.own(-at.toward, 1).start()

        self.y_first(at.y, 1 - self.x).start()

    def take(self, j):
        at = self.at
        src = at.source(j)
        self.passed(src, at.at_z(src)).wait_recv()

        @pl.when(at.inner)
        def _():
            self.passed(src, at.at_z(at.z + (at.toward if j == 1 else -at.toward))).start()

        self.y_pair(src, at.y).start()

    def close(self, j):
        src = self.at.source(j)
        if j == 0:
            for x in (0, 1):
                self.y_first(1 - self.at.y, x).wait_recv()
        else:
            self.y_pair(src, 1 - self.at.y).wait_recv()
        self.sib(src).start()

    def walk(self, between=()):
        at = self.at
        extra = list(between) + [lambda: None] * 3
        self.take(1)

        @pl.when(at.inner)
        def _():
            self.take(2)

        extra[0]()
        self.close(0)

        @pl.when(at.inner)
        def _():
            self.take(3)

        @pl.when(at.outer)
        def _():
            self.take(2)

        extra[1]()
        self.close(1)

        @pl.when(at.outer)
        def _():
            self.take(3)

        extra[2]()
        self.close(2)
        self.close(3)

    def settle(self):
        for j in range(4):
            self.sib(self.at.source(j)).wait_recv()

    def drain(self):
        at = self.at
        self.x_copy(self.x).wait_send()
        for x in (0, 1):
            self.y_first(at.y, x).wait_send()
        self.own(at.toward, 0).wait_send()

        @pl.when(at.inner)
        def _():
            self.own(-at.toward, 1).wait_send()
            for j in (1, 2, 3):
                self.passed(at.source(j), at.at_z(at.source(j))).wait_send()

        for j in range(4):
            src = at.source(j)
            if j > 0:
                self.y_pair(src, at.y).wait_send()
            self.sib(src).wait_send()


def gather_weight_sems():
    return [DMA((2,)), DMA((2,))] + [DMA((2, 2))] * 3 + [DMA((2, 4))] * 6


def gain_sems():
    return [DMA((3,)), DMA((3,)), DMA((4,)), DMA((4,))]


def turn(values, cos, sin):
    a, b = values[:, :128], values[:, 128:]
    return jnp.concatenate([a * cos - b * sin, b * cos + a * sin], axis=1)


def turn_back(values, cos, sin):
    a, b = values[:, :128], values[:, 128:]
    return jnp.concatenate([a * cos + b * sin, b * cos - a * sin], axis=1)


class WeightReturn:
    def __init__(self, at, held, bufs, sems, part, low, middle, high):
        self.at, self.held, self.part = at, held, part
        self.sib_in, self.xh_in, self.yh_in, self.xf_in, self.yf_in, self.z_in = bufs
        (
            self.so,
            self.si,
            self.xho,
            self.xhi,
            self.yho,
            self.yhi,
            self.xfo,
            self.xfi,
            self.yfo,
            self.yfi,
            self.zo,
            self.zi,
        ) = sems
        self.low, self.middle, self.high = low, middle, high
        self.x = at.s // 2
        self.rows = pl.ds(low, high - low)
        self.top = pl.ds(low, middle - low)
        self.bottom = pl.ds(middle, high - middle)
        self.by_x, self.by_y = middle > low, high > middle

    def mine(self, z, y, x, rows):
        return self.held.at[self.at.core, z * 2 + y, x, rows]

    def sib(self, z):
        pair = pl.ds(z * 2, 2)
        p = self.part
        return remote(
            self.held.at[1 - self.at.core, pair, :, self.rows],
            self.sib_in.at[pair, :, self.rows],
            self.so.at[p, z],
            self.si.at[p, z],
            self.at.sibling,
        )

    def x_half(self, z):
        p = self.part
        source = self.mine(z, 1 - self.at.y, 1 - self.x, self.top)
        return remote(
            source, self.xh_in.at[z, self.top], self.xho.at[p, z], self.xhi.at[p, z], self.at.over_x
        )

    def y_half(self, z):
        p = self.part
        source = self.mine(z, 1 - self.at.y, 1 - self.x, self.bottom)
        return remote(
            source,
            self.yh_in.at[z, self.bottom],
            self.yho.at[p, z],
            self.yhi.at[p, z],
            self.at.over_y,
        )

    def x_full(self, z):
        p = self.part
        source = self.mine(z, self.at.y, 1 - self.x, self.rows)
        return remote(
            source,
            self.xf_in.at[z, self.rows],
            self.xfo.at[p, z],
            self.xfi.at[p, z],
            self.at.over_x,
        )

    def y_full(self, z):
        p = self.part
        source = self.mine(z, 1 - self.at.y, self.x, self.rows)
        return remote(
            source,
            self.yf_in.at[z, self.rows],
            self.yfo.at[p, z],
            self.yfi.at[p, z],
            self.at.over_y,
        )

    def z_part(self, z):
        p = self.part
        source = self.mine(z, self.at.y, self.x, self.rows)
        return remote(
            source,
            self.z_in.at[self.at.z, self.rows],
            self.zo.at[p, z],
            self.zi.at[p, self.at.z],
            self.at.at_z(z),
        )

    def z_arrival(self, z):
        p = self.part
        source = self.mine(z, self.at.y, self.x, self.rows)
        return remote(
            source,
            self.z_in.at[z, self.rows],
            self.zo.at[p, z],
            self.zi.at[p, z],
            self.at.at_z(z),
        )

    def add(self, z, y, x, rows, more):
        core, f = self.at.core, z * 2 + y
        self.held[core, f, x, rows] = (
            self.held[core, f, x, rows].astype(jnp.float32) + more.astype(jnp.float32)
        ).astype(jnp.bfloat16)

    def send_sib(self):
        for j in (3, 2, 1, 0):
            self.sib(self.at.source(j)).start()

    def merge(self):
        for j in (3, 2, 1, 0):
            z = self.at.source(j)
            self.sib(z).wait_recv()
            for y in (0, 1):
                for x in (0, 1):
                    self.add(z, y, x, self.rows, self.sib_in[z * 2 + y, x, self.rows])
            (self.x_half if self.by_x else self.y_full)(z).start()
            (self.y_half if self.by_y else self.x_full)(z).start()

    def pair_up(self):
        at = self.at
        for j in (3, 2, 1, 0):
            z = at.source(j)
            if self.by_x:
                self.x_half(z).wait_recv()
                self.add(z, 1 - at.y, self.x, self.top, self.xh_in[z, self.top])
                self.y_full(z).start()
            if self.by_y:
                self.y_half(z).wait_recv()
                self.add(z, at.y, 1 - self.x, self.bottom, self.yh_in[z, self.bottom])
                self.x_full(z).start()

    def collect(self):
        at = self.at
        for j in (3, 2, 1, 0):
            z = at.source(j)
            self.y_full(z).wait_recv()
            self.x_full(z).wait_recv()
            more = self.yf_in[z, self.rows].astype(jnp.float32) + self.xf_in[
                z, self.rows
            ].astype(jnp.float32)
            self.add(z, at.y, self.x, self.rows, more)
            if j > 0:
                self.z_part(z).start()

    def total(self):
        at = self.at
        value = self.held[at.core, at.f, self.x, self.rows].astype(jnp.float32)
        for j in (3, 2, 1):
            z = at.source(j)
            self.z_arrival(z).wait_recv()
            value = value + self.z_in[z, self.rows].astype(jnp.float32)
        return value

    def drain(self):
        for j in range(4):
            z = self.at.source(j)
            for copy in (self.sib, self.x_full, self.y_full):
                copy(z).wait_send()
            if self.by_x:
                self.x_half(z).wait_send()
            if self.by_y:
                self.y_half(z).wait_send()
            if j > 0:
                self.z_part(z).wait_send()


class GainSum:
    def __init__(self, at, row, outgoing, incoming, sems):
        self.at, self.row, self.outgoing, self.incoming = at, row, outgoing, incoming
        self.out, self.inc = sems
        self.partners = (at.sibling, at.over_x, at.over_y)

    def stage(self, k):
        return remote(
            self.outgoing.at[k],
            self.incoming.at[k],
            self.out.at[k],
            self.inc.at[k],
            self.partners[k],
        )

    def last(self, src, j, device):
        return remote(
            self.outgoing.at[3],
            self.incoming.at[3 + src],
            self.out.at[2 + j],
            self.inc.at[3 + src],
            device,
        )

    def send(self, k):
        self.outgoing[k] = self.row[...]
        if k < 3:
            self.stage(k).start()
        else:
            for j in (1, 2, 3):
                self.last(self.at.z, j, self.at.at_z(self.at.source(j))).start()

    def take(self, k):
        if k < 3:
            self.stage(k).wait_recv()
            self.row[...] += self.incoming[k]
        else:
            for j in (1, 2, 3):
                src = self.at.source(j)
                self.last(src, j, self.at.at_z(src)).wait_recv()
                self.row[...] += self.incoming[3 + src]

    def drain(self):
        for k in range(3):
            self.stage(k).wait_send()
        for j in (1, 2, 3):
            self.last(self.at.z, j, self.at.at_z(self.at.source(j))).wait_send()


class Refs:
    def __init__(self, names, refs):
        for name, ref in zip(names, refs):
            setattr(self, name, ref)


def columns_of(head):
    return slice(256 * head, 256 * head + 256)


def front_phase(at, r, sems):
    core, s = at.core, at.s
    gathered = GainGather(at, r.gain_all, sems[:4])
    w_sems = sems[4:15]
    kv_out, kv_in, x_out, x_in = sems[15:19]
    w_all, kv_all = r.w_all, r.kv_all
    early = WeightGather(at, w_all, w_sems, 0, 0, 48)
    late = WeightGather(at, w_all, w_sems, 1, 48, 80)
    chip = at.f * 2 + s // 2
    entry = greet(
        [at.sibling, at.over_x, at.over_y]
        + [at.at_z(lax.rem(at.z + step, 4)) for step in (1, 2, 3)]
    )
    w_all[chip, core, 0:32] = r.own_q[...]
    w_all[chip, core, 32:48] = jnp.concatenate(
        [r.own_k[...].astype(jnp.float32), r.own_v[...].astype(jnp.float32)], axis=0
    ).astype(jnp.bfloat16)
    w_all[chip, core, 48:80] = r.own_o[...]
    device = at.f * 4 + s
    share = jnp.concatenate(
        [r.own_gains[...].astype(jnp.float32).reshape(1, 160), jnp.zeros((1, 96), jnp.float32)],
        axis=1,
    )
    r.gain_all[device] = pltpu.roll(share, lax.rem(device, 4) * 32, 1)
    pl.semaphore_wait(entry, 6)
    def x_weight(k):
        ref = (r.own_gate, r.own_up, r.own_down)[k]
        return remote(ref, r.peer_w.at[k], x_out.at[k], x_in.at[k], at.over_x)

    def gain_step(k):
        def step():
            gathered.take(k)
            if k < 3:
                gathered.send(k + 1)

        return step

    gathered.send(0)
    early.begin()
    late.begin()
    gain_step(0)()
    early.spread()
    x_weight(0).start()
    x_weight(1).start()
    gain_step(1)()
    starts = jnp.broadcast_to(r.doc[...].astype(jnp.float32).reshape(1, 128), (128, 128)).T
    r.starts[...] = starts
    place = (lax.broadcasted_iota(jnp.int32, (128, 128), 0) + s * 128).astype(jnp.float32)
    step = lax.broadcasted_iota(jnp.int32, (128, 128), 1).astype(jnp.float32)
    angle = (place - starts) * jnp.exp(step * (-2.0 / 256 * log_base))
    r.cos[...] = jnp.cos(angle)
    r.sin[...] = jnp.sin(angle)

    def first_norm():
        late.spread()
        placed = r.gain_all[...].reshape(32, 256)
        pieces = []
        for m in range(8):
            for k in range(5):
                piece = None
                if k < 4:
                    piece = placed[4 * m + k : 4 * m + k + 1, :128]
                if k > 0:
                    other = placed[4 * m + k - 1 : 4 * m + k, 128:]
                    piece = other if piece is None else piece + other
                pieces.append(piece)
        r.gains[...] = jnp.concatenate(pieces, axis=1)
        gain = gain_parts(r)
        residual = r.tokens[...].astype(jnp.float32)
        r.normed[...] = (residual * rms_scale(residual) * gain[0]).astype(jnp.bfloat16)
    early.walk((gain_step(2), gain_step(3), first_norm))
    gain = gain_parts(r)
    early.settle()
    normed = r.normed[...]
    cos, sin = r.cos[...], r.sin[...]
    mixed_rows = rows_of_all(w_all, 32, 16)
    r.wk[...] = nn(pick(0), mixed_rows).astype(jnp.bfloat16)
    r.wv[...] = nn(pick(8), mixed_rows).astype(jnp.bfloat16)
    k_raw = nt(normed, r.wk[...])
    r.k_raw[...] = k_raw
    key = turn(k_raw * rms_scale(k_raw) * gain[2], cos, sin)
    kv_all[s, :, :256] = key.astype(jnp.bfloat16)
    kv_all[s, :, 256:] = nt(normed, r.wv[...]).astype(jnp.bfloat16)

    def kv_copy(which, slot, device):
        return remote(kv_all.at[slot], kv_all.at[slot], kv_out.at[which], kv_in.at[which], device)

    peer_slot = lax.rem(s + 2, 4)
    kv_copy(0, s, at.over_x).start()
    kv_copy(1, s, at.sibling).start()

    def one_query(head):
        q_raw = nt(normed, rows_of_head(w_all, head, 0, 32))
        r.q_raw[:, columns_of(head)] = q_raw
        query = turn(q_raw * rms_scale(q_raw) * gain[1], cos, sin)
        r.query[:, columns_of(head)] = query.astype(jnp.bfloat16)

    def pass_kv():
        one_query(0)
        kv_copy(0, peer_slot, at.over_x).wait_recv()
        kv_copy(2, peer_slot, at.sibling).start()
        x_weight(2).start()
        one_query(1)

    late.walk((pass_kv, lambda: one_query(2), lambda: one_query(3)))
    other = s + 1 - 2 * core
    kv_copy(1, other, at.sibling).wait_recv()
    kv_copy(2, lax.rem(other + 2, 4), at.sibling).wait_recv()
    keys, values = kv_parts(r)
    key_place = lax.broadcasted_iota(jnp.int32, (128, 512), 1)
    query_place = lax.broadcasted_iota(jnp.int32, (128, 512), 0) + s * 128
    starts = jnp.concatenate([r.starts[...]] * 4, axis=1).astype(jnp.int32)
    allowed = (key_place >= starts) & (key_place <= query_place)
    for head in range(4):
        raw = nt(r.query[:, columns_of(head)], keys) * score_step
        scores = jnp.where(allowed, raw, hidden_score)
        weights = jnp.exp(scores - jnp.max(scores, axis=1, keepdims=True))
        prob = weights / jnp.sum(weights, axis=1, keepdims=True)
        r.prob[head] = prob
        mixed = nn(prob.astype(jnp.bfloat16), values).astype(jnp.bfloat16)
        r.mixed[:, columns_of(head)] = mixed
    late.settle()
    attn = nn(r.mixed[...], rows_of_all(w_all, 48, 32))
    r.attn[...] = attn
    middle = r.tokens[...].astype(jnp.float32) + attn * rms_scale(attn) * gain[3]
    r.middle[...] = middle
    normed_ffn = (middle * rms_scale(middle) * gain[4]).astype(jnp.bfloat16)

    def drain():
        gathered.drain()
        early.drain()
        late.drain()
        kv_copy(0, s, at.over_x).wait_send()
        kv_copy(1, s, at.sibling).wait_send()
        kv_copy(2, peer_slot, at.sibling).wait_send()

    return normed_ffn, x_weight, drain


def gain_parts(r):
    return [r.gains[:, a:b] for a, b in zip(gain_edges[:-1], gain_edges[1:])]


def kv_parts(r):
    return r.kv_all[...].reshape(512, 512)[:, :256], r.kv_all[...].reshape(512, 512)[:, 256:]


def ffn_phase(at, r, sems, normed_ffn, x_weight):
    core = at.core
    fwd_gather, fwd_sum = sems[:7], sems[7:13]
    bwd_gather, bwd_sum = sems[13:20], sems[20:26]
    x_out, x_in = sems[26:28]
    sum_bufs = (r.to_sib, r.from_sib, r.chip_sum, r.from_y, r.to_z, r.from_z)
    normed_all, grad_all = r.held.at[0], r.held.at[1]
    gates = (r.own_gate, r.peer_w.at[0])
    ups = (r.own_up, r.peer_w.at[1])
    downs = (r.own_down, r.peer_w.at[2])
    r.held[0, at.f, core] = normed_ffn

    def rows_of(which, chip):
        return jnp.concatenate([r.held[which, chip, core], r.held[which, chip, 1 - core]], axis=0)

    def weights_here():
        for k in range(3):
            x_weight(k).wait()

    def forward(chip):
        rows = rows_of(0, chip)
        total = None
        for half in (0, 1):
            gate = nt(rows, gates[half][...])
            up = nt(rows, ups[half][...])
            r.gate_keep[half, chip] = gate.astype(jnp.bfloat16)
            r.up_keep[half, chip] = up.astype(jnp.bfloat16)
            bend = jnp.tanh(gelu_c * (gate + 0.044715 * gate * gate * gate))
            hidden = (0.5 * gate * (1.0 + bend) * up).astype(jnp.bfloat16)
            r.hidden_keep[half, chip] = hidden
            part = nn(hidden, downs[half][...])
            total = part if total is None else total + part
        return total[:128], total[128:]

    finish, drain = exchange_pass(
        at, normed_all, fwd_gather, fwd_sum, sum_bufs, r.part_own, forward, 0, weights_here
    )
    gain = gain_parts(r)[5]
    upstream = r.cotangent[...].astype(jnp.float32)
    ffn_grad, _ = norm_back(finish(), gain, upstream)
    r.held[1, at.f, core] = ffn_grad.astype(jnp.bfloat16)
    drain_forward = drain

    def write_result():
        ffn_raw = r.part_own[...]
        normed = ffn_raw * rms_scale(ffn_raw)
        r.result[...] = (r.middle[...] + normed * gain).astype(jnp.bfloat16)
        share = jnp.sum(r.cotangent[...].astype(jnp.float32) * normed, axis=0, keepdims=True)
        r.gain_sum[:, gain_edges[5] : gain_edges[6]] = share
        drain_forward()

    own_grads = (r.gate_grad, r.up_grad, r.down_grad)

    def backward(chip):
        rows = rows_of(1, chip)
        total = None
        for half in (0, 1):
            dhidden = nt(rows, downs[half][...])
            gate = r.gate_keep[half, chip].astype(jnp.float32)
            up = r.up_keep[half, chip].astype(jnp.float32)
            square = gate * gate
            bend = jnp.tanh(gelu_c * (gate + 0.044715 * square * gate))
            unit = 0.5 * gate * (1.0 + bend)
            slope = 0.5 * (1.0 + bend) + 0.5 * gate * (1.0 - bend * bend) * (
                gelu_c * (1.0 + 3 * 0.044715 * square)
            )
            dgate = (dhidden * up * slope).astype(jnp.bfloat16)
            dup = (dhidden * unit).astype(jnp.bfloat16)
            part = nn(dgate, gates[half][...]) + nn(dup, ups[half][...])
            total = part if total is None else total + part
            r.gate_keep[half, chip] = dgate
            r.up_keep[half, chip] = dup
        return total[:128], total[128:]

    def x_copy(k):
        return remote(r.peer_w.at[k], r.from_x.at[k], x_out.at[k], x_in.at[k], at.over_x)

    kept = ((r.gate_keep, 0), (r.up_keep, 0), (r.hidden_keep, 1))

    def weight_grad(k, half):
        left, which = kept[k]
        total = None
        for chip in range(8):
            part = tn(left[half, chip], rows_of(which, chip))
            total = part if total is None else total + part
        return total

    def peers():
        for k in range(3):
            r.peer_w[k] = weight_grad(k, 1).astype(jnp.bfloat16)
            x_copy(k).start()

    def own(k):
        def step():
            own_grads[k][...] = weight_grad(k, 0)

        return step

    finish, drain = exchange_pass(
        at,
        grad_all,
        bwd_gather,
        bwd_sum,
        sum_bufs,
        r.part_own,
        backward,
        0,
        write_result,
        (peers, own(0), own(1), own(2)),
    )
    normed_grad = finish()
    drain()

    def complete():
        for k in range(3):
            x_copy(k).wait()
            own_grads[k][...] += r.from_x[k].astype(jnp.float32)

    return normed_grad, complete


def back_phase(at, r, sems, normed_grad, complete):
    core, s = at.core, at.s
    x = s // 2
    gain = gain_parts(r)
    cos, sin = r.cos[...], r.sin[...]
    bufs = (r.sib_in, r.half_in, r.half_in, r.xf_in, r.yf_in, r.zw_in)
    w_sems = sems[:12]
    kv_out, kv_in = sems[12:14]
    outer = WeightReturn(at, r.held, bufs, w_sems, 1, 48, 64, 80)
    inner = WeightReturn(at, r.held, bufs, w_sems, 0, 0, 16, 48)
    gain_total = GainSum(at, r.gain_sum, r.gain_out, r.gain_in, sems[14:16])

    def write(k):
        source, target = (
            (r.result, r.result_out),
            (r.token_grad, r.token_grad_out),
            (r.gate_grad, r.gate_grad_out),
            (r.up_grad, r.up_grad_out),
            (r.down_grad, r.down_grad_out),
        )[k]
        return pltpu.make_async_copy(source, target, sems[16].at[k])

    write(0).start()

    def put_gain(k, value):
        r.gain_sum[:, gain_edges[k] : gain_edges[k + 1]] = value

    def put_rows(head, low, count, rows):
        split = rows.astype(jnp.bfloat16).reshape(4, 2, count, rows.shape[-1])
        for c in range(4):
            for k in (0, 1):
                r.held[k, 2 * head + c // 2, c % 2, low : low + count] = split[c, k]

    part, gain_grad = norm_back(r.middle[...], gain[4], normed_grad)
    put_gain(4, gain_grad)
    middle_grad = r.cotangent[...].astype(jnp.float32) + part
    r.middle[...] = middle_grad
    attn_grad, gain_grad = norm_back(r.attn[...], gain[3], middle_grad)
    put_gain(3, gain_grad)
    attn_grad = attn_grad.astype(jnp.bfloat16)
    for head in range(4):
        put_rows(head, 48, 32, tn(r.mixed[:, columns_of(head)], attn_grad))
    outer.send_sib()
    keys, values = kv_parts(r)
    for head in range(4):
        mixed_grad = nt(attn_grad, rows_of_head(r.w_all, head, 48, 32)).astype(jnp.bfloat16)
        prob = r.prob[head]
        prob_grad = nt(mixed_grad, values)
        delta = jnp.sum(prob * prob_grad, axis=1, keepdims=True)
        score_grad = (prob * (prob_grad - delta)).astype(jnp.bfloat16)
        key_part = tn(score_grad, r.query[:, columns_of(head)]) * score_step
        value_part = tn(prob.astype(jnp.bfloat16), mixed_grad)
        if head == 0:
            r.kv_sum[:, :256] = key_part
            r.kv_sum[:, 256:] = value_part
        else:
            r.kv_sum[:, :256] += key_part
            r.kv_sum[:, 256:] += value_part
        r.query_grad[:, columns_of(head)] = nn(score_grad, keys) * score_step
    r.kv_part[...] = r.kv_sum[...].astype(jnp.bfloat16).reshape(2, 2, 128, 512)
    kv_sib = remote(
        r.kv_part.at[:, 1 - core], r.kv_sib.at[...], kv_out.at[0], kv_in.at[0], at.sibling
    )
    kv_sib.start()
    outer.merge()
    kv_sib.wait_recv()
    r.kv_chip[...] = (
        r.kv_part[1 - x, core].astype(jnp.float32) + r.kv_sib[1 - x].astype(jnp.float32)
    ).astype(jnp.bfloat16)
    kv_x = remote(r.kv_chip, r.kv_far, kv_out.at[1], kv_in.at[1], at.over_x)
    kv_x.start()
    normed = r.normed[...]
    query_gain = None
    for head in range(4):
        turned = turn_back(r.query_grad[:, columns_of(head)], cos, sin)
        q_raw_grad, gain_grad = norm_back(r.q_raw[:, columns_of(head)], gain[1], turned)
        query_gain = gain_grad if query_gain is None else query_gain + gain_grad
        q_raw_grad = q_raw_grad.astype(jnp.bfloat16)
        r.query[:, columns_of(head)] = q_raw_grad
        put_rows(head, 0, 32, tn(q_raw_grad, normed))
    put_gain(1, query_gain)
    outer.pair_up()
    kv_x.wait_recv()
    kv_grad = (
        r.kv_part[x, core].astype(jnp.float32)
        + r.kv_sib[x].astype(jnp.float32)
        + r.kv_far[...].astype(jnp.float32)
    )
    k_raw_grad, gain_grad = norm_back(r.k_raw[...], gain[2], turn_back(kv_grad[:, :256], cos, sin))
    put_gain(2, gain_grad)
    k_raw_grad = k_raw_grad.astype(jnp.bfloat16)
    v_raw_grad = kv_grad[:, 256:].astype(jnp.bfloat16)
    woven = (nn(k_raw_grad, pick(0)) + nn(v_raw_grad, pick(8))).astype(jnp.bfloat16)
    for head in range(4):
        put_rows(head, 32, 16, tn(woven[:, 128 * head : 128 * head + 128], normed))
    inner.send_sib()
    normed_grad = nn(k_raw_grad, r.wk[...]) + nn(v_raw_grad, r.wv[...])
    for head in range(4):
        normed_grad += nn(r.query[:, columns_of(head)], rows_of_head(r.w_all, head, 0, 32))
    part, gain_grad = norm_back(r.tokens[...].astype(jnp.float32), gain[0], normed_grad)
    put_gain(0, gain_grad)
    gain_total.send(0)
    r.token_grad[...] = r.middle[...] + part
    write(1).start()
    inner.merge()
    gain_total.take(0)
    gain_total.send(1)
    outer.collect()
    complete()
    for k in (2, 3, 4):
        write(k).start()
    inner.pair_up()
    gain_total.take(1)
    gain_total.send(2)
    inner.collect()
    gain_total.take(2)
    gain_total.send(3)
    r.o_grad[...] = outer.total()
    total = inner.total()
    r.q_grad[...] = total[:32]
    r.k_grad[...] = total[32:40]
    r.v_grad[...] = total[40:48]
    gain_total.take(3)
    device = at.f * 4 + s
    first = pl.multiple_of(device * 160 // 128 * 128, 128)
    r.gain_grad[...] = pltpu.roll(
        r.gain_sum[:, pl.ds(first, 256)], 256 - lax.rem(device, 4) * 32, 1
    )
    outer.drain()
    inner.drain()
    for k in range(5):
        write(k).wait()
    gain_total.drain()
    kv_sib.wait_send()
    kv_x.wait_send()


def layer_call(values):
    b16, f32 = jnp.bfloat16, jnp.float32
    rows, width = values["tokens"].shape
    units = values["own_gate"].shape[0]
    outs = {
        "result": ((rows, width), b16),
        "token_grad": ((rows, width), f32),
        "gain_grad": ((1, 256), f32),
        "q_grad": ((32, width), f32),
        "k_grad": ((8, width), f32),
        "v_grad": ((8, width), f32),
        "o_grad": ((32, width), f32),
        "gate_grad": ((units, width), f32),
        "up_grad": ((units, width), f32),
        "down_grad": ((units, width), f32),
    }
    scratch = {
        "gain_sum": ((1, 5120), f32),
        "w_all": ((16, 2, 80, width), b16),
        "gain_all": ((32, 1, 256), f32),
        "starts": ((rows, rows), f32),
        "cos": ((rows, rows), f32),
        "sin": ((rows, rows), f32),
        "gains": ((1, 5120), f32),
        "wk": ((256, width), b16),
        "wv": ((256, width), b16),
        "normed": ((rows, width), b16),
        "k_raw": ((rows, 256), f32),
        "q_raw": ((rows, 1024), f32),
        "query": ((rows, 1024), b16),
        "query_grad": ((rows, 1024), f32),
        "kv_all": ((4, rows, 512), b16),
        "prob": ((4, rows, 512), f32),
        "mixed": ((rows, 1024), b16),
        "attn": ((rows, width), f32),
        "middle": ((rows, width), f32),
        "peer_w": ((3, units, width), b16),
        "held": ((2, 8, 2, rows, width), b16),
        "gate_keep": ((2, 8, 2 * rows, units), b16),
        "up_keep": ((2, 8, 2 * rows, units), b16),
        "hidden_keep": ((2, 8, 2 * rows, units), b16),
        "part_own": ((rows, width), f32),
        "to_sib": ((8, rows, width), b16),
        "from_sib": ((8, rows, width), b16),
        "chip_sum": ((8, rows, width), b16),
        "from_y": ((4, rows, width), b16),
        "to_z": ((4, rows, width), b16),
        "from_z": ((2, 4, rows, width), b16),
        "from_x": ((3, units, width), b16),
        "sib_in": ((8, 2, 80, width), b16),
        "half_in": ((4, 80, width), b16),
        "xf_in": ((4, 80, width), b16),
        "yf_in": ((4, 80, width), b16),
        "zw_in": ((4, 80, width), b16),
        "kv_sum": ((4 * rows, 512), f32),
        "kv_part": ((2, 2, rows, 512), b16),
        "kv_sib": ((2, rows, 512), b16),
        "kv_chip": ((rows, 512), b16),
        "kv_far": ((rows, 512), b16),
        "gain_out": ((4, 1, 5120), f32),
        "gain_in": ((7, 1, 5120), f32),
    }
    gather_sems = [DMA((2,)), DMA((4,)), DMA((4,)), DMA((4,)), DMA((4,)), DMA((8,)), DMA((8,))]
    sum_sems = [DMA((8,)), DMA((8,)), DMA((4, 2)), DMA((4, 2)), DMA((4, 2)), DMA((2, 4, 2))]
    front_sems = gain_sems() + gather_weight_sems() + [DMA((3,))] * 4
    ffn_sems = (gather_sems + sum_sems) * 2 + [DMA((3,)), DMA((3,))]
    back_sems = [DMA((2, 4))] * 12 + [DMA((2,)), DMA((2,)), DMA((6,)), DMA((7,)), DMA((5,))]
    sems = front_sems + ffn_sems + back_sems
    large = ("result", "token_grad", "gate_grad", "up_grad", "down_grad")
    scratch.update({name: outs[name] for name in large})
    names = tuple(values) + tuple(name + "_out" if name in large else name for name in outs)
    names += tuple(scratch)

    def kernel(*refs):
        at = Place()
        r = Refs(names, refs)
        held_sems = refs[len(names) :]
        first, second = len(front_sems), len(front_sems) + len(ffn_sems)
        normed_ffn, x_weight, drain = front_phase(at, r, held_sems[:first])
        normed_grad, complete = ffn_phase(at, r, held_sems[first:second], normed_ffn, x_weight)
        back_phase(at, r, held_sems[second:], normed_grad, complete)
        drain()

    vmem = pl.BlockSpec(memory_space=pltpu.VMEM)
    out = pl.pallas_call(
        kernel,
        out_shape=tuple(jax.ShapeDtypeStruct(*spec) for spec in outs.values()),
        in_specs=[vmem] * len(values),
        out_specs=tuple(
            pl.BlockSpec(memory_space=pl.ANY) if name in large else vmem for name in outs
        ),
        scratch_shapes=[pltpu.VMEM(*spec) for spec in scratch.values()] + sems,
        compiler_params=pltpu.CompilerParams(
            collective_id=1, has_side_effects=True, vmem_limit_bytes=63 << 20
        ),
        name="layer",
    )(*values.values())
    return dict(zip(outs, out))


def settle_kernel(count, *refs):
    ins, outs, held, sems = refs[:count], refs[count : 2 * count], refs[2 * count : -1], refs[-1]
    loads = [pltpu.make_async_copy(ins[k], held[k], sems.at[0, k]) for k in range(count)]
    stores = [pltpu.make_async_copy(held[k], outs[k], sems.at[1, k]) for k in range(count)]
    for copy in loads:
        copy.start()
    for load, store in zip(loads, stores):
        load.wait()
        store.start()
    for copy in stores:
        copy.wait()


def settle(arrays):
    anywhere = pl.BlockSpec(memory_space=pl.ANY)
    return pl.pallas_call(
        partial(settle_kernel, len(arrays)),
        out_shape=tuple(jax.ShapeDtypeStruct(a.shape, a.dtype) for a in arrays),
        in_specs=[anywhere] * len(arrays),
        out_specs=tuple([anywhere] * len(arrays)),
        scratch_shapes=[pltpu.VMEM(a.shape, a.dtype) for a in arrays] + [DMA((2, len(arrays)))],
        name="settle",
    )(*arrays)


def one_kernel(
    tokens, doc_start, gains, w_query, w_key, w_value, w_out, w_gate, w_up, w_down, cotangent
):
    share = gains.shape[0]
    out = layer_call(
        {
            "tokens": tokens,
            "doc": doc_start,
            "own_gains": gains,
            "own_q": w_query.T,
            "own_k": w_key.T,
            "own_v": w_value.T,
            "own_o": w_out,
            "own_gate": w_gate.T,
            "own_up": w_up.T,
            "own_down": w_down,
            "cotangent": cotangent,
        }
    )
    names = ("result", "token_grad", "gain_grad", "q_grad", "k_grad", "v_grad", "o_grad")
    names += ("gate_grad", "up_grad", "down_grad")
    out = dict(zip(names, settle([out[name] for name in names])))
    return (
        out["result"],
        out["token_grad"],
        out["gain_grad"][0, :share],
        out["q_grad"].T,
        out["k_grad"].T,
        out["v_grad"].T,
        out["o_grad"],
        out["gate_grad"].T,
        out["up_grad"].T,
        out["down_grad"],
    )


def solution(mesh):
    in_specs = (
        P(("fsdp", "seq"), None),
        P(("fsdp", "seq")),
        P(("fsdp", "seq")),
        P(None, ("fsdp", "seq")),
        P(None, ("fsdp", "seq")),
        P(None, ("fsdp", "seq")),
        P(("fsdp", "seq"), None),
        P(None, ("fsdp", "seq")),
        P(None, ("fsdp", "seq")),
        P(("fsdp", "seq"), None),
        P(("fsdp", "seq"), None),
    )
    out_specs = (
        P(("fsdp", "seq"), None),
        P(("fsdp", "seq"), None),
        P(("fsdp", "seq")),
        P(None, ("fsdp", "seq")),
        P(None, ("fsdp", "seq")),
        P(None, ("fsdp", "seq")),
        P(("fsdp", "seq"), None),
        P(None, ("fsdp", "seq")),
        P(None, ("fsdp", "seq")),
        P(("fsdp", "seq"), None),
    )
    body = one_kernel if dict(mesh.shape) == {"fsdp": 8, "seq": 4} else local
    return jax.shard_map(body, mesh=mesh, in_specs=in_specs, out_specs=out_specs, check_vma=False)
```

```python
from functools import partial

import jax
import jax.numpy as jnp
from jax import lax
from jax.experimental import pallas as pl
from jax.experimental.pallas import tpu as pltpu
from jax.sharding import PartitionSpec as P

norm_eps = 1e-06
rope_base = 1000000.0
score_scale = 0.0625
masked_value = -1e30


def product(former, latter):
    return jnp.dot(former, latter, preferred_element_type=jnp.float32)


def inner_rows(former, latter):
    return lax.dot_general(
        former, latter, (((0,), (0,)), ((), ())), preferred_element_type=jnp.float32
    )


def outer_rows(former, latter):
    return lax.dot_general(
        former, latter, (((1,), (1,)), ((), ())), preferred_element_type=jnp.float32
    )


def scaled_norm(values, factor):
    return values * lax.rsqrt(jnp.mean(values * values, axis=-1, keepdims=True) + norm_eps) * factor


def rotate(values, cos_table, sin_table):
    half_width = values.shape[-1] // 2
    leading = values[..., :half_width]
    trailing = values[..., half_width:]
    return jnp.concatenate(
        [leading * cos_table - trailing * sin_table, trailing * cos_table + leading * sin_table],
        axis=-1,
    )


def head_norm(values, factor, cos_table, sin_table):
    return rotate(scaled_norm(values, factor), cos_table, sin_table)


def gated_unit(gate_in, up_in):
    return jax.nn.gelu(gate_in, approximate=True) * up_in


def rope_tables(places, rot_width):
    half_width = rot_width // 2
    frequency = rope_base ** (-2.0 * jnp.arange(half_width, dtype=jnp.float32) / rot_width)
    angles = places.astype(jnp.float32)[:, None] * frequency[None, :]
    return (jnp.cos(angles)[:, None, :], jnp.sin(angles)[:, None, :])


def masked_scores(queries, key_rows, bounds, offset):
    raw_scores = outer_rows(queries, key_rows) * score_scale
    query_place = offset + jnp.arange(queries.shape[0], dtype=jnp.int32)
    key_place = jnp.arange(key_rows.shape[0], dtype=jnp.int32)
    allowed = (key_place[None, :] >= bounds[:, None]) & (key_place[None, :] <= query_place[:, None])
    return jnp.where(allowed, raw_scores, masked_value)


def local(
    tokens, doc_start, gains, w_query, w_key, w_value, w_out, w_gate, w_up, w_down, cotangent
):
    tok_rows = tokens.shape[0]
    model_width = tokens.shape[1]
    run_index = lax.axis_index("seq")
    gains_all, query_w, key_w, value_w, out_w = (
        lax.all_gather(gains, ("fsdp", "seq"), axis=0, tiled=True),
        lax.all_gather(w_query, ("fsdp", "seq"), axis=1, tiled=True),
        lax.all_gather(w_key, ("fsdp", "seq"), axis=1, tiled=True),
        lax.all_gather(w_value, ("fsdp", "seq"), axis=1, tiled=True),
        lax.all_gather(w_out, ("fsdp", "seq"), axis=0, tiled=True),
    )
    gate_w, up_w, down_w = (
        lax.all_gather(w_gate, ("fsdp", "seq"), axis=1, tiled=True),
        lax.all_gather(w_up, ("fsdp", "seq"), axis=1, tiled=True),
        lax.all_gather(w_down, ("fsdp", "seq"), axis=0, tiled=True),
    )
    head_width = key_w.shape[1]
    head_count = query_w.shape[1] // head_width
    gain_values = gains_all.astype(jnp.float32)
    gain_pre = gain_values[:model_width]
    gain_query = gain_values[model_width : model_width + head_width]
    gain_key = gain_values[model_width + head_width : model_width + 2 * head_width]
    gain_post = gain_values[model_width + 2 * head_width : 2 * model_width + 2 * head_width]
    gain_pre_ffn = gain_values[2 * model_width + 2 * head_width : 3 * model_width + 2 * head_width]
    gain_post_ffn = gain_values[3 * model_width + 2 * head_width :]
    residual = tokens.astype(jnp.float32)
    normed, pre_pull = jax.vjp(scaled_norm, residual, gain_pre)
    normed_b = normed.astype(jnp.bfloat16)
    query_raw = product(normed_b, query_w).reshape(tok_rows, head_count, head_width)
    key_raw = product(normed_b, key_w).reshape(tok_rows, 1, head_width)
    value_b = product(normed_b, value_w).astype(jnp.bfloat16)
    places = run_index * tok_rows + jnp.arange(tok_rows, dtype=jnp.int32) - doc_start
    cos_table, sin_table = rope_tables(places, head_width)
    rope_norm = partial(head_norm, cos_table=cos_table, sin_table=sin_table)
    query_rot, query_pull = jax.vjp(rope_norm, query_raw, gain_query)
    key_rot, key_pull = jax.vjp(rope_norm, key_raw, gain_key)
    query_b = query_rot.reshape(tok_rows, head_count * head_width).astype(jnp.bfloat16)
    key_b = key_rot.reshape(tok_rows, head_width).astype(jnp.bfloat16)
    query_heads = lax.all_to_all(query_b, "seq", split_axis=1, concat_axis=0, tiled=True)
    key_rows, value_rows = (
        lax.all_gather(key_b, "seq", axis=0, tiled=True),
        lax.all_gather(value_b, "seq", axis=0, tiled=True),
    )
    starts = lax.all_gather(doc_start, "seq", axis=0, tiled=True)
    seq_tokens = key_rows.shape[0]
    block_rows = min(512, seq_tokens)
    block_count = seq_tokens // block_rows
    query_blocks = query_heads.reshape(block_count, block_rows, head_width)
    start_blocks = starts.reshape(block_count, block_rows)
    block_ids = jnp.arange(block_count, dtype=jnp.int32)

    def attend(block_item):
        queries, bounds, block_index = block_item
        scores = masked_scores(queries, key_rows, bounds, block_index * block_rows)
        row_max = jnp.max(scores, axis=1, keepdims=True)
        weights = jnp.exp(scores - row_max)
        row_total = jnp.sum(weights, axis=1, keepdims=True)
        probability = (weights / row_total).astype(jnp.bfloat16)
        mixed_block = product(probability, value_rows).astype(jnp.bfloat16)
        return (mixed_block, (row_max + jnp.log(row_total))[:, 0])

    mixed_blocks, lse_blocks = lax.map(attend, (query_blocks, start_blocks, block_ids))
    mixed_heads = mixed_blocks.reshape(seq_tokens, head_width)
    mixed_tokens = lax.all_to_all(mixed_heads, "seq", split_axis=0, concat_axis=1, tiled=True)
    attn_raw = product(mixed_tokens, out_w)
    attn_out, post_pull = jax.vjp(scaled_norm, attn_raw, gain_post)
    middle = residual + attn_out
    normed_ffn, pre_ffn_pull = jax.vjp(scaled_norm, middle, gain_pre_ffn)
    normed_ffn_b = normed_ffn.astype(jnp.bfloat16)
    gate_act = product(normed_ffn_b, gate_w)
    up_act = product(normed_ffn_b, up_w)
    hidden, glu_pull = jax.vjp(gated_unit, gate_act, up_act)
    hidden_b = hidden.astype(jnp.bfloat16)
    ffn_raw = product(hidden_b, down_w)
    ffn_out, post_ffn_pull = jax.vjp(scaled_norm, ffn_raw, gain_post_ffn)
    result = (middle + ffn_out).astype(jnp.bfloat16)
    gate_w, up_w, down_w = (
        lax.all_gather(w_gate, ("fsdp", "seq"), axis=1, tiled=True),
        lax.all_gather(w_up, ("fsdp", "seq"), axis=1, tiled=True),
        lax.all_gather(w_down, ("fsdp", "seq"), axis=0, tiled=True),
    )
    query_w, key_w, value_w, out_w = (
        lax.all_gather(w_query, ("fsdp", "seq"), axis=1, tiled=True),
        lax.all_gather(w_key, ("fsdp", "seq"), axis=1, tiled=True),
        lax.all_gather(w_value, ("fsdp", "seq"), axis=1, tiled=True),
        lax.all_gather(w_out, ("fsdp", "seq"), axis=0, tiled=True),
    )
    upstream = cotangent.astype(jnp.float32)
    ffn_grad, gain_post_ffn_grad = post_ffn_pull(upstream)
    ffn_grad_b = ffn_grad.astype(jnp.bfloat16)
    down_w_grad = inner_rows(hidden_b, ffn_grad_b)
    hidden_grad = outer_rows(ffn_grad_b, down_w)
    gate_grad, up_grad = glu_pull(hidden_grad)
    gate_grad_b = gate_grad.astype(jnp.bfloat16)
    up_grad_b = up_grad.astype(jnp.bfloat16)
    gate_w_grad_t = inner_rows(gate_grad_b, normed_ffn_b)
    up_w_grad_t = inner_rows(up_grad_b, normed_ffn_b)
    normed_ffn_grad = outer_rows(gate_grad_b, gate_w) + outer_rows(up_grad_b, up_w)
    middle_part, gain_pre_ffn_grad = pre_ffn_pull(normed_ffn_grad)
    middle_grad = upstream + middle_part
    attn_grad, gain_post_grad = post_pull(middle_grad)
    attn_grad_b = attn_grad.astype(jnp.bfloat16)
    out_w_grad = inner_rows(mixed_tokens, attn_grad_b)
    mixed_grad = outer_rows(attn_grad_b, out_w).astype(jnp.bfloat16)
    mixed_grad_heads = lax.all_to_all(mixed_grad, "seq", split_axis=1, concat_axis=0, tiled=True)
    grad_blocks = mixed_grad_heads.reshape(block_count, block_rows, head_width)

    def attend_back(carried, block_item):
        key_accum, value_accum = carried
        queries, bounds, block_index, lse_row, block_grad = block_item
        scores = masked_scores(queries, key_rows, bounds, block_index * block_rows)
        probability = jnp.exp(scores - lse_row[:, None])
        prob_grad = outer_rows(block_grad, value_rows)
        value_accum = value_accum + inner_rows(probability.astype(jnp.bfloat16), block_grad)
        row_delta = jnp.sum(probability * prob_grad, axis=1, keepdims=True)
        score_grad = (probability * (prob_grad - row_delta)).astype(jnp.bfloat16)
        query_grad = product(score_grad, key_rows) * score_scale
        key_accum = key_accum + inner_rows(score_grad, queries) * score_scale
        return ((key_accum, value_accum), query_grad)

    zero_rows = jnp.zeros((seq_tokens, head_width), jnp.float32)
    (key_part, value_part), query_grad_blocks = lax.scan(
        attend_back,
        (zero_rows, zero_rows),
        (query_blocks, start_blocks, block_ids, lse_blocks, grad_blocks),
    )
    key_sum, value_sum = (
        lax.psum_scatter(
            key_part.astype(jnp.bfloat16), "seq", scatter_dimension=0, tiled=True
        ).astype(jnp.float32),
        lax.psum_scatter(
            value_part.astype(jnp.bfloat16), "seq", scatter_dimension=0, tiled=True
        ).astype(jnp.float32),
    )
    query_grad_tokens = lax.all_to_all(
        query_grad_blocks.reshape(seq_tokens, head_width).astype(jnp.bfloat16),
        "seq",
        split_axis=0,
        concat_axis=1,
        tiled=True,
    ).astype(jnp.float32)
    query_raw_grad, gain_query_grad = query_pull(
        query_grad_tokens.reshape(tok_rows, head_count, head_width)
    )
    key_raw_grad, gain_key_grad = key_pull(key_sum.reshape(tok_rows, 1, head_width))
    query_raw_b = query_raw_grad.reshape(tok_rows, head_count * head_width).astype(jnp.bfloat16)
    key_raw_b = key_raw_grad.reshape(tok_rows, head_width).astype(jnp.bfloat16)
    value_raw_b = value_sum.astype(jnp.bfloat16)
    query_w_grad_t = inner_rows(query_raw_b, normed_b)
    key_w_grad_t = inner_rows(key_raw_b, normed_b)
    value_w_grad_t = inner_rows(value_raw_b, normed_b)
    normed_grad = (
        outer_rows(query_raw_b, query_w)
        + outer_rows(key_raw_b, key_w)
        + outer_rows(value_raw_b, value_w)
    )
    residual_part, gain_pre_grad = pre_pull(normed_grad)
    input_grad = middle_grad + residual_part
    gains_grad = jnp.concatenate(
        [
            gain_pre_grad,
            gain_query_grad,
            gain_key_grad,
            gain_post_grad,
            gain_pre_ffn_grad,
            gain_post_ffn_grad,
        ]
    )
    shares = (
        lax.psum_scatter(gains_grad, ("fsdp", "seq"), scatter_dimension=0, tiled=True),
        lax.psum_scatter(query_w_grad_t, ("fsdp", "seq"), scatter_dimension=0, tiled=True),
        lax.psum_scatter(key_w_grad_t, ("fsdp", "seq"), scatter_dimension=0, tiled=True),
        lax.psum_scatter(value_w_grad_t, ("fsdp", "seq"), scatter_dimension=0, tiled=True),
        lax.psum_scatter(out_w_grad, ("fsdp", "seq"), scatter_dimension=0, tiled=True),
        lax.psum_scatter(gate_w_grad_t, ("fsdp", "seq"), scatter_dimension=0, tiled=True),
        lax.psum_scatter(up_w_grad_t, ("fsdp", "seq"), scatter_dimension=0, tiled=True),
        lax.psum_scatter(down_w_grad, ("fsdp", "seq"), scatter_dimension=0, tiled=True),
    )
    return (
        result,
        input_grad,
        shares[0],
        shares[1].T,
        shares[2].T,
        shares[3].T,
        shares[4],
        shares[5].T,
        shares[6].T,
        shares[7],
    )


gelu_c = 0.7978845608028654
MESH = pl.DeviceIdType.MESH
DMA = pltpu.SemaphoreType.DMA


def nt(former, latter):
    return lax.dot_general(
        former, latter, (((1,), (1,)), ((), ())), preferred_element_type=jnp.float32
    )


def nn(former, latter):
    return lax.dot_general(
        former, latter, (((1,), (0,)), ((), ())), preferred_element_type=jnp.float32
    )


def tn(former, latter):
    return lax.dot_general(
        former, latter, (((0,), (0,)), ((), ())), preferred_element_type=jnp.float32
    )


class Place:
    def __init__(self):
        self.f = lax.axis_index("fsdp")
        self.s = lax.axis_index("seq")
        self.z = self.f // 2
        self.y = lax.rem(self.f, 2)
        self.core = lax.rem(self.s, 2)
        self.high = self.z // 2
        self.inner = self.z * (3 - self.z) == 2
        self.outer = self.z * (3 - self.z) == 0
        self.sibling = (self.f, self.s + 1 - 2 * self.core)
        self.over_x = (self.f, lax.rem(self.s + 2, 4))
        self.over_y = (self.f + 1 - 2 * self.y, self.s)
        self.toward = 1 - 2 * self.high
        self.step_first = self.toward * (1 - self.z * (3 - self.z))

    def at_z(self, z):
        return (z * 2 + self.y, self.s)

    def source(self, j):
        last = j // 3
        middle = j // 2 - last
        none = (3 - j) // 3
        first = 1 - last - middle - none
        return (
            none * self.z
            + first * (1 - self.z + 4 * self.high)
            + middle * (2 - self.high)
            + last * (3 - 3 * self.high)
        )


def remote(source, target, send_sem, recv_sem, device):
    return pltpu.make_async_remote_copy(
        src_ref=source,
        dst_ref=target,
        send_sem=send_sem,
        recv_sem=recv_sem,
        device_id=device,
        device_id_type=MESH,
    )


def greet(partners):
    entry = pltpu.get_barrier_semaphore()
    for partner in partners:
        pl.semaphore_signal(entry, inc=1, device_id=partner, device_id_type=MESH)
    return entry


def exchange_pass(at, held, gather_sems, sum_sems, sum_bufs, part_own, compute, lag=0, ready=None, then=()):
    z_own, z_next, z_in, y_out, y_in, c_out, c_in = gather_sems
    t_out, t_in, v_out, v_in, w_out, w_in = sum_sems
    to_sib, from_sib, chip_sum, from_y, to_z, from_z = sum_bufs
    f, core = at.f, at.core

    def block(chip):
        return held.at[chip, core]

    def over(chip, outgoing, incoming, device):
        return remote(block(chip), block(chip), outgoing, incoming, device)

    def own_z(step, slot):
        return over(f, z_own.at[slot], z_in.at[at.z], at.at_z(at.z + step))

    def own_z_toward():
        return own_z(at.toward, 0)

    def own_z_away():
        return own_z(-at.toward, 1)

    def pass_z(src, step):
        return over(src * 2 + at.y, z_next.at[src], z_in.at[src], at.at_z(at.z + step))

    def pass_y(src):
        return over(src * 2 + at.y, y_out.at[src], y_in.at[src], at.over_y)

    def pass_sib(chip):
        return over(chip, c_out.at[chip], c_in.at[chip], at.sibling)

    own_z_toward().start()

    @pl.when(at.inner)
    def _():
        own_z_away().start()

    pass_y(at.z).start()
    pass_sib(f).start()

    def from_z_block(src):
        return over(src * 2 + at.y, z_next.at[src], z_in.at[src], at.at_z(src))

    def take_z(j, step):
        src = at.source(j)
        from_z_block(src).wait_recv()

        @pl.when(at.inner)
        def _():
            pass_z(src, step).start()

        pass_y(src).start()
        pass_sib(src * 2 + at.y).start()

    def chip_of(i):
        return at.source(i // 2) * 2 + lax.rem(at.y + lax.rem(i, 2), 2)

    def sib_sum(i):
        return remote(to_sib.at[i], from_sib.at[i], t_out.at[i], t_in.at[i], at.sibling)

    rows = part_own.shape[0] // 4
    pieces = [pl.ds(k * rows, rows) for k in range(4)]

    def y_sum(i, k):
        return remote(
            chip_sum.at[i, pieces[k]],
            from_y.at[i // 2, pieces[k]],
            v_out.at[i // 2, k],
            v_in.at[i // 2, k],
            at.over_y,
        )

    def send_y(i):
        for k in range(4):
            y_sum(i, k).start()

    def finish_chip(i):
        sib_sum(i).wait_recv()
        chip_sum[i] = (part_own[...] + from_sib[i].astype(jnp.float32)).astype(jnp.bfloat16)

    def arrivals(i):
        @pl.when(i == 1)
        def _():
            take_z(1, at.toward)

            @pl.when(at.inner)
            def _():
                take_z(2, -at.toward)

        @pl.when((i == 3) & at.outer)
        def _():
            take_z(2, -at.toward)

        @pl.when(((i == 3) & at.inner) | ((i == 5) & at.outer))
        def _():
            take_z(3, -at.toward)

        @pl.when(lax.rem(i, 2) == 1)
        def _():
            pass_y(at.source(i // 2)).wait_recv()
            pass_sib(chip_of(i)).start()

    def one_chip(i):
        chip = chip_of(i)
        pass_sib(chip).wait_recv()
        own_part, sib_part = compute(chip)
        to_sib[i] = sib_part.astype(jnp.bfloat16)
        sib_sum(i).start()

        @pl.when(i > 0)
        def _():
            finish_chip(i - 1)

        part_own[...] = own_part

    def step(i, carried):
        @pl.when(i < 8)
        def _():
            arrivals(i)

        @pl.when(i == 7 + lag)
        def _():
            send_y(5)

        if ready is not None:

            @pl.when(i == lag)
            def _():
                ready()

        @pl.when(i >= lag)
        def _():
            one_chip(i - lag)

        return carried

    lax.fori_loop(0, 8 + lag, step, 0)
    finish_chip(7)
    for j in (3, 1, 0):
        send_y(2 * j + 1)
    later = list(then) + [lambda: None] * 4
    later[0]()

    def z_sum(target, direction, k, device=None):
        slot = (direction + 1) // 2
        return remote(
            to_z.at[target, pieces[k]],
            from_z.at[slot, target, pieces[k]],
            w_out.at[target, k],
            w_in.at[slot, target, k],
            at.at_z(at.z + direction) if device is None else device,
        )

    def z_arrival(target, direction, k):
        return z_sum(target, direction, k, at.at_z(lax.rem(at.z - direction + 4, 4)))

    def direction_of(j):
        return at.step_first if j == 1 else at.toward

    for place, j in enumerate((2, 3, 1)):
        target, direction = at.source(j), direction_of(j)
        for k, piece in enumerate(pieces):
            y_sum(2 * j + 1, k).wait_recv()
            mine = chip_sum[2 * j, piece].astype(jnp.float32) + from_y[j, piece].astype(
                jnp.float32
            )

            @pl.when(at.outer)
            def _():
                to_z[target, piece] = mine.astype(jnp.bfloat16)

            @pl.when(at.inner)
            def _():
                z_arrival(target, direction, k).wait_recv()
                ahead = from_z[(direction + 1) // 2, target, piece].astype(jnp.float32)
                to_z[target, piece] = (mine + ahead).astype(jnp.bfloat16)

            z_sum(target, direction, k).start()
        later[1 + place]()

    def finish():
        for k, piece in enumerate(pieces):
            y_sum(1, k).wait_recv()
            part_own[piece] = chip_sum[0, piece].astype(jnp.float32) + from_y[0, piece].astype(
                jnp.float32
            )
            z_arrival(at.z, -at.toward, k).wait_recv()
            part_own[piece] += from_z[(1 - at.toward) // 2, at.z, piece].astype(jnp.float32)

            @pl.when(at.inner)
            def _():
                z_arrival(at.z, at.toward, k).wait_recv()
                part_own[piece] += from_z[(1 + at.toward) // 2, at.z, piece].astype(jnp.float32)

        return part_own[...]

    def drain():
        own_z_toward().wait_send()

        @pl.when(at.inner)
        def _():
            own_z_away().wait_send()
            for j in (1, 2, 3):
                from_z_block(at.source(j)).wait_send()

        def drain_chip(i, carried):
            pass_sib(chip_of(i)).wait_send()
            sib_sum(i).wait_send()

            @pl.when(lax.rem(i, 2) == 1)
            def _():
                pass_y(at.source(i // 2)).wait_send()
                for k in range(4):
                    y_sum(i, k).wait_send()

            return carried

        lax.fori_loop(0, 8, drain_chip, 0)
        for j in (1, 2, 3):
            for k in range(4):
                z_sum(at.source(j), direction_of(j), k).wait_send()

    return finish, drain


gain_edges = (0, 1152, 1408, 1664, 2816, 3968, 5120)
score_step = 0.0625
log_base = 13.815510557964274
hidden_score = -1e30


def shape_spec(shape, dtype):
    return jax.ShapeDtypeStruct(shape, dtype)


def rms_scale(values):
    return lax.rsqrt(jnp.mean(values * values, axis=-1, keepdims=True) + norm_eps)


def norm_back(values, gain, upstream):
    scale = rms_scale(values)
    weighted = upstream * gain
    inner = jnp.mean(weighted * values, axis=-1, keepdims=True)
    back = scale * weighted - values * (scale * scale * scale * inner)
    return back, jnp.sum(upstream * values * scale, axis=0, keepdims=True)


def pick(offset):
    row = lax.broadcasted_iota(jnp.int32, (256, 512), 0)
    column = lax.broadcasted_iota(jnp.int32, (256, 512), 1)
    wanted = row // 8 * 16 + lax.rem(row, 8) + offset
    return jnp.where(column == wanted, 1.0, 0.0).astype(jnp.bfloat16)


def rows_of_all(w_all, low, count):
    return jnp.concatenate(
        [w_all[d // 2, d % 2, low : low + count] for d in range(32)], axis=0
    )


def rows_of_head(w_all, head, low, count):
    return jnp.concatenate(
        [w_all[d // 2, d % 2, low : low + count] for d in range(8 * head, 8 * head + 8)], axis=0
    )


class GainGather:
    def __init__(self, at, held, sems):
        self.at, self.held = at, held
        self.out, self.inc, self.z_out, self.z_in = sems
        x = at.s // 2
        self.spans = (
            (at.f * 4 + at.s, 1, at.sibling),
            (at.f * 4 + 2 * x, 2, at.over_x),
            (at.f * 4, 4, at.over_y),
        )

    def stage(self, k):
        first, count, partner = self.spans[k]
        span = self.held.at[pl.ds(first, count)]
        return remote(span, span, self.out.at[k], self.inc.at[k], partner)

    def last(self, src, j, device):
        span = self.held.at[pl.ds(src * 8, 8)]
        return remote(span, span, self.z_out.at[j], self.z_in.at[src], device)

    def send(self, k):
        at = self.at
        if k < 3:
            self.stage(k).start()
        else:
            for j in (1, 2, 3):
                self.last(at.z, j, at.at_z(at.source(j))).start()

    def take(self, k):
        at = self.at
        if k < 3:
            self.stage(k).wait_recv()
        else:
            for j in (1, 2, 3):
                self.last(at.source(j), j, at.at_z(at.source(j))).wait_recv()

    def drain(self):
        at = self.at
        for k in range(3):
            self.stage(k).wait_send()
        for j in (1, 2, 3):
            self.last(at.z, j, at.at_z(at.source(j))).wait_send()


class WeightGather:
    def __init__(self, at, w_all, sems, part, low, high):
        self.at, self.w_all, self.part = at, w_all, part
        (
            self.x_out,
            self.x_in,
            self.first_out,
            self.first_in,
            self.z_own,
            self.z_next,
            self.z_in,
            self.y_out,
            self.y_in,
            self.s_out,
            self.s_in,
        ) = sems
        self.rows = pl.ds(low, high - low)
        self.x = at.s // 2

    def one(self, y, x, outgoing, incoming, device):
        span = self.w_all.at[(self.at.z * 2 + y) * 2 + x, self.at.core, self.rows]
        return remote(span, span, outgoing, incoming, device)

    def pair(self, z, y, outgoing, incoming, device):
        span = self.w_all.at[pl.ds((z * 2 + y) * 2, 2), self.at.core, self.rows]
        return remote(span, span, outgoing, incoming, device)

    def x_copy(self, x):
        p, at = self.part, self.at
        return self.one(at.y, x, self.x_out.at[p], self.x_in.at[p], at.over_x)

    def y_first(self, y, x):
        p, at = self.part, self.at
        return self.one(y, x, self.first_out.at[p, x], self.first_in.at[p, x], at.over_y)

    def own(self, step, slot):
        p, at = self.part, self.at
        return self.pair(
            at.z, at.y, self.z_own.at[p, slot], self.z_in.at[p, at.z], at.at_z(at.z + step)
        )

    def passed(self, src, device):
        p = self.part
        return self.pair(src, self.at.y, self.z_next.at[p, src], self.z_in.at[p, src], device)

    def y_pair(self, src, y):
        p = self.part
        return self.pair(src, y, self.y_out.at[p, src], self.y_in.at[p, src], self.at.over_y)

    def sib(self, src):
        span = self.w_all.at[pl.ds(src * 4, 4), self.at.core, self.rows]
        p = self.part
        return remote(span, span, self.s_out.at[p, src], self.s_in.at[p, src], self.at.sibling)

    def begin(self):
        self.x_copy(self.x).start()
        self.y_first(self.at.y, self.x).start()

    def spread(self):
        at = self.at
        self.x_copy(1 - self.x).wait_recv()
        self.own(at.toward, 0).start()

        @pl.when(at.inner)
        def _():
            self.own(-at.toward, 1).start()

        self.y_first(at.y, 1 - self.x).start()

    def take(self, j):
        at = self.at
        src = at.source(j)
        self.passed(src, at.at_z(src)).wait_recv()

        @pl.when(at.inner)
        def _():
            self.passed(src, at.at_z(at.z + (at.toward if j == 1 else -at.toward))).start()

        self.y_pair(src, at.y).start()

    def close(self, j):
        src = self.at.source(j)
        if j == 0:
            for x in (0, 1):
                self.y_first(1 - self.at.y, x).wait_recv()
        else:
            self.y_pair(src, 1 - self.at.y).wait_recv()
        self.sib(src).start()

    def walk(self, between=()):
        at = self.at
        extra = list(between) + [lambda: None] * 3
        self.take(1)

        @pl.when(at.inner)
        def _():
            self.take(2)

        extra[0]()
        self.close(0)

        @pl.when(at.inner)
        def _():
            self.take(3)

        @pl.when(at.outer)
        def _():
            self.take(2)

        extra[1]()
        self.close(1)

        @pl.when(at.outer)
        def _():
            self.take(3)

        extra[2]()
        self.close(2)
        self.close(3)

    def settle(self):
        for j in range(4):
            self.sib(self.at.source(j)).wait_recv()

    def drain(self):
        at = self.at
        self.x_copy(self.x).wait_send()
        for x in (0, 1):
            self.y_first(at.y, x).wait_send()
        self.own(at.toward, 0).wait_send()

        @pl.when(at.inner)
        def _():
            self.own(-at.toward, 1).wait_send()
            for j in (1, 2, 3):
                self.passed(at.source(j), at.at_z(at.source(j))).wait_send()

        for j in range(4):
            src = at.source(j)
            if j > 0:
                self.y_pair(src, at.y).wait_send()
            self.sib(src).wait_send()


def gather_weight_sems():
    return [DMA((2,)), DMA((2,))] + [DMA((2, 2))] * 3 + [DMA((2, 4))] * 6


def gain_sems():
    return [DMA((3,)), DMA((3,)), DMA((4,)), DMA((4,))]


def turn(values, cos, sin):
    a, b = values[:, :128], values[:, 128:]
    return jnp.concatenate([a * cos - b * sin, b * cos + a * sin], axis=1)


def turn_back(values, cos, sin):
    a, b = values[:, :128], values[:, 128:]
    return jnp.concatenate([a * cos + b * sin, b * cos - a * sin], axis=1)


class WeightReturn:
    def __init__(self, at, held, bufs, sems, part, low, middle, high):
        self.at, self.held, self.part = at, held, part
        self.sib_in, self.xh_in, self.yh_in, self.xf_in, self.yf_in, self.z_in = bufs
        (
            self.so,
            self.si,
            self.xho,
            self.xhi,
            self.yho,
            self.yhi,
            self.xfo,
            self.xfi,
            self.yfo,
            self.yfi,
            self.zo,
            self.zi,
        ) = sems
        self.low, self.middle, self.high = low, middle, high
        self.x = at.s // 2
        self.rows = pl.ds(low, high - low)
        self.top = pl.ds(low, middle - low)
        self.bottom = pl.ds(middle, high - middle)
        self.by_x, self.by_y = middle > low, high > middle

    def mine(self, z, y, x, rows):
        return self.held.at[self.at.core, z * 2 + y, x, rows]

    def sib(self, z):
        pair = pl.ds(z * 2, 2)
        p = self.part
        return remote(
            self.held.at[1 - self.at.core, pair, :, self.rows],
            self.sib_in.at[pair, :, self.rows],
            self.so.at[p, z],
            self.si.at[p, z],
            self.at.sibling,
        )

    def x_half(self, z):
        p = self.part
        source = self.mine(z, 1 - self.at.y, 1 - self.x, self.top)
        return remote(
            source, self.xh_in.at[z, self.top], self.xho.at[p, z], self.xhi.at[p, z], self.at.over_x
        )

    def y_half(self, z):
        p = self.part
        source = self.mine(z, 1 - self.at.y, 1 - self.x, self.bottom)
        return remote(
            source,
            self.yh_in.at[z, self.bottom],
            self.yho.at[p, z],
            self.yhi.at[p, z],
            self.at.over_y,
        )

    def x_full(self, z):
        p = self.part
        source = self.mine(z, self.at.y, 1 - self.x, self.rows)
        return remote(
            source,
            self.xf_in.at[z, self.rows],
            self.xfo.at[p, z],
            self.xfi.at[p, z],
            self.at.over_x,
        )

    def y_full(self, z):
        p = self.part
        source = self.mine(z, 1 - self.at.y, self.x, self.rows)
        return remote(
            source,
            self.yf_in.at[z, self.rows],
            self.yfo.at[p, z],
            self.yfi.at[p, z],
            self.at.over_y,
        )

    def z_part(self, z):
        p = self.part
        source = self.mine(z, self.at.y, self.x, self.rows)
        return remote(
            source,
            self.z_in.at[self.at.z, self.rows],
            self.zo.at[p, z],
            self.zi.at[p, self.at.z],
            self.at.at_z(z),
        )

    def z_arrival(self, z):
        p = self.part
        source = self.mine(z, self.at.y, self.x, self.rows)
        return remote(
            source,
            self.z_in.at[z, self.rows],
            self.zo.at[p, z],
            self.zi.at[p, z],
            self.at.at_z(z),
        )

    def add(self, z, y, x, rows, more):
        core, f = self.at.core, z * 2 + y
        self.held[core, f, x, rows] = (
            self.held[core, f, x, rows].astype(jnp.float32) + more.astype(jnp.float32)
        ).astype(jnp.bfloat16)

    def merge(self):
        for j in (3, 2, 1, 0):
            z = self.at.source(j)
            self.sib(z).wait_recv()
            for y in (0, 1):
                for x in (0, 1):
                    self.add(z, y, x, self.rows, self.sib_in[z * 2 + y, x, self.rows])
            (self.x_half if self.by_x else self.y_full)(z).start()
            (self.y_half if self.by_y else self.x_full)(z).start()

    def pair_up(self):
        at = self.at
        for j in (3, 2, 1, 0):
            z = at.source(j)
            if self.by_x:
                self.x_half(z).wait_recv()
                self.add(z, 1 - at.y, self.x, self.top, self.xh_in[z, self.top])
                self.y_full(z).start()
            if self.by_y:
                self.y_half(z).wait_recv()
                self.add(z, at.y, 1 - self.x, self.bottom, self.yh_in[z, self.bottom])
                self.x_full(z).start()

    def collect(self):
        at = self.at
        for j in (3, 2, 1, 0):
            z = at.source(j)
            self.y_full(z).wait_recv()
            self.x_full(z).wait_recv()
            more = self.yf_in[z, self.rows].astype(jnp.float32) + self.xf_in[
                z, self.rows
            ].astype(jnp.float32)
            self.add(z, at.y, self.x, self.rows, more)
            if j > 0:
                self.z_part(z).start()

    def total(self):
        at = self.at
        value = self.held[at.core, at.f, self.x, self.rows].astype(jnp.float32)
        for j in (3, 2, 1):
            z = at.source(j)
            self.z_arrival(z).wait_recv()
            value = value + self.z_in[z, self.rows].astype(jnp.float32)
        return value

    def drain(self):
        for j in range(4):
            z = self.at.source(j)
            for copy in (self.sib, self.x_full, self.y_full):
                copy(z).wait_send()
            if self.by_x:
                self.x_half(z).wait_send()
            if self.by_y:
                self.y_half(z).wait_send()
            if j > 0:
                self.z_part(z).wait_send()


class GainSum:
    def __init__(self, at, row, outgoing, incoming, sems):
        self.at, self.row, self.outgoing, self.incoming = at, row, outgoing, incoming
        self.out, self.inc = sems
        self.partners = (at.sibling, at.over_x, at.over_y)

    def stage(self, k):
        return remote(
            self.outgoing.at[k],
            self.incoming.at[k],
            self.out.at[k],
            self.inc.at[k],
            self.partners[k],
        )

    def last(self, src, j, device):
        return remote(
            self.outgoing.at[3],
            self.incoming.at[3 + src],
            self.out.at[2 + j],
            self.inc.at[3 + src],
            device,
        )

    def send(self, k):
        self.outgoing[k] = self.row[...]
        if k < 3:
            self.stage(k).start()
        else:
            for j in (1, 2, 3):
                self.last(self.at.z, j, self.at.at_z(self.at.source(j))).start()

    def take(self, k):
        if k < 3:
            self.stage(k).wait_recv()
            self.row[...] += self.incoming[k]
        else:
            for j in (1, 2, 3):
                src = self.at.source(j)
                self.last(src, j, self.at.at_z(src)).wait_recv()
                self.row[...] += self.incoming[3 + src]

    def drain(self):
        for k in range(3):
            self.stage(k).wait_send()
        for j in (1, 2, 3):
            self.last(self.at.z, j, self.at.at_z(self.at.source(j))).wait_send()


class Refs:
    def __init__(self, names, refs):
        for name, ref in zip(names, refs):
            setattr(self, name, ref)


def columns_of(head):
    return slice(256 * head, 256 * head + 256)


def front_phase(at, r, sems):
    core, s = at.core, at.s
    gathered = GainGather(at, r.gain_all, sems[:4])
    w_sems = sems[4:15]
    kv_out, kv_in, x_out, x_in = sems[15:19]
    w_all, kv_all = r.w_all, r.kv_all
    early = WeightGather(at, w_all, w_sems, 0, 0, 48)
    late = WeightGather(at, w_all, w_sems, 1, 48, 80)
    chip = at.f * 2 + s // 2
    entry = greet(
        [at.sibling, at.over_x, at.over_y]
        + [at.at_z(lax.rem(at.z + step, 4)) for step in (1, 2, 3)]
    )
    w_all[chip, core, 0:32] = r.own_q[...]
    w_all[chip, core, 32:48] = jnp.concatenate(
        [r.own_k[...].astype(jnp.float32), r.own_v[...].astype(jnp.float32)], axis=0
    ).astype(jnp.bfloat16)
    w_all[chip, core, 48:80] = r.own_o[...]
    device = at.f * 4 + s
    share = jnp.concatenate(
        [r.own_gains[...].astype(jnp.float32).reshape(1, 160), jnp.zeros((1, 96), jnp.float32)],
        axis=1,
    )
    r.gain_all[device] = pltpu.roll(share, lax.rem(device, 4) * 32, 1)
    pl.semaphore_wait(entry, 6)
    def x_weight(k):
        ref = (r.own_gate, r.own_up, r.own_down)[k]
        return remote(ref, r.peer_w.at[k], x_out.at[k], x_in.at[k], at.over_x)

    def gain_step(k):
        def step():
            gathered.take(k)
            if k < 3:
                gathered.send(k + 1)

        return step

    gathered.send(0)
    early.begin()
    late.begin()
    gain_step(0)()
    early.spread()
    x_weight(0).start()
    x_weight(1).start()
    gain_step(1)()
    starts = jnp.broadcast_to(r.doc[...].astype(jnp.float32).reshape(1, 128), (128, 128)).T
    r.starts[...] = starts
    place = (lax.broadcasted_iota(jnp.int32, (128, 128), 0) + s * 128).astype(jnp.float32)
    step = lax.broadcasted_iota(jnp.int32, (128, 128), 1).astype(jnp.float32)
    angle = (place - starts) * jnp.exp(step * (-2.0 / 256 * log_base))
    r.cos[...] = jnp.cos(angle)
    r.sin[...] = jnp.sin(angle)

    def first_norm():
        late.spread()
        placed = r.gain_all[...].reshape(32, 256)
        pieces = []
        for m in range(8):
            for k in range(5):
                piece = None
                if k < 4:
                    piece = placed[4 * m + k : 4 * m + k + 1, :128]
                if k > 0:
                    other = placed[4 * m + k - 1 : 4 * m + k, 128:]
                    piece = other if piece is None else piece + other
                pieces.append(piece)
        r.gains[...] = jnp.concatenate(pieces, axis=1)
        gain = gain_parts(r)
        residual = r.tokens[...].astype(jnp.float32)
        r.normed[...] = (residual * rms_scale(residual) * gain[0]).astype(jnp.bfloat16)
    early.walk((gain_step(2), gain_step(3), first_norm))
    gain = gain_parts(r)
    early.settle()
    normed = r.normed[...]
    cos, sin = r.cos[...], r.sin[...]
    mixed_rows = rows_of_all(w_all, 32, 16)
    r.wk[...] = nn(pick(0), mixed_rows).astype(jnp.bfloat16)
    r.wv[...] = nn(pick(8), mixed_rows).astype(jnp.bfloat16)
    k_raw = nt(normed, r.wk[...])
    r.k_raw[...] = k_raw
    key = turn(k_raw * rms_scale(k_raw) * gain[2], cos, sin)
    kv_all[s, :, :256] = key.astype(jnp.bfloat16)
    kv_all[s, :, 256:] = nt(normed, r.wv[...]).astype(jnp.bfloat16)

    def kv_copy(which, slot, device):
        return remote(kv_all.at[slot], kv_all.at[slot], kv_out.at[which], kv_in.at[which], device)

    peer_slot = lax.rem(s + 2, 4)
    kv_copy(0, s, at.over_x).start()
    kv_copy(1, s, at.sibling).start()

    def one_query(head):
        q_raw = nt(normed, rows_of_head(w_all, head, 0, 32))
        r.q_raw[:, columns_of(head)] = q_raw
        query = turn(q_raw * rms_scale(q_raw) * gain[1], cos, sin)
        r.query[:, columns_of(head)] = query.astype(jnp.bfloat16)

    def pass_kv():
        one_query(0)
        kv_copy(0, peer_slot, at.over_x).wait_recv()
        kv_copy(2, peer_slot, at.sibling).start()
        x_weight(2).start()
        one_query(1)

    late.walk((pass_kv, lambda: one_query(2), lambda: one_query(3)))
    other = s + 1 - 2 * core
    kv_copy(1, other, at.sibling).wait_recv()
    kv_copy(2, lax.rem(other + 2, 4), at.sibling).wait_recv()
    keys, values = kv_parts(r)
    key_place = lax.broadcasted_iota(jnp.int32, (128, 512), 1)
    query_place = lax.broadcasted_iota(jnp.int32, (128, 512), 0) + s * 128
    starts = jnp.concatenate([r.starts[...]] * 4, axis=1).astype(jnp.int32)
    allowed = (key_place >= starts) & (key_place <= query_place)
    for head in range(4):
        raw = nt(r.query[:, columns_of(head)], keys) * score_step
        scores = jnp.where(allowed, raw, hidden_score)
        weights = jnp.exp(scores - jnp.max(scores, axis=1, keepdims=True))
        prob = weights / jnp.sum(weights, axis=1, keepdims=True)
        r.prob[head] = prob
        mixed = nn(prob.astype(jnp.bfloat16), values).astype(jnp.bfloat16)
        r.mixed[:, columns_of(head)] = mixed
    late.settle()
    attn = nn(r.mixed[...], rows_of_all(w_all, 48, 32))
    r.attn[...] = attn
    middle = r.tokens[...].astype(jnp.float32) + attn * rms_scale(attn) * gain[3]
    r.middle[...] = middle
    normed_ffn = (middle * rms_scale(middle) * gain[4]).astype(jnp.bfloat16)

    def drain():
        gathered.drain()
        early.drain()
        late.drain()
        kv_copy(0, s, at.over_x).wait_send()
        kv_copy(1, s, at.sibling).wait_send()
        kv_copy(2, peer_slot, at.sibling).wait_send()

    return normed_ffn, x_weight, drain


def gain_parts(r):
    return [r.gains[:, a:b] for a, b in zip(gain_edges[:-1], gain_edges[1:])]


def kv_parts(r):
    return r.kv_all[...].reshape(512, 512)[:, :256], r.kv_all[...].reshape(512, 512)[:, 256:]


def ffn_phase(at, r, sems, normed_ffn, x_weight):
    core = at.core
    fwd_gather, fwd_sum = sems[:7], sems[7:13]
    bwd_gather, bwd_sum = sems[13:20], sems[20:26]
    x_out, x_in = sems[26:28]
    sum_bufs = (r.to_sib, r.from_sib, r.chip_sum, r.from_y, r.to_z, r.from_z)
    normed_all, grad_all = r.held.at[0], r.held.at[1]
    gates = (r.own_gate, r.peer_w.at[0])
    ups = (r.own_up, r.peer_w.at[1])
    downs = (r.own_down, r.peer_w.at[2])
    r.held[0, at.f, core] = normed_ffn

    def rows_of(which, chip):
        return jnp.concatenate([r.held[which, chip, core], r.held[which, chip, 1 - core]], axis=0)

    def weights_here():
        for k in range(3):
            x_weight(k).wait()

    def forward(chip):
        rows = rows_of(0, chip)
        total = None
        for half in (0, 1):
            gate = nt(rows, gates[half][...])
            up = nt(rows, ups[half][...])
            r.gate_keep[half, chip] = gate.astype(jnp.bfloat16)
            r.up_keep[half, chip] = up.astype(jnp.bfloat16)
            bend = jnp.tanh(gelu_c * (gate + 0.044715 * gate * gate * gate))
            hidden = (0.5 * gate * (1.0 + bend) * up).astype(jnp.bfloat16)
            r.hidden_keep[half, chip] = hidden
            part = nn(hidden, downs[half][...])
            total = part if total is None else total + part
        return total[:128], total[128:]

    finish, drain = exchange_pass(
        at, normed_all, fwd_gather, fwd_sum, sum_bufs, r.part_own, forward, 0, weights_here
    )
    gain = gain_parts(r)[5]
    upstream = r.cotangent[...].astype(jnp.float32)
    ffn_grad, _ = norm_back(finish(), gain, upstream)
    r.held[1, at.f, core] = ffn_grad.astype(jnp.bfloat16)
    drain_forward = drain

    def write_result():
        ffn_raw = r.part_own[...]
        normed = ffn_raw * rms_scale(ffn_raw)
        r.result[...] = (r.middle[...] + normed * gain).astype(jnp.bfloat16)
        share = jnp.sum(r.cotangent[...].astype(jnp.float32) * normed, axis=0, keepdims=True)
        r.gain_sum[:, gain_edges[5] : gain_edges[6]] = share
        drain_forward()

    own_grads = (r.gate_grad, r.up_grad, r.down_grad)

    def backward(chip):
        rows = rows_of(1, chip)
        total = None
        for half in (0, 1):
            dhidden = nt(rows, downs[half][...])
            gate = r.gate_keep[half, chip].astype(jnp.float32)
            up = r.up_keep[half, chip].astype(jnp.float32)
            square = gate * gate
            bend = jnp.tanh(gelu_c * (gate + 0.044715 * square * gate))
            unit = 0.5 * gate * (1.0 + bend)
            slope = 0.5 * (1.0 + bend) + 0.5 * gate * (1.0 - bend * bend) * (
                gelu_c * (1.0 + 3 * 0.044715 * square)
            )
            dgate = (dhidden * up * slope).astype(jnp.bfloat16)
            dup = (dhidden * unit).astype(jnp.bfloat16)
            part = nn(dgate, gates[half][...]) + nn(dup, ups[half][...])
            total = part if total is None else total + part
            r.gate_keep[half, chip] = dgate
            r.up_keep[half, chip] = dup
        return total[:128], total[128:]

    def x_copy(k):
        return remote(r.peer_w.at[k], r.from_x.at[k], x_out.at[k], x_in.at[k], at.over_x)

    kept = ((r.gate_keep, 0), (r.up_keep, 0), (r.hidden_keep, 1))

    def weight_grad(k, half):
        left, which = kept[k]
        total = None
        for chip in range(8):
            part = tn(left[half, chip], rows_of(which, chip))
            total = part if total is None else total + part
        return total

    def peers():
        for k in range(3):
            r.peer_w[k] = weight_grad(k, 1).astype(jnp.bfloat16)
            x_copy(k).start()

    def own(k):
        def step():
            own_grads[k][...] = weight_grad(k, 0)

        return step

    finish, drain = exchange_pass(
        at,
        grad_all,
        bwd_gather,
        bwd_sum,
        sum_bufs,
        r.part_own,
        backward,
        0,
        write_result,
        (peers, own(0), own(1), own(2)),
    )
    normed_grad = finish()
    drain()

    def complete():
        for k in range(3):
            x_copy(k).wait()
            own_grads[k][...] += r.from_x[k].astype(jnp.float32)

    return normed_grad, complete


def back_phase(at, r, sems, normed_grad, complete):
    core, s = at.core, at.s
    x = s // 2
    gain = gain_parts(r)
    cos, sin = r.cos[...], r.sin[...]
    bufs = (r.sib_in, r.half_in, r.half_in, r.xf_in, r.yf_in, r.zw_in)
    w_sems = sems[:12]
    kv_out, kv_in = sems[12:14]
    outer = WeightReturn(at, r.held, bufs, w_sems, 1, 48, 64, 80)
    inner = WeightReturn(at, r.held, bufs, w_sems, 0, 0, 16, 48)
    gain_total = GainSum(at, r.gain_sum, r.gain_out, r.gain_in, sems[14:16])

    def write(k):
        source, target = (
            (r.result, r.result_out),
            (r.token_grad, r.token_grad_out),
            (r.gate_grad, r.gate_grad_out),
            (r.up_grad, r.up_grad_out),
            (r.down_grad, r.down_grad_out),
        )[k]
        return pltpu.make_async_copy(source, target, sems[16].at[k])

    write(0).start()

    def put_gain(k, value):
        r.gain_sum[:, gain_edges[k] : gain_edges[k + 1]] = value

    def put_rows(head, low, count, rows):
        split = rows.astype(jnp.bfloat16).reshape(4, 2, count, rows.shape[-1])
        for c in range(4):
            for k in (0, 1):
                r.held[k, 2 * head + c // 2, c % 2, low : low + count] = split[c, k]

    part, gain_grad = norm_back(r.middle[...], gain[4], normed_grad)
    put_gain(4, gain_grad)
    middle_grad = r.cotangent[...].astype(jnp.float32) + part
    r.middle[...] = middle_grad
    attn_grad, gain_grad = norm_back(r.attn[...], gain[3], middle_grad)
    put_gain(3, gain_grad)
    attn_grad = attn_grad.astype(jnp.bfloat16)
    for head in range(4):
        put_rows(head, 48, 32, tn(r.mixed[:, columns_of(head)], attn_grad))
        outer.sib(head).start()
    keys, values = kv_parts(r)
    for head in range(4):
        mixed_grad = nt(attn_grad, rows_of_head(r.w_all, head, 48, 32)).astype(jnp.bfloat16)
        prob = r.prob[head]
        prob_grad = nt(mixed_grad, values)
        delta = jnp.sum(prob * prob_grad, axis=1, keepdims=True)
        score_grad = (prob * (prob_grad - delta)).astype(jnp.bfloat16)
        key_part = tn(score_grad, r.query[:, columns_of(head)]) * score_step
        value_part = tn(prob.astype(jnp.bfloat16), mixed_grad)
        if head == 0:
            r.kv_sum[:, :256] = key_part
            r.kv_sum[:, 256:] = value_part
        else:
            r.kv_sum[:, :256] += key_part
            r.kv_sum[:, 256:] += value_part
        r.query_grad[:, columns_of(head)] = nn(score_grad, keys) * score_step
    r.kv_part[...] = r.kv_sum[...].astype(jnp.bfloat16).reshape(2, 2, 128, 512)
    kv_sib = remote(
        r.kv_part.at[:, 1 - core], r.kv_sib.at[...], kv_out.at[0], kv_in.at[0], at.sibling
    )
    kv_sib.start()
    outer.merge()
    kv_sib.wait_recv()
    r.kv_chip[...] = (
        r.kv_part[1 - x, core].astype(jnp.float32) + r.kv_sib[1 - x].astype(jnp.float32)
    ).astype(jnp.bfloat16)
    kv_x = remote(r.kv_chip, r.kv_far, kv_out.at[1], kv_in.at[1], at.over_x)
    kv_x.start()
    normed = r.normed[...]
    query_gain = None
    for head in range(4):
        turned = turn_back(r.query_grad[:, columns_of(head)], cos, sin)
        q_raw_grad, gain_grad = norm_back(r.q_raw[:, columns_of(head)], gain[1], turned)
        query_gain = gain_grad if query_gain is None else query_gain + gain_grad
        q_raw_grad = q_raw_grad.astype(jnp.bfloat16)
        r.query[:, columns_of(head)] = q_raw_grad
        put_rows(head, 0, 32, tn(q_raw_grad, normed))
    put_gain(1, query_gain)
    outer.pair_up()
    kv_x.wait_recv()
    kv_grad = (
        r.kv_part[x, core].astype(jnp.float32)
        + r.kv_sib[x].astype(jnp.float32)
        + r.kv_far[...].astype(jnp.float32)
    )
    k_raw_grad, gain_grad = norm_back(r.k_raw[...], gain[2], turn_back(kv_grad[:, :256], cos, sin))
    put_gain(2, gain_grad)
    k_raw_grad = k_raw_grad.astype(jnp.bfloat16)
    v_raw_grad = kv_grad[:, 256:].astype(jnp.bfloat16)
    woven = (nn(k_raw_grad, pick(0)) + nn(v_raw_grad, pick(8))).astype(jnp.bfloat16)
    for head in range(4):
        put_rows(head, 32, 16, tn(woven[:, 128 * head : 128 * head + 128], normed))
        inner.sib(head).start()
    normed_grad = nn(k_raw_grad, r.wk[...]) + nn(v_raw_grad, r.wv[...])
    for head in range(4):
        normed_grad += nn(r.query[:, columns_of(head)], rows_of_head(r.w_all, head, 0, 32))
    part, gain_grad = norm_back(r.tokens[...].astype(jnp.float32), gain[0], normed_grad)
    put_gain(0, gain_grad)
    gain_total.send(0)
    r.token_grad[...] = r.middle[...] + part
    write(1).start()
    inner.merge()
    gain_total.take(0)
    gain_total.send(1)
    outer.collect()
    complete()
    for k in (2, 3, 4):
        write(k).start()
    inner.pair_up()
    gain_total.take(1)
    gain_total.send(2)
    inner.collect()
    gain_total.take(2)
    gain_total.send(3)
    r.o_grad[...] = outer.total()
    total = inner.total()
    r.q_grad[...] = total[:32]
    r.k_grad[...] = total[32:40]
    r.v_grad[...] = total[40:48]
    gain_total.take(3)
    device = at.f * 4 + s
    first = pl.multiple_of(device * 160 // 128 * 128, 128)
    r.gain_grad[...] = pltpu.roll(
        r.gain_sum[:, pl.ds(first, 256)], 256 - lax.rem(device, 4) * 32, 1
    )
    outer.drain()
    inner.drain()
    for k in range(5):
        write(k).wait()
    gain_total.drain()
    kv_sib.wait_send()
    kv_x.wait_send()


def layer_call(values):
    b16, f32 = jnp.bfloat16, jnp.float32
    rows, width = values["tokens"].shape
    units = values["own_gate"].shape[0]
    outs = {
        "result": ((rows, width), b16),
        "token_grad": ((rows, width), f32),
        "gain_grad": ((1, 256), f32),
        "q_grad": ((32, width), f32),
        "k_grad": ((8, width), f32),
        "v_grad": ((8, width), f32),
        "o_grad": ((32, width), f32),
        "gate_grad": ((units, width), f32),
        "up_grad": ((units, width), f32),
        "down_grad": ((units, width), f32),
    }
    scratch = {
        "gain_sum": ((1, 5120), f32),
        "w_all": ((16, 2, 80, width), b16),
        "gain_all": ((32, 1, 256), f32),
        "starts": ((rows, rows), f32),
        "cos": ((rows, rows), f32),
        "sin": ((rows, rows), f32),
        "gains": ((1, 5120), f32),
        "wk": ((256, width), b16),
        "wv": ((256, width), b16),
        "normed": ((rows, width), b16),
        "k_raw": ((rows, 256), f32),
        "q_raw": ((rows, 1024), f32),
        "query": ((rows, 1024), b16),
        "query_grad": ((rows, 1024), f32),
        "kv_all": ((4, rows, 512), b16),
        "prob": ((4, rows, 512), f32),
        "mixed": ((rows, 1024), b16),
        "attn": ((rows, width), f32),
        "middle": ((rows, width), f32),
        "peer_w": ((3, units, width), b16),
        "held": ((2, 8, 2, rows, width), b16),
        "gate_keep": ((2, 8, 2 * rows, units), b16),
        "up_keep": ((2, 8, 2 * rows, units), b16),
        "hidden_keep": ((2, 8, 2 * rows, units), b16),
        "part_own": ((rows, width), f32),
        "to_sib": ((8, rows, width), b16),
        "from_sib": ((8, rows, width), b16),
        "chip_sum": ((8, rows, width), b16),
        "from_y": ((4, rows, width), b16),
        "to_z": ((4, rows, width), b16),
        "from_z": ((2, 4, rows, width), b16),
        "from_x": ((3, units, width), b16),
        "sib_in": ((8, 2, 80, width), b16),
        "half_in": ((4, 80, width), b16),
        "xf_in": ((4, 80, width), b16),
        "yf_in": ((4, 80, width), b16),
        "zw_in": ((4, 80, width), b16),
        "kv_sum": ((4 * rows, 512), f32),
        "kv_part": ((2, 2, rows, 512), b16),
        "kv_sib": ((2, rows, 512), b16),
        "kv_chip": ((rows, 512), b16),
        "kv_far": ((rows, 512), b16),
        "gain_out": ((4, 1, 5120), f32),
        "gain_in": ((7, 1, 5120), f32),
    }
    gather_sems = [DMA((2,)), DMA((4,)), DMA((4,)), DMA((4,)), DMA((4,)), DMA((8,)), DMA((8,))]
    sum_sems = [DMA((8,)), DMA((8,)), DMA((4, 4)), DMA((4, 4)), DMA((4, 4)), DMA((2, 4, 4))]
    front_sems = gain_sems() + gather_weight_sems() + [DMA((3,))] * 4
    ffn_sems = (gather_sems + sum_sems) * 2 + [DMA((3,)), DMA((3,))]
    back_sems = [DMA((2, 4))] * 12 + [DMA((2,)), DMA((2,)), DMA((6,)), DMA((7,)), DMA((5,))]
    sems = front_sems + ffn_sems + back_sems
    large = ("result", "token_grad", "gate_grad", "up_grad", "down_grad")
    scratch.update({name: outs[name] for name in large})
    names = tuple(values) + tuple(name + "_out" if name in large else name for name in outs)
    names += tuple(scratch)

    def kernel(*refs):
        at = Place()
        r = Refs(names, refs)
        held_sems = refs[len(names) :]
        first, second = len(front_sems), len(front_sems) + len(ffn_sems)
        normed_ffn, x_weight, drain = front_phase(at, r, held_sems[:first])
        normed_grad, complete = ffn_phase(at, r, held_sems[first:second], normed_ffn, x_weight)
        back_phase(at, r, held_sems[second:], normed_grad, complete)
        drain()

    vmem = pl.BlockSpec(memory_space=pltpu.VMEM)
    out = pl.pallas_call(
        kernel,
        out_shape=tuple(jax.ShapeDtypeStruct(*spec) for spec in outs.values()),
        in_specs=[vmem] * len(values),
        out_specs=tuple(
            pl.BlockSpec(memory_space=pl.ANY) if name in large else vmem for name in outs
        ),
        scratch_shapes=[pltpu.VMEM(*spec) for spec in scratch.values()] + sems,
        compiler_params=pltpu.CompilerParams(
            collective_id=1, has_side_effects=True, vmem_limit_bytes=63 << 20
        ),
        name="layer",
    )(*values.values())
    return dict(zip(outs, out))


def settle_kernel(count, *refs):
    ins, outs, held, sems = refs[:count], refs[count : 2 * count], refs[2 * count : -1], refs[-1]
    loads = [pltpu.make_async_copy(ins[k], held[k], sems.at[0, k]) for k in range(count)]
    stores = [pltpu.make_async_copy(held[k], outs[k], sems.at[1, k]) for k in range(count)]
    for copy in loads:
        copy.start()
    for load, store in zip(loads, stores):
        load.wait()
        store.start()
    for copy in stores:
        copy.wait()


def settle(arrays):
    anywhere = pl.BlockSpec(memory_space=pl.ANY)
    return pl.pallas_call(
        partial(settle_kernel, len(arrays)),
        out_shape=tuple(jax.ShapeDtypeStruct(a.shape, a.dtype) for a in arrays),
        in_specs=[anywhere] * len(arrays),
        out_specs=tuple([anywhere] * len(arrays)),
        scratch_shapes=[pltpu.VMEM(a.shape, a.dtype) for a in arrays] + [DMA((2, len(arrays)))],
        name="settle",
    )(*arrays)


def one_kernel(
    tokens, doc_start, gains, w_query, w_key, w_value, w_out, w_gate, w_up, w_down, cotangent
):
    share = gains.shape[0]
    out = layer_call(
        {
            "tokens": tokens,
            "doc": doc_start,
            "own_gains": gains,
            "own_q": w_query.T,
            "own_k": w_key.T,
            "own_v": w_value.T,
            "own_o": w_out,
            "own_gate": w_gate.T,
            "own_up": w_up.T,
            "own_down": w_down,
            "cotangent": cotangent,
        }
    )
    names = ("result", "token_grad", "gain_grad", "q_grad", "k_grad", "v_grad", "o_grad")
    names += ("gate_grad", "up_grad", "down_grad")
    out = dict(zip(names, settle([out[name] for name in names])))
    return (
        out["result"],
        out["token_grad"],
        out["gain_grad"][0, :share],
        out["q_grad"].T,
        out["k_grad"].T,
        out["v_grad"].T,
        out["o_grad"],
        out["gate_grad"].T,
        out["up_grad"].T,
        out["down_grad"],
    )


def solution(mesh):
    in_specs = (
        P(("fsdp", "seq"), None),
        P(("fsdp", "seq")),
        P(("fsdp", "seq")),
        P(None, ("fsdp", "seq")),
        P(None, ("fsdp", "seq")),
        P(None, ("fsdp", "seq")),
        P(("fsdp", "seq"), None),
        P(None, ("fsdp", "seq")),
        P(None, ("fsdp", "seq")),
        P(("fsdp", "seq"), None),
        P(("fsdp", "seq"), None),
    )
    out_specs = (
        P(("fsdp", "seq"), None),
        P(("fsdp", "seq"), None),
        P(("fsdp", "seq")),
        P(None, ("fsdp", "seq")),
        P(None, ("fsdp", "seq")),
        P(None, ("fsdp", "seq")),
        P(("fsdp", "seq"), None),
        P(None, ("fsdp", "seq")),
        P(None, ("fsdp", "seq")),
        P(("fsdp", "seq"), None),
    )
    body = one_kernel if dict(mesh.shape) == {"fsdp": 8, "seq": 4} else local
    return jax.shard_map(body, mesh=mesh, in_specs=in_specs, out_specs=out_specs, check_vma=False)
```
